128 devices in a mesh: tm: 8 (over x_lo, z), rows: 16 (over y, x_hi, core).
Axes of the slice: x: 4 (x_hi: 2, x_lo: 2; x = x_hi * 2 + x_lo), y: 4, z: 4, core: 2. Of those that a mesh axis runs over, the one named last changes fastest.
Arguments:
- features: bfloat16 [8, 256, 64, 256], P('tm', 'rows'), may hold values from -6 to 6
- block_shift: int32 [3, 4, 8, 32, 32], P(None, None, 'tm', 'rows'), may hold values from -5 to 5
- quarter_pel: int32 [3, 4, 8, 32, 32], P(None, None, 'tm', 'rows'), may hold values from 0 to 3
- update_mask: int32 [3, 8], P(None, 'tm'), may hold values 0 or 1
- uniting_weight: bfloat16 [3, 3, 64, 192], replicated, may hold values from -0.15625 to 0.15625
- mixing_weight: bfloat16 [3, 3, 64, 64], replicated, may hold values from -0.25 to 0.25
Outputs:
- refined: bfloat16 [8, 256, 64, 256], P('tm', 'rows')
The draws below stay inside these ranges and needn't reach their ends.
All inputs are finite; a program needn't handle non-finite values. No bound on the sum of `update_mask` on one device may be relied on, other than what follows from the above.
Results may differ from the reference program's by a relative error of at most 0.0057.
Values may be sent and summed in bfloat16 or wider, within the bound.
No kernel may reach another device: no remote copies, remote signals or barrier semaphores. Data moves between devices by JAX's collectives and lax.ppermute only.
A program may use at most 128 MiB of HBM per device.

```python
import jax
import jax.numpy as jnp
from jax import lax

CH = 64
WIDTH = 256
LEVELS = 3
SPAN = 5
FRAMES = 8
HEIGHT = 256


def place_ends(drawn, stream_key, smallest, high):
    longest = drawn.shape.index(max(drawn.shape))
    spots = []
    for shift in (0, 1):
        where = [jax.random.randint(jax.random.fold_in(stream_key, axis), (), 0, length) for axis, length in enumerate(drawn.shape)]
        where[longest] = (where[longest] + shift) % drawn.shape[longest]
        spots.append(tuple(where))
    return drawn.at[spots[0]].set(smallest).at[spots[1]].set(high)


def shard_levels(key, dims, pieces, low, high):
    def one(dim, shards_of):
        heights = jax.random.uniform(jax.random.fold_in(jax.random.fold_in(key, 6), dim), (shards_of,), jnp.float32, low / len(pieces), high / len(pieces))
        return jnp.repeat(jnp.exp(heights), dims[dim] // shards_of).reshape((-1,) + (1,) * (len(dims) - dim - 1))

    loudness = one(*pieces[0])
    for cut in pieces[1:]:
        loudness = loudness * one(*cut)
    return loudness


def scatter_about(own_key, extent, deviation, bound, split=(), kind=jnp.bfloat16):
    gain = shard_levels(own_key, extent, split, -0.22, 0.18) if split else 1.0
    entries = jax.random.normal(own_key, extent, jnp.float32) * deviation * gain
    return jnp.minimum(jnp.maximum(entries, -bound), bound).astype(kind)


def setup_inputs(seed: int = 0) -> dict:
    arg_keys = jax.random.split(jax.random.key(seed), 7)
    return {
        "features": scatter_about(arg_keys[0], (FRAMES, HEIGHT, CH, WIDTH), 1.0, 6.0, ((0, 8), (1, 16))),
        "block_shift": place_ends(jax.random.randint(arg_keys[1], (LEVELS, 4, FRAMES, HEIGHT // 8, WIDTH // 8), -SPAN, SPAN + 1), jax.random.fold_in(arg_keys[1], 1), -SPAN, SPAN).astype(jnp.int32),
        "quarter_pel": place_ends(jax.random.randint(arg_keys[2], (LEVELS, 4, FRAMES, HEIGHT // 8, WIDTH // 8), 0, 4), jax.random.fold_in(arg_keys[2], 1), 0, 3).astype(jnp.int32),
        "update_mask": place_ends((jax.random.randint(arg_keys[3], (LEVELS, FRAMES), 0, 4) < 3).astype(jnp.int32), jax.random.fold_in(arg_keys[3], 1), 0, 1),
        "uniting_weight": scatter_about(arg_keys[4], (3, 3, CH, 3 * CH), (27 * CH) ** -0.5, 0.15625),
        "mixing_weight": scatter_about(arg_keys[5], (3, 3, CH, CH), (9 * CH) ** -0.5, 0.25),
    }


def enlarge(values):
    return jnp.repeat(jnp.repeat(values, 8, axis=0), 8, axis=1)


def warp(panel_band, shifts, quarters):
    height, channels, columns = panel_band.shape
    margin = SPAN + 1
    padded = jnp.pad(panel_band.astype(jnp.float32), ((margin, margin), (0, 0), (margin, margin)))
    shift_rows = enlarge(shifts[0])
    shift_cols = enlarge(shifts[1])
    part_rows = enlarge(quarters[0]).astype(jnp.float32) * 0.25
    part_cols = enlarge(quarters[1]).astype(jnp.float32) * 0.25
    rows_at = jnp.arange(height, dtype=jnp.int32)[:, None] + shift_rows + margin
    cols_at = jnp.arange(columns, dtype=jnp.int32)[None, :] + shift_cols + margin
    summed = jnp.zeros((height, columns, channels), jnp.float32)
    for row_tap in (0, 1):
        weight_rows = part_rows if row_tap == 1 else 1.0 - part_rows
        for col_tap in (0, 1):
            weight_cols = part_cols if col_tap == 1 else 1.0 - part_cols
            picked = padded[rows_at + row_tap, :, cols_at + col_tap]
            summed = summed + (weight_rows * weight_cols)[:, :, None] * picked
    return jnp.transpose(summed, (0, 2, 1)).astype(jnp.bfloat16)


def convolve(inputs, weight):
    height, channels, columns = inputs.shape
    padded = jnp.pad(inputs.astype(jnp.float32), ((1, 1), (0, 0), (1, 1)))
    summed = jnp.zeros((height, weight.shape[2], columns), jnp.float32)
    for tap_row in range(3):
        for tap_col in range(3):
            window = padded[tap_row:tap_row + height, :, tap_col:tap_col + columns]
            summed = summed + jnp.einsum("oc,hcw->how", weight[tap_row, tap_col].astype(jnp.float32), window)
    return summed


def reference(features, block_shift, quarter_pel, update_mask, uniting_weight, mixing_weight):
    current = features
    for level_index in range(LEVELS - 1, -1, -1):
        distance = 2 ** level_index
        earlier = jnp.roll(current, distance, axis=0)
        following = jnp.roll(current, -distance, axis=0)
        shifts = jnp.moveaxis(block_shift[level_index], 1, 0)
        quarters = jnp.moveaxis(quarter_pel[level_index], 1, 0)
        masks = update_mask[level_index]

        def refine(item):
            before_band, after_band, own_band, shift_frame, quarter_frame, mask_value = item
            warped_earlier = warp(before_band, shift_frame[0:2], quarter_frame[0:2])
            warped_later = warp(after_band, shift_frame[2:4], quarter_frame[2:4])
            joined = jnp.concatenate([warped_earlier, warped_later, own_band], axis=1)
            uniting_sum = convolve(joined, uniting_weight)
            activation = (uniting_sum * jax.nn.sigmoid(uniting_sum)).astype(jnp.bfloat16)
            mixing_sum = convolve(activation, mixing_weight)
            return (own_band.astype(jnp.float32) + mask_value.astype(jnp.float32) * mixing_sum).astype(jnp.bfloat16)

        current = lax.map(refine, (earlier, following, current, shifts, quarters, masks))
    return current
```

```python
import functools

import jax
import jax.numpy as jnp
from jax import lax
from jax.experimental import pallas as pl
from jax.experimental.pallas import tpu as pltpu
from jax.sharding import PartitionSpec as P

LEVELS = 3
CH = 64
WIDTH = 256
HALF = 8
F32 = jnp.float32
BF16 = jnp.bfloat16


def pick_rows(v, bits, w0, w1, outs):
    b8, b4, b2, b1 = bits
    n8, n4, n2, n1 = outs + 8, outs + 4, outs + 2, outs + 1
    x8 = [jnp.where(b8, v[j + 8], v[j]) if j < outs + 3 else v[j] for j in range(n8)]
    x4 = [jnp.where(b4, x8[j + 4], x8[j]) for j in range(n4)]
    x2 = [jnp.where(b2, x4[j + 2], x4[j]) for j in range(n2)]
    x1 = [jnp.where(b1, x2[j + 1], x2[j]) for j in range(n1)]
    return [w0 * x1[i] + w1 * x1[i + 1] for i in range(outs)]


def level_kernel(sources, flags, vals, wu, wm, *refs):
    pieces = [refs[4 * i : 4 * i + 4] for i in range(sources)]
    own_top, own_a, own_b, own_bot, out_a, out_b, out_first, out_last = refs[
        4 * sources : 4 * sources + 8
    ]
    src, table, cols, passed, joined, act = refs[4 * sources + 8 :]

    for i in range(sources):
        for p in range(4):
            src[i, 8 * p : 8 * p + 8] = pieces[i][p][...]
    own_at = 2 * CH
    joined[0:2, own_at : own_at + CH] = own_top[...]
    joined[2:10, own_at : own_at + CH] = own_a[...]
    joined[10:18, own_at : own_at + CH] = own_b[...]
    joined[18:20, own_at : own_at + CH] = own_bot[...]

    block_of = lax.broadcasted_iota(jnp.int32, (32, WIDTH), 1) // 8
    spread = (block_of == lax.broadcasted_iota(jnp.int32, (32, WIDTH), 0)).astype(F32)
    table[...] = jnp.dot(
        vals[...].astype(F32).astype(BF16), spread.astype(BF16), preferred_element_type=F32
    )

    has_above = flags[0] > 0
    has_below = flags[1] > 0

    def warp_block(which, block, first_source, count, outs, put):
        base = (which * 4 + block) * 8
        entry = table[pl.ds(pl.multiple_of(base, 8), 8), :]
        dy = entry[0:1].astype(jnp.int32)
        dx = entry[1:2].astype(jnp.int32)
        fy = entry[2:3] * 0.25
        fx = entry[3:4] * 0.25
        off = lax.broadcasted_iota(jnp.int32, (WIDTH, WIDTH), 0) - (
            lax.broadcasted_iota(jnp.int32, (WIDTH, WIDTH), 1) + dx
        )
        cols[...] = jnp.where(
            off == 0, 1.0 - fx, jnp.where(off == 1, fx, 0.0)
        ).astype(BF16)
        source = which if sources == 2 else 0
        window = src[source, pl.ds(first_source, count)].reshape(count * CH, WIDTH)
        passed[0:count] = jnp.dot(
            window, cols[...], preferred_element_type=F32
        ).reshape(count, CH, WIDTH)
        s = dy + 5
        lanes = (16, WIDTH)
        bits = [jnp.broadcast_to((s & b) != 0, lanes) for b in (8, 4, 2, 1)]
        w1 = jnp.broadcast_to(fy, lanes)
        w0 = 1.0 - w1
        for c in range(CH // 16):
            v = [passed[u, 16 * c : 16 * c + 16, :] for u in range(count)]
            for i, row in enumerate(pick_rows(v, bits, w0, w1, outs)):
                put(i, 16 * c, row)

    @pl.loop(0, 4)
    def _(n):
        which, block = n // 2, n % 2

        def put(i, c, row):
            at = pl.multiple_of(which * CH + c, 16)
            joined[2 + 8 * block + i, pl.ds(at, 16), :] = row.astype(BF16)

        warp_block(which, block + 1, 3 + 8 * block, 19, 8, put)

    @pl.loop(0, 4)
    def _(n):
        which, side = n // 2, n % 2
        keep = jnp.where(side == 0, has_above, has_below).astype(F32)

        def put(i, c, row):
            at = pl.multiple_of(which * CH + c, 16)
            joined[18 * side + i, pl.ds(at, 16), :] = (row * keep).astype(BF16)

        warp_block(which, 3 * side, 1 + 18 * side, 13, 2, put)

    lane = lax.broadcasted_iota(jnp.int32, (CH, WIDTH), 1)
    not_first = lane > 0
    not_last = lane < WIDTH - 1

    def gather_taps(s):
        left = jnp.where(not_first, pltpu.roll(s[0:CH], 1, 1), 0.0)
        right = jnp.where(not_last, pltpu.roll(s[2 * CH :], WIDTH - 1, 1), 0.0)
        return s[CH : 2 * CH] + left + right

    @pl.loop(0, 18)
    def _(a):
        window = joined[pl.ds(a, 3)].reshape(9 * CH, WIDTH)
        total = gather_taps(jnp.dot(wu[...], window, preferred_element_type=F32))
        half = 0.5 * total
        value = half + half * jnp.tanh(half)
        keep = jnp.where(
            a == 0, has_above, jnp.where(a == 17, has_below, True)
        ).astype(F32)
        act[a] = (value * keep).astype(BF16)

    scale = flags[2].astype(F32)

    def finish(y):
        window = act[pl.ds(y, 3)].reshape(3 * CH, WIDTH)
        total = gather_taps(jnp.dot(wm[...], window, preferred_element_type=F32))
        own = joined[y + 2, own_at : own_at + CH, :].astype(F32)
        return (own + scale * total).astype(BF16)

    @pl.loop(0, HALF)
    def _(y):
        out_a[y] = finish(y)

    @pl.loop(0, HALF)
    def _(y):
        out_b[y] = finish(y + HALF)

    out_first[...] = out_a[0:2]
    out_last[...] = out_b[6:8]


def run_level(flags, vals, wu, wm, sources, own, interpret=False):
    half = jax.ShapeDtypeStruct((HALF, CH, WIDTH), BF16)
    edge = jax.ShapeDtypeStruct((2, CH, WIDTH), BF16)
    operands = [p for s in sources for p in s] + list(own)
    vmem = pl.BlockSpec(memory_space=pltpu.VMEM)
    return pl.pallas_call(
        functools.partial(level_kernel, len(sources)),
        out_shape=(half, half, edge, edge),
        in_specs=[pl.BlockSpec(memory_space=pltpu.SMEM)] + [vmem] * (3 + len(operands)),
        out_specs=(vmem,) * 4,
        scratch_shapes=[
            pltpu.VMEM((len(sources), 32, CH, WIDTH), BF16),
            pltpu.VMEM((64, WIDTH), F32),
            pltpu.VMEM((WIDTH, WIDTH), BF16),
            pltpu.VMEM((19, CH, WIDTH), F32),
            pltpu.VMEM((20, 3 * CH, WIDTH), BF16),
            pltpu.VMEM((18, CH, WIDTH), BF16),
        ],
        cost_estimate=pl.CostEstimate(
            flops=3_000_000_000, bytes_accessed=4_000_000, transcendentals=300_000
        ),
        interpret=interpret,
    )(flags, vals, wu, wm, *operands)


def moved(x, axis, distance, wrap):
    count = lax.axis_size(axis)
    route = [
        (i, (i + distance) % count) for i in range(count) if wrap or 0 <= i + distance < count
    ]
    return lax.ppermute(x, axis, route)


def level_values(packed, level):
    t = packed[:, level]
    t = t.reshape(2, 2, 2, 4, 32)
    t = jnp.transpose(t, (1, 3, 0, 2, 4)).reshape(2, 4, 4, 32)
    return jnp.pad(t, ((0, 0), (0, 0), (0, 4), (0, 0))).reshape(64, 32)


def tap_weights(w):
    o, j = w.shape[2], w.shape[3]
    return jnp.transpose(w, (1, 2, 0, 3)).reshape(3 * o, 3 * j)


def shards(features, block_shift, quarter_pel, update_mask, uniting_weight, mixing_weight):
    band = features[0]
    a, b = band[:HALF], band[HALF:]
    first, last = band[:2], band[-2:]
    row = lax.axis_index("rows")
    rows = lax.axis_size("rows")
    own = jnp.stack([block_shift[:, :, 0], quarter_pel[:, :, 0]])
    above = moved(own[:, :, :, 1:2], "rows", 1, False)
    below = moved(own[:, :, :, 0:1], "rows", -1, False)
    packed = jnp.concatenate([above, own, below], axis=3)
    wu, wm = tap_weights(uniting_weight), tap_weights(mixing_weight)
    frames = lax.axis_size("tm")
    for level in range(LEVELS - 1, -1, -1):
        distance = 2**level
        steps = [distance] if 2 * distance == frames else [distance, -distance]
        own_top = moved(last, "rows", 1, False)
        own_bot = moved(first, "rows", -1, False)
        sources = []
        for step in steps:
            ra = moved(a, "tm", step, True)
            rb = moved(b, "tm", step, True)
            sources.append((ra, rb))
        sources = [
            (moved(rb, "rows", 1, False), ra, rb, moved(ra, "rows", -1, False))
            for ra, rb in sources
        ]
        flags = jnp.stack(
            [
                (row > 0).astype(jnp.int32),
                (row < rows - 1).astype(jnp.int32),
                update_mask[level, 0],
            ]
        )
        a, b, first, last = run_level(
            flags, level_values(packed, level), wu, wm, sources, (own_top, a, b, own_bot)
        )
    return jnp.concatenate([a, b])[None]


def solution(mesh):
    placed = (
        P("tm", "rows", None, None),
        P(None, None, "tm", "rows", None),
        P(None, None, "tm", "rows", None),
        P(None, "tm"),
        P(),
        P(),
    )
    return jax.shard_map(
        shards, mesh=mesh, in_specs=placed, out_specs=P("tm", "rows", None, None), check_vma=False
    )
```

```python
import functools

import jax
import jax.numpy as jnp
from jax import lax
from jax.experimental import pallas as pl
from jax.experimental.pallas import tpu as pltpu
from jax.sharding import PartitionSpec as P

LEVELS = 3
CH = 64
WIDTH = 256
HALF = 8
F32 = jnp.float32
BF16 = jnp.bfloat16


def pick_rows(v, bits, w0, w1, outs):
    b8, b4, b2, b1 = bits
    n8, n4, n2, n1 = outs + 8, outs + 4, outs + 2, outs + 1
    x8 = [jnp.where(b8, v[j + 8], v[j]) if j < outs + 3 else v[j] for j in range(n8)]
    x4 = [jnp.where(b4, x8[j + 4], x8[j]) for j in range(n4)]
    x2 = [jnp.where(b2, x4[j + 2], x4[j]) for j in range(n2)]
    x1 = [jnp.where(b1, x2[j + 1], x2[j]) for j in range(n1)]
    return [w0 * x1[i] + w1 * x1[i + 1] for i in range(outs)]


def level_kernel(sources, final, flags, vals, wu, wm, *refs):
    pieces = [refs[4 * i : 4 * i + 4] for i in range(sources)]
    own_outer, own_edge, own_inner, own_near = refs[4 * sources : 4 * sources + 4]
    outs = refs[4 * sources + 4 : -6]
    src, table, cols, passed, joined, act = refs[-6:]
    turned = flags[0]

    def at(place, size):
        return place + turned * (size - 2 * place)

    for i in range(sources):
        for p in range(4):
            src[i, pl.ds(at(8 * p, 24), 8)] = pieces[i][p][...]
    own_at = 2 * CH
    own_ch = slice(own_at, own_at + CH)
    joined[pl.ds(at(0, 18), 2), own_ch] = own_outer[...]
    joined[pl.ds(at(2, 12), 8), own_ch] = own_edge[...]
    joined[pl.ds(at(10, 12), 8), own_ch] = own_inner[...]
    joined[pl.ds(at(18, 18), 2), own_ch] = own_near[...]

    block_of = lax.broadcasted_iota(jnp.int32, (32, WIDTH), 1) // 8
    spread = (block_of == lax.broadcasted_iota(jnp.int32, (32, WIDTH), 0)).astype(F32)
    table[...] = jnp.dot(
        vals[...].astype(F32).astype(BF16), spread.astype(BF16), preferred_element_type=F32
    )

    has_above = flags[1] > 0
    has_below = flags[2] > 0

    def warp_block(which, block, first_source, count, outs, put):
        base = (which * 4 + block) * 8
        entry = table[pl.ds(pl.multiple_of(base, 8), 8), :]
        dy = entry[0:1].astype(jnp.int32)
        dx = entry[1:2].astype(jnp.int32)
        fy = entry[2:3] * 0.25
        fx = entry[3:4] * 0.25
        off = lax.broadcasted_iota(jnp.int32, (WIDTH, WIDTH), 0) - (
            lax.broadcasted_iota(jnp.int32, (WIDTH, WIDTH), 1) + dx
        )
        cols[...] = jnp.where(
            off == 0, 1.0 - fx, jnp.where(off == 1, fx, 0.0)
        ).astype(BF16)
        source = which ^ flags[4] if sources == 2 else 0
        window = src[source, pl.ds(first_source, count)].reshape(count * CH, WIDTH)
        passed[0:count] = jnp.dot(
            window, cols[...], preferred_element_type=F32
        ).reshape(count, CH, WIDTH)
        s = dy + 5
        lanes = (16, WIDTH)
        bits = [jnp.broadcast_to((s & b) != 0, lanes) for b in (8, 4, 2, 1)]
        w1 = jnp.broadcast_to(fy, lanes)
        w0 = 1.0 - w1
        for c in range(CH // 16):
            v = [passed[u, 16 * c : 16 * c + 16, :] for u in range(count)]
            for i, row in enumerate(pick_rows(v, bits, w0, w1, outs)):
                put(i, 16 * c, row)

    @pl.loop(0, 4)
    def _(n):
        which, block = n // 2, n % 2

        def put(i, c, row):
            at = pl.multiple_of(which * CH + c, 16)
            joined[2 + 8 * block + i, pl.ds(at, 16), :] = row.astype(BF16)

        warp_block(which, block + 1, 3 + 8 * block, 19, 8, put)

    @pl.loop(0, 4)
    def _(n):
        which, side = n // 2, n % 2
        keep = jnp.where(side == 0, has_above, has_below).astype(F32)

        def put(i, c, row):
            at = pl.multiple_of(which * CH + c, 16)
            joined[18 * side + i, pl.ds(at, 16), :] = (row * keep).astype(BF16)

        warp_block(which, 3 * side, 1 + 18 * side, 13, 2, put)

    lane = lax.broadcasted_iota(jnp.int32, (CH, WIDTH), 1)
    not_first = lane > 0
    not_last = lane < WIDTH - 1

    def gather_taps(s):
        left = jnp.where(not_first, pltpu.roll(s[0:CH], 1, 1), 0.0)
        right = jnp.where(not_last, pltpu.roll(s[2 * CH :], WIDTH - 1, 1), 0.0)
        return s[CH : 2 * CH] + left + right

    @pl.loop(0, 18)
    def _(a):
        window = joined[pl.ds(a, 3)].reshape(9 * CH, WIDTH)
        total = gather_taps(jnp.dot(wu[...], window, preferred_element_type=F32))
        half = 0.5 * total
        value = half + half * jnp.tanh(half)
        keep = jnp.where(
            a == 0, has_above, jnp.where(a == 17, has_below, True)
        ).astype(F32)
        act[a] = (value * keep).astype(BF16)

    scale = flags[3].astype(F32)

    def finish(y):
        window = act[pl.ds(y, 3)].reshape(3 * CH, WIDTH)
        total = gather_taps(jnp.dot(wm[...], window, preferred_element_type=F32))
        own = joined[y + 2, own_ch, :].astype(F32)
        return (own + scale * total).astype(BF16)

    if final:
        (out,) = outs

        @pl.loop(0, 16)
        def _(y):
            out[y] = finish(y)

    else:
        out_edge, out_inner, out_rim, out_near = outs

        @pl.loop(0, HALF)
        def _(y):
            out_edge[y] = finish(y + at(0, 8))

        @pl.loop(0, HALF)
        def _(y):
            out_inner[y] = finish(y + at(8, 8))

        out_rim[...] = out_edge[pl.ds(at(0, 6), 2)]
        out_near[...] = out_inner[pl.ds(at(6, 6), 2)]


def run_level(flags, vals, wu, wm, sources, own, final, interpret=False):
    half = jax.ShapeDtypeStruct((HALF, CH, WIDTH), BF16)
    edge = jax.ShapeDtypeStruct((2, CH, WIDTH), BF16)
    full = jax.ShapeDtypeStruct((2 * HALF, CH, WIDTH), BF16)
    operands = [p for s in sources for p in s] + list(own)
    vmem = pl.BlockSpec(memory_space=pltpu.VMEM)
    out_shape = (full,) if final else (half, half, edge, edge)
    return pl.pallas_call(
        functools.partial(level_kernel, len(sources), final),
        out_shape=out_shape,
        in_specs=[pl.BlockSpec(memory_space=pltpu.SMEM)] + [vmem] * (3 + len(operands)),
        out_specs=(vmem,) * len(out_shape),
        scratch_shapes=[
            pltpu.VMEM((len(sources), 32, CH, WIDTH), BF16),
            pltpu.VMEM((64, WIDTH), F32),
            pltpu.VMEM((WIDTH, WIDTH), BF16),
            pltpu.VMEM((19, CH, WIDTH), F32),
            pltpu.VMEM((20, 3 * CH, WIDTH), BF16),
            pltpu.VMEM((18, CH, WIDTH), BF16),
        ],
        cost_estimate=pl.CostEstimate(
            flops=3_000_000_000, bytes_accessed=4_000_000, transcendentals=300_000
        ),
        interpret=interpret,
    )(flags, vals, wu, wm, *operands)


def send(x, frame_to=lambda t: t, row_to=lambda r: r):
    frames, rows = lax.axis_size("tm"), lax.axis_size("rows")
    route = [
        (t * rows + r, (frame_to(t) % frames) * rows + row_to(r))
        for t in range(frames)
        for r in range(rows)
        if 0 <= row_to(r) < rows
    ]
    return lax.ppermute(x, ("tm", "rows"), route)


def off_chip(r):
    return r + 1 if r % 2 else r - 1


def on_chip(r):
    return r ^ 1


def level_values(packed, level):
    t = packed[:, level]
    t = t.reshape(2, 2, 2, 4, 32)
    t = jnp.transpose(t, (1, 3, 0, 2, 4)).reshape(2, 4, 4, 32)
    return jnp.pad(t, ((0, 0), (0, 0), (0, 4), (0, 0))).reshape(64, 32)


def tap_weights(w):
    o, j = w.shape[2], w.shape[3]
    return jnp.transpose(w, (1, 2, 0, 3)).reshape(3 * o, 3 * j)


def shards(features, block_shift, quarter_pel, update_mask, uniting_weight, mixing_weight):
    band = features[0]
    row = lax.axis_index("rows")
    rows = lax.axis_size("rows")
    frames = lax.axis_size("tm")
    turned = row % 2
    edge = lax.dynamic_slice_in_dim(band, 8 * turned, HALF, axis=0)
    inner = lax.dynamic_slice_in_dim(band, 8 - 8 * turned, HALF, axis=0)
    rim = lax.dynamic_slice_in_dim(band, 14 * turned, 2, axis=0)
    near = lax.dynamic_slice_in_dim(band, 14 - 14 * turned, 2, axis=0)
    own = jnp.stack([block_shift[:, :, 0], quarter_pel[:, :, 0]])
    above = send(own[:, :, :, 1:2], row_to=lambda r: r + 1)
    below = send(own[:, :, :, 0:1], row_to=lambda r: r - 1)
    packed = jnp.concatenate([above, own, below], axis=3)
    wu, wm = tap_weights(uniting_weight), tap_weights(mixing_weight)
    for level in range(LEVELS - 1, -1, -1):
        distance = 2**level
        swapped = jnp.int32(0)
        if 2 * distance == frames:

            def flip(t):
                return t + distance

            sources = [
                (send(edge, flip, off_chip), send(edge, flip), send(inner, flip)),
            ]
        elif 4 * distance == frames:

            def across(t):
                return t + distance if t % (2 * distance) < distance else t - distance

            def flip(t):
                return t + 2 * distance

            e, i = send(edge, across), send(inner, across)
            sources = [
                (send(edge, across, off_chip), e, i),
                (send(e, flip, off_chip), send(e, flip), send(i, flip)),
            ]
            swapped = (lax.axis_index("tm") % (2 * distance) < distance).astype(jnp.int32)
        else:
            sources = []
            for step in (distance, -distance):

                def to(t, step=step):
                    return t + step

                sources.append((send(edge, to, off_chip), send(edge, to), send(inner, to)))
        own_outer = send(rim, row_to=off_chip)
        own_near = send(near, row_to=on_chip)
        sources = [(h, e, i, send(i, row_to=on_chip)) for h, e, i in sources]
        flags = jnp.stack(
            [
                turned,
                (row > 0).astype(jnp.int32),
                (row < rows - 1).astype(jnp.int32),
                update_mask[level, 0],
                swapped,
            ]
        )
        outs = run_level(
            flags,
            level_values(packed, level),
            wu,
            wm,
            sources,
            (own_outer, edge, inner, own_near),
            level == 0,
        )
        if level:
            edge, inner, rim, near = outs
    return outs[0][None]


def solution(mesh):
    placed = (
        P("tm", "rows", None, None),
        P(None, None, "tm", "rows", None),
        P(None, None, "tm", "rows", None),
        P(None, "tm"),
        P(),
        P(),
    )
    return jax.shard_map(
        shards, mesh=mesh, in_specs=placed, out_specs=P("tm", "rows", None, None), check_vma=False
    )
```

```python
import functools

import jax
import jax.numpy as jnp
from jax import lax
from jax.experimental import pallas as pl
from jax.experimental.pallas import tpu as pltpu
from jax.sharding import PartitionSpec as P


LEVELS = 3
CH = 64
WIDTH = 256
HALF = 8
F32 = jnp.float32
BF16 = jnp.bfloat16


def pick_rows(v, bits, w0, w1, outs):
    b8, b4, b2, b1 = bits
    n8, n4, n2, n1 = outs + 8, outs + 4, outs + 2, outs + 1
    x8 = [jnp.where(b8, v[j + 8], v[j]) if j < outs + 3 else v[j] for j in range(n8)]
    x4 = [jnp.where(b4, x8[j + 4], x8[j]) for j in range(n4)]
    x2 = [jnp.where(b2, x4[j + 2], x4[j]) for j in range(n2)]
    x1 = [jnp.where(b1, x2[j + 1], x2[j]) for j in range(n1)]
    return [w0 * x1[i] + w1 * x1[i + 1] for i in range(outs)]


BLOCKS = ((1, 3, 19, 8, 2), (2, 11, 19, 8, 10), (0, 1, 13, 2, 0), (3, 19, 13, 2, 18))
OWN = slice(2 * CH, 3 * CH)


def turn(turned, place, size):
    return place + turned * (size - 2 * place)


def columns_kernel(vals, cols, table):
    block_of = lax.broadcasted_iota(jnp.int32, (32, WIDTH), 1) // 8
    spread = (block_of == lax.broadcasted_iota(jnp.int32, (32, WIDTH), 0)).astype(F32)
    table[...] = jnp.dot(
        vals[...].astype(F32).astype(BF16), spread.astype(BF16), preferred_element_type=F32
    )
    apart = lax.broadcasted_iota(jnp.int32, (WIDTH, WIDTH), 0) - lax.broadcasted_iota(
        jnp.int32, (WIDTH, WIDTH), 1
    )

    @pl.loop(0, cols.shape[0])
    def _(n):
        entry = table[pl.ds(pl.multiple_of(n * 8, 8), 8), :]
        off = apart - entry[1:2].astype(jnp.int32)
        fx = entry[3:4] * 0.25
        cols[n] = jnp.where(off == 0, 1.0 - fx, jnp.where(off == 1, fx, 0.0)).astype(BF16)


def make_columns(vals, interpret=False):
    count = vals.shape[0] // 8
    vmem = pl.BlockSpec(memory_space=pltpu.VMEM)
    return pl.pallas_call(
        columns_kernel,
        out_shape=(
            jax.ShapeDtypeStruct((count, WIDTH, WIDTH), BF16),
            jax.ShapeDtypeStruct((count * 8, WIDTH), F32),
        ),
        in_specs=[vmem],
        out_specs=(vmem, vmem),
        cost_estimate=pl.CostEstimate(
            flops=100_000_000, bytes_accessed=3_000_000, transcendentals=0
        ),
        interpret=interpret,
    )(vals)


def warp_into(flags, cols, table, source_of, base, passed, put_of):
    has_above = (flags[1] > 0).astype(F32)
    has_below = (flags[2] > 0).astype(F32)
    lanes = (16, WIDTH)

    @pl.loop(0, 2)
    def _(which):
        put = put_of(which)

        def column_pass(k):
            block, first, count, _, _ = BLOCKS[k]
            window = source_of(which, first, count).reshape(count * CH, WIDTH)
            passed[k][...] = jnp.dot(
                window, cols[base + which * 4 + block], preferred_element_type=F32
            ).reshape(count, CH, WIDTH)

        def row_pass(k):
            block, _, count, outs, start = BLOCKS[k]
            at = (base + which * 4 + block) * 8
            entry = table[pl.ds(pl.multiple_of(at, 8), 8), :]
            s = entry[0:1].astype(jnp.int32) + 5
            keep = {0: has_above, 3: has_below}.get(block, 1.0)
            bits = [jnp.broadcast_to((s & b) != 0, lanes) for b in (8, 4, 2, 1)]
            fy = entry[2:3] * 0.25
            w1 = jnp.broadcast_to(fy * keep, lanes)
            w0 = jnp.broadcast_to((1.0 - fy) * keep, lanes)
            for c in range(CH // 16):
                v = [passed[k][u, 16 * c : 16 * c + 16, :] for u in range(count)]
                for i, row in enumerate(pick_rows(v, bits, w0, w1, outs)):
                    put(start + i, 16 * c, row.astype(BF16))

        column_pass(0)
        for k in range(4):
            if k < 3:
                column_pass(k + 1)
            row_pass(k)


def convolve_band(flags, wu, wm, joined, act, final, outs):
    has_above = flags[1] > 0
    has_below = flags[2] > 0
    turned = flags[0]
    lane = lax.broadcasted_iota(jnp.int32, (CH, WIDTH), 1)
    not_first = lane > 0
    not_last = lane < WIDTH - 1

    def gather_taps(s):
        left = jnp.where(not_first, pltpu.roll(s[0:CH], 1, 1), 0.0)
        right = jnp.where(not_last, pltpu.roll(s[2 * CH :], WIDTH - 1, 1), 0.0)
        return s[CH : 2 * CH] + left + right

    def activate(a):
        window = joined[pl.ds(a, 3)].reshape(9 * CH, WIDTH)
        total = gather_taps(jnp.dot(wu[...], window, preferred_element_type=F32))
        half = 0.5 * total
        value = half + half * jnp.tanh(half)
        keep = jnp.where(
            a == 0, has_above, jnp.where(a == 17, has_below, True)
        ).astype(F32)
        act[a] = (value * keep).astype(BF16)

    @pl.loop(0, 6)
    def _(n):
        for k in range(3):
            activate(3 * n + k)

    scale = flags[3].astype(F32)

    def finish(y):
        window = act[pl.ds(y, 3)].reshape(3 * CH, WIDTH)
        total = gather_taps(jnp.dot(wm[...], window, preferred_element_type=F32))
        own = joined[y + 2, OWN, :].astype(F32)
        return (own + scale * total).astype(BF16)

    if final:
        (out,) = outs

        @pl.loop(0, 4)
        def _(n):
            for k in range(4):
                out[4 * n + k] = finish(4 * n + k)

    else:
        out_edge, out_inner, out_rim, out_near = outs

        @pl.loop(0, 4)
        def _(n):
            for k in range(2):
                y = 2 * n + k
                out_edge[y] = finish(y + turn(turned, 0, 8))
                out_inner[y] = finish(y + turn(turned, 8, 8))

        out_rim[...] = out_edge[pl.ds(turn(turned, 0, 6), 2)]
        out_near[...] = out_inner[pl.ds(turn(turned, 6, 6), 2)]


def stack_rows(target, turned, pieces):
    for p in range(4):
        target[pl.ds(turn(turned, 8 * p, 24), 8)] = pieces[p][...]


def level_kernel(sources, base, flags, cols, table, wu, wm, *refs):
    own_outer, own_edge, own_inner, own_near = refs[4 * sources : 4 * sources + 4]
    outs = refs[4 * sources + 4 : 4 * sources + 8]
    src, joined, act = refs[4 * sources + 8 : 4 * sources + 11]
    passed = refs[4 * sources + 11 :]
    turned = flags[0]
    for i in range(sources):
        stack_rows(src.at[i], turned, refs[4 * i : 4 * i + 4])
    joined[pl.ds(turn(turned, 0, 18), 2), OWN] = own_outer[...]
    joined[pl.ds(turn(turned, 2, 12), 8), OWN] = own_edge[...]
    joined[pl.ds(turn(turned, 10, 12), 8), OWN] = own_inner[...]
    joined[pl.ds(turn(turned, 18, 18), 2), OWN] = own_near[...]

    def source_of(which, first, count):
        return src[which ^ flags[4] if sources == 2 else 0, first : first + count]

    def put_of(which):
        def put(row, c, value):
            joined[row, pl.ds(pl.multiple_of(which * CH + c, 16), 16), :] = value

        return put

    warp_into(flags, cols, table, source_of, base, passed, put_of)
    convolve_band(flags, wu, wm, joined, act, False, outs)


def warp_kernel(base, flags, cols, table, outer, edge, inner, near, out, src, *passed):
    stack_rows(src, flags[0], (outer, edge, inner, near))

    def source_of(which, first, count):
        return src[first : first + count]

    def put_of(which):
        def put(row, c, value):
            out[which, row, c : c + 16, :] = value

        return put

    warp_into(flags, cols, table, source_of, base, passed, put_of)


def last_kernel(flags, wu, wm, outer, edge, inner, near, earlier, later, out, joined, act):
    turned = flags[0]
    joined[pl.ds(turn(turned, 0, 18), 2), OWN] = outer[pl.ds(turn(turned, 6, 6), 2)]
    joined[pl.ds(turn(turned, 2, 12), 8), OWN] = edge[...]
    joined[pl.ds(turn(turned, 10, 12), 8), OWN] = inner[...]
    joined[pl.ds(turn(turned, 18, 18), 2), OWN] = near[pl.ds(turn(turned, 0, 6), 2)]
    joined[:, 0:CH] = earlier[...]
    joined[:, CH : 2 * CH] = later[...]
    convolve_band(flags, wu, wm, joined, act, True, (out,))


def on_core(kernel, out_shape, scratch, cost, operands, interpret):
    vmem = pl.BlockSpec(memory_space=pltpu.VMEM)
    return pl.pallas_call(
        kernel,
        out_shape=out_shape,
        in_specs=[pl.BlockSpec(memory_space=pltpu.SMEM)] + [vmem] * (len(operands) - 1),
        out_specs=(vmem,) * len(out_shape),
        scratch_shapes=scratch,
        cost_estimate=pl.CostEstimate(
            flops=cost, bytes_accessed=4_000_000, transcendentals=300_000
        ),
        interpret=interpret,
    )(*operands)


def passed_buffers():
    return [pltpu.VMEM((count, CH, WIDTH), F32) for _, _, count, _, _ in BLOCKS]


def band_buffers():
    return [pltpu.VMEM((20, 3 * CH, WIDTH), BF16), pltpu.VMEM((18, CH, WIDTH), BF16)]


def run_level(flags, cols, table, base, wu, wm, sources, own, interpret=False):
    half = jax.ShapeDtypeStruct((HALF, CH, WIDTH), BF16)
    edge = jax.ShapeDtypeStruct((2, CH, WIDTH), BF16)
    operands = [flags, cols, table, wu, wm] + [p for s in sources for p in s] + list(own)
    scratch = [pltpu.VMEM((len(sources), 32, CH, WIDTH), BF16)]
    return on_core(
        functools.partial(level_kernel, len(sources), base),
        (half, half, edge, edge),
        scratch + band_buffers() + passed_buffers(),
        3_000_000_000,
        operands,
        interpret,
    )


def run_warp(flags, cols, table, base, pieces, interpret=False):
    return on_core(
        functools.partial(warp_kernel, base),
        (jax.ShapeDtypeStruct((2, 20, CH, WIDTH), BF16),),
        [pltpu.VMEM((32, CH, WIDTH), BF16)] + passed_buffers(),
        1_500_000_000,
        [flags, cols, table, *pieces],
        interpret,
    )[0]


def run_last(flags, wu, wm, own, warped, interpret=False):
    return on_core(
        last_kernel,
        (jax.ShapeDtypeStruct((2 * HALF, CH, WIDTH), BF16),),
        band_buffers(),
        1_500_000_000,
        [flags, wu, wm, *own, *warped],
        interpret,
    )[0]


def send(x, frame_to=lambda t: t, row_to=lambda r: r):
    frames, rows = lax.axis_size("tm"), lax.axis_size("rows")
    route = [
        (t * rows + r, (frame_to(t) % frames) * rows + row_to(r))
        for t in range(frames)
        for r in range(rows)
        if 0 <= row_to(r) < rows
    ]
    return lax.ppermute(x, ("tm", "rows"), route)


def off_chip(r):
    return r + 1 if r % 2 else r - 1


def on_chip(r):
    return r ^ 1


def level_values(t):
    t = t.reshape(2, 2, 2, 4, 32)
    t = jnp.transpose(t, (1, 3, 0, 2, 4)).reshape(2, 4, 4, 32)
    return jnp.pad(t, ((0, 0), (0, 0), (0, 4), (0, 0))).reshape(64, 32)


def tap_weights(w):
    o, j = w.shape[2], w.shape[3]
    return jnp.transpose(w, (1, 2, 0, 3)).reshape(3 * o, 3 * j)


def shards(features, block_shift, quarter_pel, update_mask, uniting_weight, mixing_weight):
    band = features[0]
    row = lax.axis_index("rows")
    rows = lax.axis_size("rows")
    turned = row % 2
    edge = lax.dynamic_slice_in_dim(band, 8 * turned, HALF, axis=0)
    inner = lax.dynamic_slice_in_dim(band, 8 - 8 * turned, HALF, axis=0)
    rim = lax.dynamic_slice_in_dim(band, 14 * turned, 2, axis=0)
    near = lax.dynamic_slice_in_dim(band, 14 - 14 * turned, 2, axis=0)
    wu, wm = tap_weights(uniting_weight), tap_weights(mixing_weight)

    def to_other(t):
        return t + 4

    def across(t):
        return t + 2 if t % 4 < 2 else t - 2

    def ahead(t):
        return t + 1

    def back(t):
        return t - 1

    e = send(edge, to_other)
    i = send(inner, to_other)
    h = send(edge, to_other, off_chip)
    own = jnp.stack([block_shift[:, :, 0], quarter_pel[:, :, 0]])
    above = send(own[:, :, :, 1:2], row_to=lambda r: r + 1)
    below = send(own[:, :, :, 0:1], row_to=lambda r: r - 1)
    packed = jnp.concatenate([above, own, below], axis=3)
    for_ahead = send(packed[:, 0, 0:2], back)
    for_back = send(packed[:, 0, 2:4], ahead)
    own_outer = send(rim, row_to=off_chip)
    own_near = send(near, row_to=on_chip)
    n = send(i, row_to=on_chip)
    cols, table = make_columns(
        jnp.concatenate(
            [
                level_values(packed[:, 2]),
                level_values(packed[:, 1]),
                level_values(jnp.concatenate([for_ahead, for_back], axis=1)),
            ]
        )
    )
    common = [turned, (row > 0).astype(jnp.int32), (row < rows - 1).astype(jnp.int32)]
    swapped = (lax.axis_index("tm") % 4 < 2).astype(jnp.int32)
    flags = [jnp.stack(common + [update_mask[k, 0], swapped]) for k in range(LEVELS)]

    edge, inner, rim, near = run_level(
        flags[2], cols, table, 0, wu, wm, [(h, e, i, n)], (own_outer, edge, inner, own_near)
    )

    own_outer = send(rim, row_to=off_chip)
    own_near = send(near, row_to=on_chip)
    e = send(edge, across)
    i = send(inner, across)
    h = send(edge, across, off_chip)
    xe = send(e, to_other)
    xh = send(e, to_other, off_chip)
    xi = send(i, to_other)
    n = send(i, row_to=on_chip)
    xn = send(xi, row_to=on_chip)
    edge, inner, _, _ = run_level(
        flags[1],
        cols,
        table,
        8,
        wu,
        wm,
        [(h, e, i, n), (xh, xe, xi, xn)],
        (own_outer, edge, inner, own_near),
    )

    outer = send(edge, row_to=off_chip)
    near = send(inner, row_to=on_chip)
    own = (outer, edge, inner, near)
    warped = run_warp(flags[0], cols, table, 16, own)
    earlier = send(warped[0], ahead)
    later = send(warped[1], back)
    return run_last(flags[0], wu, wm, own, (earlier, later))[None]


def solution(mesh):
    placed = (
        P("tm", "rows", None, None),
        P(None, None, "tm", "rows", None),
        P(None, None, "tm", "rows", None),
        P(None, "tm"),
        P(),
        P(),
    )
    return jax.shard_map(
        shards, mesh=mesh, in_specs=placed, out_specs=P("tm", "rows", None, None), check_vma=False
    )
```

```python
import functools

import jax
import jax.numpy as jnp
from jax import lax
from jax.experimental import pallas as pl
from jax.experimental.pallas import tpu as pltpu
from jax.sharding import PartitionSpec as P


LEVELS = 3
CH = 64
WIDTH = 256
HALF = 8
VMEM_LIMIT = 28 << 20
F32 = jnp.float32
BF16 = jnp.bfloat16


def pick_rows(v, bits, w0, w1, outs):
    b8, b4, b2, b1 = bits
    n8, n4, n2, n1 = outs + 8, outs + 4, outs + 2, outs + 1
    x8 = [jnp.where(b8, v[j + 8], v[j]) if j < outs + 3 else v[j] for j in range(n8)]
    x4 = [jnp.where(b4, x8[j + 4], x8[j]) for j in range(n4)]
    x2 = [jnp.where(b2, x4[j + 2], x4[j]) for j in range(n2)]
    x1 = [jnp.where(b1, x2[j + 1], x2[j]) for j in range(n1)]
    return [w0 * x1[i] + w1 * x1[i + 1] for i in range(outs)]


BLOCKS = ((1, 3, 19, 8, 2), (2, 11, 19, 8, 10), (0, 1, 13, 2, 0), (3, 19, 13, 2, 18))
OWN = slice(2 * CH, 3 * CH)


def turn(turned, place, size):
    return place + turned * (size - 2 * place)


def columns_kernel(vals, cols, table):
    block_of = lax.broadcasted_iota(jnp.int32, (32, WIDTH), 1) // 8
    spread = (block_of == lax.broadcasted_iota(jnp.int32, (32, WIDTH), 0)).astype(F32)
    table[...] = jnp.dot(vals[...], spread.astype(BF16), preferred_element_type=F32)
    apart = lax.broadcasted_iota(jnp.int32, (WIDTH, WIDTH), 0) - lax.broadcasted_iota(
        jnp.int32, (WIDTH, WIDTH), 1
    )

    @pl.loop(0, cols.shape[0])
    def _(n):
        entry = table[pl.ds(pl.multiple_of(n * 8, 8), 8), :]
        off = apart - entry[1:2].astype(jnp.int32)
        fx = entry[3:4] * 0.25
        cols[n] = jnp.where(off == 0, 1.0 - fx, jnp.where(off == 1, fx, 0.0)).astype(BF16)


def make_columns(vals, interpret=False):
    count = vals.shape[0] // 8
    vmem = pl.BlockSpec(memory_space=pltpu.VMEM)
    return pl.pallas_call(
        columns_kernel,
        out_shape=(
            jax.ShapeDtypeStruct((count, WIDTH, WIDTH), BF16),
            jax.ShapeDtypeStruct((count * 8, WIDTH), F32),
        ),
        in_specs=[vmem],
        out_specs=(vmem, vmem),
        cost_estimate=pl.CostEstimate(
            flops=100_000_000, bytes_accessed=3_000_000, transcendentals=0
        ),
        interpret=interpret,
    )(vals)


def warp_into(flags, cols, table, source_of, passed, put_of):
    has_above = (flags[1] > 0).astype(F32)
    has_below = (flags[2] > 0).astype(F32)
    lanes = (16, WIDTH)

    @pl.loop(0, 2)
    def _(which):
        put = put_of(which)

        def column_pass(k):
            block, first, count, _, _ = BLOCKS[k]
            window = source_of(which, first, count).reshape(count * CH, WIDTH)
            passed[k][...] = jnp.dot(
                window, cols[which * 4 + block], preferred_element_type=F32
            ).reshape(count, CH, WIDTH)

        def row_pass(k):
            block, _, count, outs, start = BLOCKS[k]
            at = (which * 4 + block) * 8
            entry = table[pl.ds(pl.multiple_of(at, 8), 8), :]
            s = entry[0:1].astype(jnp.int32) + 5
            keep = {0: has_above, 3: has_below}.get(block, 1.0)
            bits = [jnp.broadcast_to((s & b) != 0, lanes) for b in (8, 4, 2, 1)]
            fy = entry[2:3] * 0.25
            w1 = jnp.broadcast_to(fy * keep, lanes)
            w0 = jnp.broadcast_to((1.0 - fy) * keep, lanes)
            for c in range(CH // 16):
                v = [passed[k][u, 16 * c : 16 * c + 16, :] for u in range(count)]
                for i, row in enumerate(pick_rows(v, bits, w0, w1, outs)):
                    put(start + i, 16 * c, row.astype(BF16))

        column_pass(0)
        for k in range(4):
            if k < 3:
                column_pass(k + 1)
            row_pass(k)


def convolve_band(flags, wu, wm, joined, act, final, outs):
    has_above = flags[1] > 0
    has_below = flags[2] > 0
    turned = flags[0]
    lane = lax.broadcasted_iota(jnp.int32, (CH, WIDTH), 1)
    not_first = lane > 0
    not_last = lane < WIDTH - 1

    def gather_taps(s):
        left = jnp.where(not_first, pltpu.roll(s[0:CH], 1, 1), 0.0)
        right = jnp.where(not_last, pltpu.roll(s[2 * CH :], WIDTH - 1, 1), 0.0)
        return s[CH : 2 * CH] + left + right

    def activate(a):
        window = joined[pl.ds(a, 3)].reshape(9 * CH, WIDTH)
        total = gather_taps(jnp.dot(wu[...], window, preferred_element_type=F32))
        half = 0.5 * total
        value = half + half * jnp.tanh(half)
        keep = jnp.where(
            a == 0, has_above, jnp.where(a == 17, has_below, True)
        ).astype(F32)
        act[a] = (value * keep).astype(BF16)

    @pl.loop(0, 6)
    def _(n):
        for k in range(3):
            activate(3 * n + k)

    scale = flags[3].astype(F32)

    def finish(y):
        window = act[pl.ds(y, 3)].reshape(3 * CH, WIDTH)
        total = gather_taps(jnp.dot(wm[...], window, preferred_element_type=F32))
        own = joined[y + 2, OWN, :].astype(F32)
        return (own + scale * total).astype(BF16)

    if final:
        (out,) = outs

        @pl.loop(0, 4)
        def _(n):
            for k in range(4):
                out[4 * n + k] = finish(4 * n + k)

    else:
        out_edge, out_inner, out_rim, out_near = outs

        @pl.loop(0, 4)
        def _(n):
            for k in range(2):
                y = 2 * n + k
                out_edge[y] = finish(y + turn(turned, 0, 8))
                out_inner[y] = finish(y + turn(turned, 8, 8))

        out_rim[...] = out_edge[pl.ds(turn(turned, 0, 6), 2)]
        out_near[...] = out_inner[pl.ds(turn(turned, 6, 6), 2)]


def stack_rows(target, turned, pieces):
    for p in range(4):
        target[pl.ds(turn(turned, 8 * p, 24), 8)] = pieces[p][...]


def level_kernel(sources, flags, cols, table, wu, wm, *refs):
    own_outer, own_edge, own_inner, own_near = refs[4 * sources : 4 * sources + 4]
    outs = refs[4 * sources + 4 : 4 * sources + 8]
    src, joined, act = refs[4 * sources + 8 : 4 * sources + 11]
    passed = refs[4 * sources + 11 :]
    turned = flags[0]
    for i in range(sources):
        stack_rows(src.at[i], turned, refs[4 * i : 4 * i + 4])
    joined[pl.ds(turn(turned, 0, 18), 2), OWN] = own_outer[0:2]
    joined[pl.ds(turn(turned, 2, 12), 8), OWN] = own_edge[...]
    joined[pl.ds(turn(turned, 10, 12), 8), OWN] = own_inner[...]
    joined[pl.ds(turn(turned, 18, 18), 2), OWN] = own_near[0:2]

    def source_of(which, first, count):
        return src[which ^ flags[4] if sources == 2 else 0, first : first + count]

    def put_of(which):
        def put(row, c, value):
            joined[row, pl.ds(pl.multiple_of(which * CH + c, 16), 16), :] = value

        return put

    warp_into(flags, cols, table, source_of, passed, put_of)
    convolve_band(flags, wu, wm, joined, act, False, outs)


def warp_kernel(flags, cols, table, outer, edge, inner, near, ahead, back, src, both, *passed):
    stack_rows(src, flags[0], (outer, edge, inner, near))

    def source_of(which, first, count):
        return src[first : first + count]

    def put_of(which):
        def put(row, c, value):
            both[which, row, c : c + 16, :] = value

        return put

    warp_into(flags, cols, table, source_of, passed, put_of)
    ahead[...] = both[0]
    back[...] = both[1]


def last_kernel(flags, wu, wm, outer, edge, inner, near, earlier, later, out, joined, act):
    turned = flags[0]
    joined[pl.ds(turn(turned, 0, 18), 2), OWN] = outer[pl.ds(turn(turned, 6, 6), 2)]
    joined[pl.ds(turn(turned, 2, 12), 8), OWN] = edge[...]
    joined[pl.ds(turn(turned, 10, 12), 8), OWN] = inner[...]
    joined[pl.ds(turn(turned, 18, 18), 2), OWN] = near[pl.ds(turn(turned, 0, 6), 2)]
    joined[:, 0:CH] = earlier[...]
    joined[:, CH : 2 * CH] = later[...]
    convolve_band(flags, wu, wm, joined, act, True, (out,))


def on_core(kernel, out_shape, scratch, cost, operands, interpret):
    vmem = pl.BlockSpec(memory_space=pltpu.VMEM)
    return pl.pallas_call(
        kernel,
        out_shape=out_shape,
        in_specs=[pl.BlockSpec(memory_space=pltpu.SMEM)] + [vmem] * (len(operands) - 1),
        out_specs=(vmem,) * len(out_shape),
        scratch_shapes=scratch,
        compiler_params=pltpu.CompilerParams(vmem_limit_bytes=VMEM_LIMIT),
        cost_estimate=pl.CostEstimate(
            flops=cost, bytes_accessed=4_000_000, transcendentals=300_000
        ),
        interpret=interpret,
    )(*operands)


def passed_buffers():
    return [pltpu.VMEM((count, CH, WIDTH), F32) for _, _, count, _, _ in BLOCKS]


def band_buffers():
    return [pltpu.VMEM((20, 3 * CH, WIDTH), BF16), pltpu.VMEM((18, CH, WIDTH), BF16)]


def run_level(flags, cols, table, wu, wm, sources, own, interpret=False):
    half = jax.ShapeDtypeStruct((HALF, CH, WIDTH), BF16)
    edge = jax.ShapeDtypeStruct((2, CH, WIDTH), BF16)
    operands = [flags, cols, table, wu, wm] + [p for s in sources for p in s] + list(own)
    scratch = [pltpu.VMEM((len(sources), 32, CH, WIDTH), BF16)]
    return on_core(
        functools.partial(level_kernel, len(sources)),
        (half, half, edge, edge),
        scratch + band_buffers() + passed_buffers(),
        3_000_000_000,
        operands,
        interpret,
    )


def run_warp(flags, cols, table, pieces, interpret=False):
    return on_core(
        warp_kernel,
        (jax.ShapeDtypeStruct((20, CH, WIDTH), BF16),) * 2,
        [pltpu.VMEM((32, CH, WIDTH), BF16), pltpu.VMEM((2, 20, CH, WIDTH), BF16)]
        + passed_buffers(),
        1_500_000_000,
        [flags, cols, table, *pieces],
        interpret,
    )


def run_last(flags, wu, wm, own, warped, interpret=False):
    return on_core(
        last_kernel,
        (jax.ShapeDtypeStruct((2 * HALF, CH, WIDTH), BF16),),
        band_buffers(),
        1_500_000_000,
        [flags, wu, wm, *own, *warped],
        interpret,
    )[0]


def send(x, frame_to=lambda t: t, row_to=lambda r: r):
    frames, rows = lax.axis_size("tm"), lax.axis_size("rows")
    route = [
        (t * rows + r, (frame_to(t) % frames) * rows + row_to(r))
        for t in range(frames)
        for r in range(rows)
        if 0 <= row_to(r) < rows
    ]
    return lax.ppermute(x, ("tm", "rows"), route)


def off_chip(r):
    return r + 1 if r % 2 else r - 1


def on_chip(r):
    return r ^ 1


def level_values(t):
    t = t.reshape(2, 2, 2, 4, 32)
    t = jnp.transpose(t, (1, 3, 0, 2, 4)).reshape(2, 4, 4, 32)
    return jnp.pad(t, ((0, 0), (0, 0), (0, 4), (0, 0))).reshape(64, 32)


def tap_weights(w):
    o, j = w.shape[2], w.shape[3]
    return jnp.transpose(w, (1, 2, 0, 3)).reshape(3 * o, 3 * j)


def with_table(rows, entries):
    plane = jnp.pad(entries.reshape(3, WIDTH), ((0, CH - 3), (0, 0)))
    return jnp.concatenate([rows, plane[None]])


def table_of(payload):
    return payload[2, 0:3].reshape(2, LEVELS, 4, 1, 32)


def shards(features, block_shift, quarter_pel, update_mask, uniting_weight, mixing_weight):
    band = features[0]
    row = lax.axis_index("rows")
    rows = lax.axis_size("rows")
    turned = row % 2
    edge = lax.dynamic_slice_in_dim(band, 8 * turned, HALF, axis=0)
    inner = lax.dynamic_slice_in_dim(band, 8 - 8 * turned, HALF, axis=0)
    rim = lax.dynamic_slice_in_dim(band, 14 * turned, 2, axis=0)
    near = lax.dynamic_slice_in_dim(band, 14 - 14 * turned, 2, axis=0)
    wu, wm = tap_weights(uniting_weight), tap_weights(mixing_weight)
    common = [turned, (row > 0).astype(jnp.int32), (row < rows - 1).astype(jnp.int32)]
    swapped = (lax.axis_index("tm") % 4 < 2).astype(jnp.int32)
    flags = [jnp.stack(common + [update_mask[k, 0], swapped]) for k in range(LEVELS)]

    def to_other(t):
        return t + 4

    def across(t):
        return t + 2 if t % 4 < 2 else t - 2

    def ahead(t):
        return t + 1

    def back(t):
        return t - 1

    own = jnp.stack([block_shift[:, :, 0], quarter_pel[:, :, 0]]).astype(BF16)
    at_edge = jnp.where(turned == 1, own[:, :, :, 1], own[:, :, :, 0])
    at_near = jnp.where(turned == 1, own[:, :, :, 0], own[:, :, :, 1])

    e = send(edge, to_other)
    h = send(edge, to_other, off_chip)
    i = send(inner, to_other)
    own_outer = send(with_table(rim, at_edge), row_to=off_chip)
    own_near = send(with_table(near, at_near), row_to=on_chip)
    n = send(i, row_to=on_chip)
    outer_table, near_table = table_of(own_outer), table_of(own_near)
    packed = jnp.concatenate(
        [
            jnp.where(turned == 1, near_table, outer_table),
            own,
            jnp.where(turned == 1, outer_table, near_table),
        ],
        axis=3,
    )
    cols, table = make_columns(level_values(packed[:, 2]))
    edge, inner, rim, near = run_level(
        flags[2], cols, table, wu, wm, [(h, e, i, n)], (own_outer, edge, inner, own_near)
    )

    own_outer = send(rim, row_to=off_chip)
    own_near = send(near, row_to=on_chip)
    e = send(edge, across)
    i = send(inner, across)
    h = send(edge, across, off_chip)
    xe = send(e, to_other)
    xh = send(e, to_other, off_chip)
    xi = send(i, to_other)
    n = send(i, row_to=on_chip)
    for_ahead = send(packed[:, 0, 0:2], back)
    for_back = send(packed[:, 0, 2:4], ahead)
    xn = send(xi, row_to=on_chip)
    cols, table = make_columns(level_values(packed[:, 1]))
    edge, inner, _, _ = run_level(
        flags[1],
        cols,
        table,
        wu,
        wm,
        [(h, e, i, n), (xh, xe, xi, xn)],
        (own_outer, edge, inner, own_near),
    )

    outer = send(edge, row_to=off_chip)
    near = send(inner, row_to=on_chip)
    cols, table = make_columns(
        level_values(jnp.concatenate([for_ahead, for_back], axis=1))
    )
    own = (outer, edge, inner, near)
    to_ahead, to_back = run_warp(flags[0], cols, table, own)
    earlier = send(to_ahead, ahead)
    later = send(to_back, back)
    return run_last(flags[0], wu, wm, own, (earlier, later))[None]


def solution(mesh):
    placed = (
        P("tm", "rows", None, None),
        P(None, None, "tm", "rows", None),
        P(None, None, "tm", "rows", None),
        P(None, "tm"),
        P(),
        P(),
    )
    return jax.shard_map(
        shards, mesh=mesh, in_specs=placed, out_specs=P("tm", "rows", None, None), check_vma=False
    )
```

```python
import functools

import jax
import jax.numpy as jnp
from jax import lax
from jax.experimental import pallas as pl
from jax.experimental.pallas import tpu as pltpu
from jax.sharding import PartitionSpec as P


LEVELS = 3
CH = 64
WIDTH = 256
HALF = 8
VMEM_LIMIT = 16 << 20
F32 = jnp.float32
BF16 = jnp.bfloat16


def pick_rows(v, bits, w0, w1, outs):
    b8, b4, b2, b1 = bits
    n8, n4, n2, n1 = outs + 8, outs + 4, outs + 2, outs + 1
    x8 = [jnp.where(b8, v[j + 8], v[j]) if j < outs + 3 else v[j] for j in range(n8)]
    x4 = [jnp.where(b4, x8[j + 4], x8[j]) for j in range(n4)]
    x2 = [jnp.where(b2, x4[j + 2], x4[j]) for j in range(n2)]
    x1 = [jnp.where(b1, x2[j + 1], x2[j]) for j in range(n1)]
    return [w0 * x1[i] + w1 * x1[i + 1] for i in range(outs)]


BLOCKS = ((1, 3, 19, 8, 2), (2, 11, 19, 8, 10), (0, 1, 13, 2, 0), (3, 19, 13, 2, 18))
OWN = slice(2 * CH, 3 * CH)


def turn(turned, place, size):
    return place + turned * (size - 2 * place)


def columns_kernel(vals, cols, table):
    block_of = lax.broadcasted_iota(jnp.int32, (32, WIDTH), 1) // 8
    spread = (block_of == lax.broadcasted_iota(jnp.int32, (32, WIDTH), 0)).astype(F32)
    table[...] = jnp.dot(vals[...], spread.astype(BF16), preferred_element_type=F32)
    apart = lax.broadcasted_iota(jnp.int32, (WIDTH, WIDTH), 0) - lax.broadcasted_iota(
        jnp.int32, (WIDTH, WIDTH), 1
    )

    @pl.loop(0, cols.shape[0])
    def _(n):
        entry = table[pl.ds(pl.multiple_of(n * 8, 8), 8), :]
        off = apart - entry[1:2].astype(jnp.int32)
        fx = entry[3:4] * 0.25
        cols[n] = jnp.where(off == 0, 1.0 - fx, jnp.where(off == 1, fx, 0.0)).astype(BF16)


def make_columns(vals, interpret=False):
    count = vals.shape[0] // 8
    vmem = pl.BlockSpec(memory_space=pltpu.VMEM)
    return pl.pallas_call(
        columns_kernel,
        out_shape=(
            jax.ShapeDtypeStruct((count, WIDTH, WIDTH), BF16),
            jax.ShapeDtypeStruct((count * 8, WIDTH), F32),
        ),
        in_specs=[vmem],
        out_specs=(vmem, vmem),
        compiler_params=pltpu.CompilerParams(vmem_limit_bytes=VMEM_LIMIT),
        cost_estimate=pl.CostEstimate(
            flops=100_000_000, bytes_accessed=3_000_000, transcendentals=0
        ),
        interpret=interpret,
    )(vals)


def warp_into(flags, cols, table, source_of, passed, put_of):
    has_above = (flags[1] > 0).astype(F32)
    has_below = (flags[2] > 0).astype(F32)
    lanes = (16, WIDTH)

    @pl.loop(0, 2)
    def _(which):
        put = put_of(which)

        def column_pass(k):
            block, first, count, _, _ = BLOCKS[k]
            window = source_of(which, first, count).reshape(count * CH, WIDTH)
            passed[k][...] = jnp.dot(
                window, cols[which * 4 + block], preferred_element_type=F32
            ).reshape(count, CH, WIDTH)

        def row_pass(k):
            block, _, count, outs, start = BLOCKS[k]
            at = (which * 4 + block) * 8
            entry = table[pl.ds(pl.multiple_of(at, 8), 8), :]
            s = entry[0:1].astype(jnp.int32) + 5
            keep = {0: has_above, 3: has_below}.get(block, 1.0)
            bits = [jnp.broadcast_to((s & b) != 0, lanes) for b in (8, 4, 2, 1)]
            fy = entry[2:3] * 0.25
            w1 = jnp.broadcast_to(fy * keep, lanes)
            w0 = jnp.broadcast_to((1.0 - fy) * keep, lanes)
            for c in range(CH // 16):
                v = [passed[k][u, 16 * c : 16 * c + 16, :] for u in range(count)]
                for i, row in enumerate(pick_rows(v, bits, w0, w1, outs)):
                    put(start + i, 16 * c, row.astype(BF16))

        column_pass(0)
        for k in range(4):
            if k < 3:
                column_pass(k + 1)
            row_pass(k)


def convolve_band(flags, wu, wm, joined, act, final, outs):
    has_above = flags[1] > 0
    has_below = flags[2] > 0
    turned = flags[0]
    lane = lax.broadcasted_iota(jnp.int32, (CH, WIDTH), 1)
    not_first = lane > 0
    not_last = lane < WIDTH - 1

    def gather_taps(s):
        left = jnp.where(not_first, pltpu.roll(s[0:CH], 1, 1), 0.0)
        right = jnp.where(not_last, pltpu.roll(s[2 * CH :], WIDTH - 1, 1), 0.0)
        return s[CH : 2 * CH] + left + right

    def activate(a):
        window = joined[pl.ds(a, 3)].reshape(9 * CH, WIDTH)
        total = gather_taps(jnp.dot(wu[...], window, preferred_element_type=F32))
        half = 0.5 * total
        value = half + half * jnp.tanh(half)
        keep = jnp.where(
            a == 0, has_above, jnp.where(a == 17, has_below, True)
        ).astype(F32)
        act[a] = (value * keep).astype(BF16)

    @pl.loop(0, 3)
    def _(n):
        for k in range(6):
            activate(6 * n + k)

    scale = flags[3].astype(F32)

    def finish(y):
        window = act[pl.ds(y, 3)].reshape(3 * CH, WIDTH)
        total = gather_taps(jnp.dot(wm[...], window, preferred_element_type=F32))
        own = joined[y + 2, OWN, :].astype(F32)
        return (own + scale * total).astype(BF16)

    if final:
        (out,) = outs

        @pl.loop(0, 2)
        def _(n):
            for k in range(8):
                out[8 * n + k] = finish(8 * n + k)

    else:
        out_edge, out_inner, out_rim, out_near = outs

        @pl.loop(0, 2)
        def _(n):
            for k in range(4):
                y = 4 * n + k
                out_edge[y] = finish(y + turn(turned, 0, 8))
                out_inner[y] = finish(y + turn(turned, 8, 8))

        out_rim[...] = out_edge[pl.ds(turn(turned, 0, 6), 2)]
        out_near[...] = out_inner[pl.ds(turn(turned, 6, 6), 2)]


def stack_rows(target, turned, pieces):
    for p in range(4):
        target[pl.ds(turn(turned, 8 * p, 24), 8)] = pieces[p][...]


def level_kernel(sources, flags, cols, table, wu, wm, *refs):
    own_outer, own_edge, own_inner, own_near = refs[4 * sources : 4 * sources + 4]
    outs = refs[4 * sources + 4 : 4 * sources + 8]
    src, joined, act = refs[4 * sources + 8 : 4 * sources + 11]
    passed = refs[4 * sources + 11 :]
    turned = flags[0]
    for i in range(sources):
        stack_rows(src.at[i], turned, refs[4 * i : 4 * i + 4])
    joined[pl.ds(turn(turned, 0, 18), 2), OWN] = own_outer[0:2]
    joined[pl.ds(turn(turned, 2, 12), 8), OWN] = own_edge[...]
    joined[pl.ds(turn(turned, 10, 12), 8), OWN] = own_inner[...]
    joined[pl.ds(turn(turned, 18, 18), 2), OWN] = own_near[0:2]

    def source_of(which, first, count):
        return src[which ^ flags[4] if sources == 2 else 0, first : first + count]

    def put_of(which):
        def put(row, c, value):
            joined[row, pl.ds(pl.multiple_of(which * CH + c, 16), 16), :] = value

        return put

    warp_into(flags, cols, table, source_of, passed, put_of)
    convolve_band(flags, wu, wm, joined, act, False, outs)


def warp_kernel(flags, cols, table, outer, edge, inner, near, ahead, back, src, both, *passed):
    stack_rows(src, flags[0], (outer, edge, inner, near))

    def source_of(which, first, count):
        return src[first : first + count]

    def put_of(which):
        def put(row, c, value):
            both[which, row, c : c + 16, :] = value

        return put

    warp_into(flags, cols, table, source_of, passed, put_of)
    ahead[...] = both[0]
    back[...] = both[1]


def last_kernel(flags, wu, wm, outer, edge, inner, near, earlier, later, out, joined, act):
    turned = flags[0]
    joined[pl.ds(turn(turned, 0, 18), 2), OWN] = outer[pl.ds(turn(turned, 6, 6), 2)]
    joined[pl.ds(turn(turned, 2, 12), 8), OWN] = edge[...]
    joined[pl.ds(turn(turned, 10, 12), 8), OWN] = inner[...]
    joined[pl.ds(turn(turned, 18, 18), 2), OWN] = near[pl.ds(turn(turned, 0, 6), 2)]
    joined[:, 0:CH] = earlier[...]
    joined[:, CH : 2 * CH] = later[...]
    convolve_band(flags, wu, wm, joined, act, True, (out,))


def on_core(kernel, out_shape, scratch, cost, operands, interpret):
    vmem = pl.BlockSpec(memory_space=pltpu.VMEM)
    return pl.pallas_call(
        kernel,
        out_shape=out_shape,
        in_specs=[pl.BlockSpec(memory_space=pltpu.SMEM)] + [vmem] * (len(operands) - 1),
        out_specs=(vmem,) * len(out_shape),
        scratch_shapes=scratch,
        compiler_params=pltpu.CompilerParams(vmem_limit_bytes=VMEM_LIMIT),
        cost_estimate=pl.CostEstimate(
            flops=cost, bytes_accessed=4_000_000, transcendentals=300_000
        ),
        interpret=interpret,
    )(*operands)


def passed_buffers():
    return [pltpu.VMEM((count, CH, WIDTH), F32) for _, _, count, _, _ in BLOCKS]


def band_buffers():
    return [pltpu.VMEM((20, 3 * CH, WIDTH), BF16), pltpu.VMEM((18, CH, WIDTH), BF16)]


def run_level(flags, cols, table, wu, wm, sources, own, interpret=False):
    half = jax.ShapeDtypeStruct((HALF, CH, WIDTH), BF16)
    edge = jax.ShapeDtypeStruct((2, CH, WIDTH), BF16)
    operands = [flags, cols, table, wu, wm] + [p for s in sources for p in s] + list(own)
    scratch = [pltpu.VMEM((len(sources), 32, CH, WIDTH), BF16)]
    return on_core(
        functools.partial(level_kernel, len(sources)),
        (half, half, edge, edge),
        scratch + band_buffers() + passed_buffers(),
        3_000_000_000,
        operands,
        interpret,
    )


def run_warp(flags, cols, table, pieces, interpret=False):
    return on_core(
        warp_kernel,
        (jax.ShapeDtypeStruct((20, CH, WIDTH), BF16),) * 2,
        [pltpu.VMEM((32, CH, WIDTH), BF16), pltpu.VMEM((2, 20, CH, WIDTH), BF16)]
        + passed_buffers(),
        1_500_000_000,
        [flags, cols, table, *pieces],
        interpret,
    )


def run_last(flags, wu, wm, own, warped, interpret=False):
    return on_core(
        last_kernel,
        (jax.ShapeDtypeStruct((2 * HALF, CH, WIDTH), BF16),),
        band_buffers(),
        1_500_000_000,
        [flags, wu, wm, *own, *warped],
        interpret,
    )[0]


def send(x, frame_to=lambda t: t, row_to=lambda r: r):
    frames, rows = lax.axis_size("tm"), lax.axis_size("rows")
    route = [
        (t * rows + r, (frame_to(t) % frames) * rows + row_to(r))
        for t in range(frames)
        for r in range(rows)
        if 0 <= row_to(r) < rows
    ]
    return lax.ppermute(x, ("tm", "rows"), route)


def off_chip(r):
    return r + 1 if r % 2 else r - 1


def on_chip(r):
    return r ^ 1


def level_values(t):
    t = t.reshape(2, 2, 2, 4, 32)
    t = jnp.transpose(t, (1, 3, 0, 2, 4)).reshape(2, 4, 4, 32)
    return jnp.pad(t, ((0, 0), (0, 0), (0, 4), (0, 0))).reshape(64, 32)


def tap_weights(w):
    o, j = w.shape[2], w.shape[3]
    return jnp.transpose(w, (1, 2, 0, 3)).reshape(3 * o, 3 * j)


def with_table(rows, entries):
    plane = jnp.pad(entries.reshape(3, WIDTH), ((0, CH - 3), (0, 0)))
    return jnp.concatenate([rows, plane[None]])


def table_of(payload):
    return payload[2, 0:3].reshape(2, LEVELS, 4, 1, 32)


def shards(features, block_shift, quarter_pel, update_mask, uniting_weight, mixing_weight):
    band = features[0]
    row = lax.axis_index("rows")
    rows = lax.axis_size("rows")
    turned = row % 2
    edge = lax.dynamic_slice_in_dim(band, 8 * turned, HALF, axis=0)
    inner = lax.dynamic_slice_in_dim(band, 8 - 8 * turned, HALF, axis=0)
    rim = lax.dynamic_slice_in_dim(band, 14 * turned, 2, axis=0)
    near = lax.dynamic_slice_in_dim(band, 14 - 14 * turned, 2, axis=0)
    wu, wm = tap_weights(uniting_weight), tap_weights(mixing_weight)
    common = [turned, (row > 0).astype(jnp.int32), (row < rows - 1).astype(jnp.int32)]
    swapped = (lax.axis_index("tm") % 4 < 2).astype(jnp.int32)
    flags = [jnp.stack(common + [update_mask[k, 0], swapped]) for k in range(LEVELS)]

    def to_other(t):
        return t + 4

    def across(t):
        return t + 2 if t % 4 < 2 else t - 2

    def ahead(t):
        return t + 1

    def back(t):
        return t - 1

    own = jnp.stack([block_shift[:, :, 0], quarter_pel[:, :, 0]]).astype(BF16)
    at_edge = jnp.where(turned == 1, own[:, :, :, 1], own[:, :, :, 0])
    at_near = jnp.where(turned == 1, own[:, :, :, 0], own[:, :, :, 1])

    e = send(edge, to_other)
    h = send(edge, to_other, off_chip)
    i = send(inner, to_other)
    own_outer = send(with_table(rim, at_edge), row_to=off_chip)
    own_near = send(with_table(near, at_near), row_to=on_chip)
    n = send(i, row_to=on_chip)
    outer_table, near_table = table_of(own_outer), table_of(own_near)
    packed = jnp.concatenate(
        [
            jnp.where(turned == 1, near_table, outer_table),
            own,
            jnp.where(turned == 1, outer_table, near_table),
        ],
        axis=3,
    )
    cols, table = make_columns(level_values(packed[:, 2]))
    edge, inner, rim, near = run_level(
        flags[2], cols, table, wu, wm, [(h, e, i, n)], (own_outer, edge, inner, own_near)
    )

    own_outer = send(rim, row_to=off_chip)
    own_near = send(near, row_to=on_chip)
    e = send(edge, across)
    i = send(inner, across)
    xe = send(e, to_other)
    xh = send(e, to_other, off_chip)
    h = send(xe, to_other, off_chip)
    xi = send(i, to_other)
    n = send(i, row_to=on_chip)
    for_ahead = send(packed[:, 0, 0:2], back)
    for_back = send(packed[:, 0, 2:4], ahead)
    xn = send(xi, row_to=on_chip)
    cols, table = make_columns(level_values(packed[:, 1]))
    edge, inner, _, _ = run_level(
        flags[1],
        cols,
        table,
        wu,
        wm,
        [(h, e, i, n), (xh, xe, xi, xn)],
        (own_outer, edge, inner, own_near),
    )

    outer = send(edge, row_to=off_chip)
    near = send(inner, row_to=on_chip)
    cols, table = make_columns(
        level_values(jnp.concatenate([for_ahead, for_back], axis=1))
    )
    own = (outer, edge, inner, near)
    to_ahead, to_back = run_warp(flags[0], cols, table, own)
    earlier = send(to_ahead, ahead)
    later = send(to_back, back)
    return run_last(flags[0], wu, wm, own, (earlier, later))[None]


def solution(mesh):
    placed = (
        P("tm", "rows", None, None),
        P(None, None, "tm", "rows", None),
        P(None, None, "tm", "rows", None),
        P(None, "tm"),
        P(),
        P(),
    )
    return jax.shard_map(
        shards, mesh=mesh, in_specs=placed, out_specs=P("tm", "rows", None, None), check_vma=False
    )
```

```python
import functools

import jax
import jax.numpy as jnp
from jax import lax
from jax.experimental import pallas as pl
from jax.experimental.pallas import tpu as pltpu
from jax.sharding import PartitionSpec as P


LEVELS = 3
CH = 64
WIDTH = 256
HALF = 8
VMEM_LIMIT = 16 << 20
F32 = jnp.float32
BF16 = jnp.bfloat16


def pick_rows(v, bits, w0, w1, outs):
    b8, b4, b2, b1 = bits
    n8, n4, n2, n1 = outs + 8, outs + 4, outs + 2, outs + 1
    x8 = [jnp.where(b8, v[j + 8], v[j]) if j < outs + 3 else v[j] for j in range(n8)]
    x4 = [jnp.where(b4, x8[j + 4], x8[j]) for j in range(n4)]
    x2 = [jnp.where(b2, x4[j + 2], x4[j]) for j in range(n2)]
    x1 = [jnp.where(b1, x2[j + 1], x2[j]) for j in range(n1)]
    return [w0 * x1[i] + w1 * x1[i + 1] for i in range(outs)]


BLOCKS = ((1, 3, 19, 8, 2), (2, 11, 19, 8, 10), (0, 1, 13, 2, 0), (3, 19, 13, 2, 18))
OWN = slice(2 * CH, 3 * CH)


def turn(turned, place, size):
    return place + turned * (size - 2 * place)


def columns_kernel(vals, cols, table):
    block_of = lax.broadcasted_iota(jnp.int32, (32, WIDTH), 1) // 8
    spread = (block_of == lax.broadcasted_iota(jnp.int32, (32, WIDTH), 0)).astype(F32)
    table[...] = jnp.dot(vals[...], spread.astype(BF16), preferred_element_type=F32)
    apart = lax.broadcasted_iota(jnp.int32, (WIDTH, WIDTH), 0) - lax.broadcasted_iota(
        jnp.int32, (WIDTH, WIDTH), 1
    )

    @pl.loop(0, cols.shape[0])
    def _(n):
        entry = table[pl.ds(pl.multiple_of(n * 8, 8), 8), :]
        off = apart - entry[1:2].astype(jnp.int32)
        fx = entry[3:4] * 0.25
        cols[n] = jnp.where(off == 0, 1.0 - fx, jnp.where(off == 1, fx, 0.0)).astype(BF16)


def make_columns(vals, interpret=False):
    count = vals.shape[0] // 8
    vmem = pl.BlockSpec(memory_space=pltpu.VMEM)
    return pl.pallas_call(
        columns_kernel,
        out_shape=(
            jax.ShapeDtypeStruct((count, WIDTH, WIDTH), BF16),
            jax.ShapeDtypeStruct((count * 8, WIDTH), F32),
        ),
        in_specs=[vmem],
        out_specs=(vmem, vmem),
        compiler_params=pltpu.CompilerParams(vmem_limit_bytes=VMEM_LIMIT),
        cost_estimate=pl.CostEstimate(
            flops=100_000_000, bytes_accessed=3_000_000, transcendentals=0
        ),
        interpret=interpret,
    )(vals)


def warp_into(flags, cols, table, source_of, passed, put_of):
    has_above = (flags[1] > 0).astype(F32)
    has_below = (flags[2] > 0).astype(F32)
    lanes = (16, WIDTH)

    @pl.loop(0, 2)
    def _(which):
        put = put_of(which)

        def column_pass(k):
            block, first, count, _, _ = BLOCKS[k]
            window = source_of(which, first, count).reshape(count * CH, WIDTH)
            passed[k][...] = jnp.dot(
                window, cols[which * 4 + block], preferred_element_type=F32
            ).reshape(count, CH, WIDTH)

        def row_pass(k):
            block, _, count, outs, start = BLOCKS[k]
            at = (which * 4 + block) * 8
            entry = table[pl.ds(pl.multiple_of(at, 8), 8), :]
            s = entry[0:1].astype(jnp.int32) + 5
            keep = {0: has_above, 3: has_below}.get(block, 1.0)
            bits = [jnp.broadcast_to((s & b) != 0, lanes) for b in (8, 4, 2, 1)]
            fy = entry[2:3] * 0.25
            w1 = jnp.broadcast_to(fy * keep, lanes)
            w0 = jnp.broadcast_to((1.0 - fy) * keep, lanes)
            for c in range(CH // 16):
                v = [passed[k][u, 16 * c : 16 * c + 16, :] for u in range(count)]
                for i, row in enumerate(pick_rows(v, bits, w0, w1, outs)):
                    put(start + i, 16 * c, row.astype(BF16))

        column_pass(0)
        for k in range(4):
            if k < 3:
                column_pass(k + 1)
            row_pass(k)


def convolve_band(flags, wu, wm, joined, act, final, outs):
    has_above = flags[1] > 0
    has_below = flags[2] > 0
    turned = flags[0]
    lane = lax.broadcasted_iota(jnp.int32, (CH, WIDTH), 1)
    not_first = lane > 0
    not_last = lane < WIDTH - 1

    def gather_taps(s):
        left = jnp.where(not_first, pltpu.roll(s[0:CH], 1, 1), 0.0)
        right = jnp.where(not_last, pltpu.roll(s[2 * CH :], WIDTH - 1, 1), 0.0)
        return s[CH : 2 * CH] + left + right

    def activate(a):
        window = joined[pl.ds(a, 3)].reshape(9 * CH, WIDTH)
        total = gather_taps(jnp.dot(wu[...], window, preferred_element_type=F32))
        half = 0.5 * total
        value = half + half * jnp.tanh(half)
        keep = jnp.where(
            a == 0, has_above, jnp.where(a == 17, has_below, True)
        ).astype(F32)
        act[a] = (value * keep).astype(BF16)

    @pl.loop(0, 3)
    def _(n):
        for k in range(6):
            activate(6 * n + k)

    scale = flags[3].astype(F32)

    def finish(y):
        window = act[pl.ds(y, 3)].reshape(3 * CH, WIDTH)
        total = gather_taps(jnp.dot(wm[...], window, preferred_element_type=F32))
        own = joined[y + 2, OWN, :].astype(F32)
        return (own + scale * total).astype(BF16)

    if final:
        (out,) = outs

        @pl.loop(0, 2)
        def _(n):
            for k in range(8):
                out[8 * n + k] = finish(8 * n + k)

    else:
        out_edge, out_inner, out_rim, out_near = outs

        @pl.loop(0, 2)
        def _(n):
            for k in range(4):
                y = 4 * n + k
                out_edge[y] = finish(y + turn(turned, 0, 8))
                out_inner[y] = finish(y + turn(turned, 8, 8))

        out_rim[...] = out_edge[pl.ds(turn(turned, 0, 6), 2)]
        out_near[...] = out_inner[pl.ds(turn(turned, 6, 6), 2)]


def stack_rows(target, turned, pieces):
    for p in range(4):
        target[pl.ds(turn(turned, 8 * p, 24), 8)] = pieces[p][...]


def level_kernel(sources, flags, cols, table, wu, wm, *refs):
    own_outer, own_edge, own_inner, own_near = refs[4 * sources : 4 * sources + 4]
    outs = refs[4 * sources + 4 : 4 * sources + 8]
    src, joined, act = refs[4 * sources + 8 : 4 * sources + 11]
    passed = refs[4 * sources + 11 :]
    turned = flags[0]
    for i in range(sources):
        stack_rows(src.at[i], turned, refs[4 * i : 4 * i + 4])
    joined[pl.ds(turn(turned, 0, 18), 2), OWN] = own_outer[0:2]
    joined[pl.ds(turn(turned, 2, 12), 8), OWN] = own_edge[...]
    joined[pl.ds(turn(turned, 10, 12), 8), OWN] = own_inner[...]
    joined[pl.ds(turn(turned, 18, 18), 2), OWN] = own_near[0:2]

    def source_of(which, first, count):
        return src[which ^ flags[4] if sources == 2 else 0, first : first + count]

    def put_of(which):
        def put(row, c, value):
            joined[row, pl.ds(pl.multiple_of(which * CH + c, 16), 16), :] = value

        return put

    warp_into(flags, cols, table, source_of, passed, put_of)
    convolve_band(flags, wu, wm, joined, act, False, outs)


def warp_kernel(flags, cols, table, outer, edge, inner, near, ahead, back, src, both, *passed):
    stack_rows(src, flags[0], (outer, edge, inner, near))

    def source_of(which, first, count):
        return src[first : first + count]

    def put_of(which):
        def put(row, c, value):
            both[which, row, c : c + 16, :] = value

        return put

    warp_into(flags, cols, table, source_of, passed, put_of)
    ahead[...] = both[0]
    back[...] = both[1]


def last_kernel(flags, wu, wm, outer, edge, inner, near, earlier, later, out, joined, act):
    turned = flags[0]
    joined[pl.ds(turn(turned, 0, 18), 2), OWN] = outer[pl.ds(turn(turned, 6, 6), 2)]
    joined[pl.ds(turn(turned, 2, 12), 8), OWN] = edge[...]
    joined[pl.ds(turn(turned, 10, 12), 8), OWN] = inner[...]
    joined[pl.ds(turn(turned, 18, 18), 2), OWN] = near[pl.ds(turn(turned, 0, 6), 2)]
    joined[:, 0:CH] = earlier[...]
    joined[:, CH : 2 * CH] = later[...]
    convolve_band(flags, wu, wm, joined, act, True, (out,))


def on_core(kernel, out_shape, scratch, cost, operands, interpret):
    vmem = pl.BlockSpec(memory_space=pltpu.VMEM)
    return pl.pallas_call(
        kernel,
        out_shape=out_shape,
        in_specs=[pl.BlockSpec(memory_space=pltpu.SMEM)] + [vmem] * (len(operands) - 1),
        out_specs=(vmem,) * len(out_shape),
        scratch_shapes=scratch,
        compiler_params=pltpu.CompilerParams(vmem_limit_bytes=VMEM_LIMIT),
        cost_estimate=pl.CostEstimate(
            flops=cost, bytes_accessed=4_000_000, transcendentals=300_000
        ),
        interpret=interpret,
    )(*operands)


def passed_buffers():
    return [pltpu.VMEM((count, CH, WIDTH), F32) for _, _, count, _, _ in BLOCKS]


def band_buffers():
    return [pltpu.VMEM((20, 3 * CH, WIDTH), BF16), pltpu.VMEM((18, CH, WIDTH), BF16)]


def run_level(flags, cols, table, wu, wm, sources, own, interpret=False):
    half = jax.ShapeDtypeStruct((HALF, CH, WIDTH), BF16)
    edge = jax.ShapeDtypeStruct((2, CH, WIDTH), BF16)
    operands = [flags, cols, table, wu, wm] + [p for s in sources for p in s] + list(own)
    scratch = [pltpu.VMEM((len(sources), 32, CH, WIDTH), BF16)]
    return on_core(
        functools.partial(level_kernel, len(sources)),
        (half, half, edge, edge),
        scratch + band_buffers() + passed_buffers(),
        3_000_000_000,
        operands,
        interpret,
    )


def run_warp(flags, cols, table, pieces, interpret=False):
    return on_core(
        warp_kernel,
        (jax.ShapeDtypeStruct((20, CH, WIDTH), BF16),) * 2,
        [pltpu.VMEM((32, CH, WIDTH), BF16), pltpu.VMEM((2, 20, CH, WIDTH), BF16)]
        + passed_buffers(),
        1_500_000_000,
        [flags, cols, table, *pieces],
        interpret,
    )


def run_last(flags, wu, wm, own, warped, interpret=False):
    return on_core(
        last_kernel,
        (jax.ShapeDtypeStruct((2 * HALF, CH, WIDTH), BF16),),
        band_buffers(),
        1_500_000_000,
        [flags, wu, wm, *own, *warped],
        interpret,
    )[0]


def send(x, frame_to=lambda t: t, row_to=lambda r: r):
    frames, rows = lax.axis_size("tm"), lax.axis_size("rows")
    route = [
        (t * rows + r, (frame_to(t) % frames) * rows + row_to(r))
        for t in range(frames)
        for r in range(rows)
        if 0 <= row_to(r) < rows
    ]
    return lax.ppermute(x, ("tm", "rows"), route)


def off_chip(r):
    return r + 1 if r % 2 else r - 1


def on_chip(r):
    return r ^ 1


def level_values(t):
    t = t.reshape(2, 2, 2, 4, 32)
    t = jnp.transpose(t, (1, 3, 0, 2, 4)).reshape(2, 4, 4, 32)
    return jnp.pad(t, ((0, 0), (0, 0), (0, 4), (0, 0))).reshape(64, 32)


def tap_weights(w):
    o, j = w.shape[2], w.shape[3]
    return jnp.transpose(w, (1, 2, 0, 3)).reshape(3 * o, 3 * j)


def with_table(rows, entries):
    plane = jnp.pad(entries.reshape(3, WIDTH), ((0, CH - 3), (0, 0)))
    return jnp.concatenate([rows, plane[None]])


def table_of(payload):
    return payload[2, 0:3].reshape(2, LEVELS, 4, 1, 32)


def shards(features, block_shift, quarter_pel, update_mask, uniting_weight, mixing_weight):
    band = features[0]
    row = lax.axis_index("rows")
    rows = lax.axis_size("rows")
    turned = row % 2
    edge = lax.dynamic_slice_in_dim(band, 8 * turned, HALF, axis=0)
    inner = lax.dynamic_slice_in_dim(band, 8 - 8 * turned, HALF, axis=0)
    rim = lax.dynamic_slice_in_dim(band, 14 * turned, 2, axis=0)
    near = lax.dynamic_slice_in_dim(band, 14 - 14 * turned, 2, axis=0)
    wu, wm = tap_weights(uniting_weight), tap_weights(mixing_weight)
    common = [turned, (row > 0).astype(jnp.int32), (row < rows - 1).astype(jnp.int32)]
    swapped = (lax.axis_index("tm") % 4 < 2).astype(jnp.int32)
    flags = [jnp.stack(common + [update_mask[k, 0], swapped]) for k in range(LEVELS)]

    def to_other(t):
        return t + 4

    def across(t):
        return t + 2 if t % 4 < 2 else t - 2

    def ahead(t):
        return t + 1

    def back(t):
        return t - 1

    own = jnp.stack([block_shift[:, :, 0], quarter_pel[:, :, 0]]).astype(BF16)
    at_edge = jnp.where(turned == 1, own[:, :, :, 1], own[:, :, :, 0])
    at_near = jnp.where(turned == 1, own[:, :, :, 0], own[:, :, :, 1])

    e = send(edge, to_other)
    h = send(edge, to_other, off_chip)
    i = send(inner, to_other)
    own_outer = send(with_table(rim, at_edge), row_to=off_chip)
    own_near = send(with_table(near, at_near), row_to=on_chip)
    n = send(i, row_to=on_chip)
    outer_table, near_table = table_of(own_outer), table_of(own_near)
    packed = jnp.concatenate(
        [
            jnp.where(turned == 1, near_table, outer_table),
            own,
            jnp.where(turned == 1, outer_table, near_table),
        ],
        axis=3,
    )
    values, later_values, ahead_entries, back_entries, wu, wm, *flags = (
        lax.optimization_barrier(
            (
                level_values(packed[:, 2]),
                level_values(packed[:, 1]),
                packed[:, 0, 0:2],
                packed[:, 0, 2:4],
                wu,
                wm,
                *flags,
            )
        )
    )
    cols, table = make_columns(values)
    edge, inner, rim, near = run_level(
        flags[2], cols, table, wu, wm, [(h, e, i, n)], (own_outer, edge, inner, own_near)
    )

    own_outer = send(rim, row_to=off_chip)
    own_near = send(near, row_to=on_chip)
    e = send(edge, across)
    i = send(inner, across)
    xe = send(e, to_other)
    xh = send(e, to_other, off_chip)
    h = send(xe, to_other, off_chip)
    xi = send(i, to_other)
    n = send(i, row_to=on_chip)
    for_ahead = send(ahead_entries, back)
    for_back = send(back_entries, ahead)
    xn = send(xi, row_to=on_chip)
    cols, table = make_columns(later_values)
    edge, inner, _, _ = run_level(
        flags[1],
        cols,
        table,
        wu,
        wm,
        [(h, e, i, n), (xh, xe, xi, xn)],
        (own_outer, edge, inner, own_near),
    )

    outer = send(edge, row_to=off_chip)
    near = send(inner, row_to=on_chip)
    cols, table = make_columns(
        level_values(jnp.concatenate([for_ahead, for_back], axis=1))
    )
    own = (outer, edge, inner, near)
    to_ahead, to_back = run_warp(flags[0], cols, table, own)
    earlier = send(to_ahead, ahead)
    later = send(to_back, back)
    return run_last(flags[0], wu, wm, own, (earlier, later))[None]


def solution(mesh):
    placed = (
        P("tm", "rows", None, None),
        P(None, None, "tm", "rows", None),
        P(None, None, "tm", "rows", None),
        P(None, "tm"),
        P(),
        P(),
    )
    return jax.shard_map(
        shards, mesh=mesh, in_specs=placed, out_specs=P("tm", "rows", None, None), check_vma=False
    )
```

```python
import functools

import jax
import jax.numpy as jnp
from jax import lax
from jax.experimental import pallas as pl
from jax.experimental.pallas import tpu as pltpu
from jax.sharding import PartitionSpec as P


LEVELS = 3
CH = 64
WIDTH = 256
HALF = 8
VMEM_LIMIT = 16 << 20
F32 = jnp.float32
BF16 = jnp.bfloat16


def pick_rows(v, bits, w0, w1, outs):
    b8, b4, b2, b1 = bits
    n8, n4, n2, n1 = outs + 8, outs + 4, outs + 2, outs + 1
    x8 = [jnp.where(b8, v[j + 8], v[j]) if j < outs + 3 else v[j] for j in range(n8)]
    x4 = [jnp.where(b4, x8[j + 4], x8[j]) for j in range(n4)]
    x2 = [jnp.where(b2, x4[j + 2], x4[j]) for j in range(n2)]
    x1 = [jnp.where(b1, x2[j + 1], x2[j]) for j in range(n1)]
    return [w0 * x1[i] + w1 * x1[i + 1] for i in range(outs)]


BLOCKS = ((1, 3, 19, 8, 2), (2, 11, 19, 8, 10), (0, 1, 13, 2, 0), (3, 19, 13, 2, 18))
OWN = slice(2 * CH, 3 * CH)


def turn(turned, place, size):
    return place + turned * (size - 2 * place)


def columns_kernel(vals, cols, table):
    block_of = lax.broadcasted_iota(jnp.int32, (32, WIDTH), 1) // 8
    spread = (block_of == lax.broadcasted_iota(jnp.int32, (32, WIDTH), 0)).astype(F32)
    table[...] = jnp.dot(vals[...], spread.astype(BF16), preferred_element_type=F32)
    apart = lax.broadcasted_iota(jnp.int32, (WIDTH, WIDTH), 0) - lax.broadcasted_iota(
        jnp.int32, (WIDTH, WIDTH), 1
    )

    @pl.loop(0, cols.shape[0])
    def _(n):
        entry = table[pl.ds(pl.multiple_of(n * 8, 8), 8), :]
        off = apart - entry[1:2].astype(jnp.int32)
        fx = entry[3:4] * 0.25
        cols[n] = jnp.where(off == 0, 1.0 - fx, jnp.where(off == 1, fx, 0.0)).astype(BF16)


def make_columns(vals, interpret=False):
    count = vals.shape[0] // 8
    vmem = pl.BlockSpec(memory_space=pltpu.VMEM)
    return pl.pallas_call(
        columns_kernel,
        out_shape=(
            jax.ShapeDtypeStruct((count, WIDTH, WIDTH), BF16),
            jax.ShapeDtypeStruct((count * 8, WIDTH), F32),
        ),
        in_specs=[vmem],
        out_specs=(vmem, vmem),
        compiler_params=pltpu.CompilerParams(vmem_limit_bytes=VMEM_LIMIT),
        cost_estimate=pl.CostEstimate(
            flops=100_000_000, bytes_accessed=3_000_000, transcendentals=0
        ),
        interpret=interpret,
    )(vals)


def column_pass(buffer, window, matrix):
    count = window.shape[0]
    buffer[...] = jnp.dot(
        window.reshape(count * CH, WIDTH), matrix, preferred_element_type=F32
    ).reshape(count, CH, WIDTH)


def row_pass(buffer, entry, keep, outs, put):
    lanes = (16, WIDTH)
    s = entry[0:1].astype(jnp.int32) + 5
    bits = [jnp.broadcast_to((s & b) != 0, lanes) for b in (8, 4, 2, 1)]
    fy = entry[2:3] * 0.25
    w1 = jnp.broadcast_to(fy * keep, lanes)
    w0 = jnp.broadcast_to((1.0 - fy) * keep, lanes)
    for c in range(CH // 16):
        v = [buffer[u, 16 * c : 16 * c + 16, :] for u in range(buffer.shape[0])]
        for i, row in enumerate(pick_rows(v, bits, w0, w1, outs)):
            put(i, 16 * c, row.astype(BF16))


def entry_at(table, n):
    return table[pl.ds(pl.multiple_of(n * 8, 8), 8), :]


def warp_into(flags, cols, table, source_of, passed, put_of):
    has_above = (flags[1] > 0).astype(F32)
    has_below = (flags[2] > 0).astype(F32)

    @pl.loop(0, 2)
    def _(which):
        put = put_of(which)

        def columns(k):
            block, first, count, _, _ = BLOCKS[k]
            column_pass(passed[k], source_of(which, first, count), cols[which * 4 + block])

        def rows(k):
            block, _, _, outs, start = BLOCKS[k]
            keep = {0: has_above, 3: has_below}.get(block, 1.0)
            row_pass(
                passed[k],
                entry_at(table, which * 4 + block),
                keep,
                outs,
                lambda i, c, value: put(start + i, c, value),
            )

        columns(0)
        for k in range(4):
            if k < 3:
                columns(k + 1)
            rows(k)


class Convolutions:
    def __init__(self, flags, wu, wm, joined, act):
        self.flags, self.wu, self.wm, self.joined, self.act = flags, wu, wm, joined, act
        lane = lax.broadcasted_iota(jnp.int32, (CH, WIDTH), 1)
        self.not_first = lane > 0
        self.not_last = lane < WIDTH - 1

    def gather_taps(self, s):
        left = jnp.where(self.not_first, pltpu.roll(s[0:CH], 1, 1), 0.0)
        right = jnp.where(self.not_last, pltpu.roll(s[2 * CH :], WIDTH - 1, 1), 0.0)
        return s[CH : 2 * CH] + left + right

    def activate(self, a):
        window = self.joined[pl.ds(a, 3)].reshape(9 * CH, WIDTH)
        total = self.gather_taps(jnp.dot(self.wu[...], window, preferred_element_type=F32))
        half = 0.5 * total
        value = half + half * jnp.tanh(half)
        inside = jnp.where(
            a == 0, self.flags[1] > 0, jnp.where(a == 17, self.flags[2] > 0, True)
        )
        self.act[a] = (value * inside.astype(F32)).astype(BF16)

    def finish(self, y):
        window = self.act[pl.ds(y, 3)].reshape(3 * CH, WIDTH)
        total = self.gather_taps(jnp.dot(self.wm[...], window, preferred_element_type=F32))
        own = self.joined[y + 2, OWN, :].astype(F32)
        return (own + self.flags[3].astype(F32) * total).astype(BF16)


def stack_rows(target, turned, pieces):
    for p in range(4):
        target[pl.ds(turn(turned, 8 * p, 24), 8)] = pieces[p][...]


def level_kernel(sources, level, flags, cols, table, wu, wm, *refs):
    flags = flags.at[level]
    own_outer, own_edge, own_inner, own_near = refs[4 * sources : 4 * sources + 4]
    outs = refs[4 * sources + 4 : 4 * sources + 8]
    src, joined, act = refs[4 * sources + 8 : 4 * sources + 11]
    passed = refs[4 * sources + 11 :]
    turned = flags[0]
    for i in range(sources):
        stack_rows(src.at[i], turned, refs[4 * i : 4 * i + 4])
    joined[pl.ds(turn(turned, 0, 18), 2), OWN] = own_outer[0:2]
    joined[pl.ds(turn(turned, 2, 12), 8), OWN] = own_edge[...]
    joined[pl.ds(turn(turned, 10, 12), 8), OWN] = own_inner[...]
    joined[pl.ds(turn(turned, 18, 18), 2), OWN] = own_near[0:2]

    def source_of(which, first, count):
        return src[which ^ flags[4] if sources == 2 else 0, first : first + count]

    def put_of(which):
        def put(row, c, value):
            joined[row, pl.ds(pl.multiple_of(which * CH + c, 16), 16), :] = value

        return put

    warp_into(flags, cols, table, source_of, passed, put_of)
    conv = Convolutions(flags, wu, wm, joined, act)

    @pl.loop(0, 3)
    def _(n):
        for k in range(6):
            conv.activate(6 * n + k)

    out_edge, out_inner, out_rim, out_near = outs

    @pl.loop(0, 2)
    def _(n):
        for k in range(4):
            y = 4 * n + k
            out_edge[y] = conv.finish(y + turn(turned, 0, 8))
            out_inner[y] = conv.finish(y + turn(turned, 8, 8))

    out_rim[...] = out_edge[pl.ds(turn(turned, 0, 6), 2)]
    out_near[...] = out_inner[pl.ds(turn(turned, 6, 6), 2)]


def warp_half_kernel(is_outer, flags, cols, table, *refs):
    flags = flags.at[0]
    pieces, (ahead, back, src, both, main_rows, halo_rows) = refs[:3], refs[3:]
    turned = flags[0]
    part = turned if is_outer else 1 - turned
    for p in range(3):
        place = p if is_outer else p + 1
        src[pl.ds(turn(turned, 8 * place, 24), 8)] = pieces[p][...]
    keep = (jnp.where(part == 1, flags[2], flags[1]) > 0).astype(F32)

    @pl.loop(0, 2)
    def _(which):
        def put_from(start):
            def put(i, c, value):
                both[which, start + i, c : c + 16, :] = value

            return put

        main, halo = which * 4 + 1 + part, which * 4 + 3 * part
        column_pass(main_rows, src[pl.ds(3 + 8 * part, 19)], cols[main])
        column_pass(halo_rows, src[pl.ds(1 + 18 * part, 13)], cols[halo])
        row_pass(main_rows, entry_at(table, main), 1.0, 8, put_from(2 - 2 * part))
        row_pass(halo_rows, entry_at(table, halo), keep, 2, put_from(8 * part))

    ahead[...] = both[0]
    back[...] = both[1]


def last_inner_kernel(
    flags, wu, wm, inner, near, earlier, later, out_act, out_rows, joined, act
):
    flags = flags.at[0]
    turned = flags[0]
    part = 1 - turned
    joined[pl.ds(turn(turned, 10, 12), 8), OWN] = inner[...]
    joined[pl.ds(turn(turned, 18, 18), 2), OWN] = near[pl.ds(turn(turned, 0, 6), 2)]
    joined[pl.ds(10 * part, 10), 0:CH] = earlier[...]
    joined[pl.ds(10 * part, 10), CH : 2 * CH] = later[...]
    conv = Convolutions(flags, wu, wm, joined, act)

    @pl.loop(0, 2)
    def _(n):
        for k in range(4):
            conv.activate(10 * part + 4 * n + k)

    for k in range(6):
        out_rows[k] = conv.finish(10 * part + k)
    out_act[...] = act[pl.ds(10 * part, 8)]


def last_outer_kernel(
    flags,
    wu,
    wm,
    outer,
    edge,
    inner,
    near,
    inner_earlier,
    inner_later,
    inner_act,
    inner_rows,
    earlier,
    later,
    out,
    joined,
    act,
):
    flags = flags.at[0]
    turned = flags[0]
    part = turned
    joined[pl.ds(turn(turned, 0, 18), 2), OWN] = outer[pl.ds(turn(turned, 6, 6), 2)]
    joined[pl.ds(turn(turned, 2, 12), 8), OWN] = edge[...]
    joined[pl.ds(turn(turned, 10, 12), 8), OWN] = inner[...]
    joined[pl.ds(turn(turned, 18, 18), 2), OWN] = near[pl.ds(turn(turned, 0, 6), 2)]
    joined[pl.ds(10 * part, 10), 0:CH] = earlier[...]
    joined[pl.ds(10 * part, 10), CH : 2 * CH] = later[...]
    joined[pl.ds(10 - 10 * part, 10), 0:CH] = inner_earlier[...]
    joined[pl.ds(10 - 10 * part, 10), CH : 2 * CH] = inner_later[...]
    act[pl.ds(10 - 10 * part, 8)] = inner_act[...]
    out[pl.ds(10 - 10 * part, 6)] = inner_rows[...]
    conv = Convolutions(flags, wu, wm, joined, act)

    @pl.loop(0, 2)
    def _(n):
        for k in range(5):
            conv.activate(8 * part + 5 * n + k)

    @pl.loop(0, 2)
    def _(n):
        for k in range(5):
            y = 6 * part + 5 * n + k
            out[y] = conv.finish(y)


def on_core(kernel, out_shape, scratch, cost, operands, interpret):
    vmem = pl.BlockSpec(memory_space=pltpu.VMEM)
    return pl.pallas_call(
        kernel,
        out_shape=out_shape,
        in_specs=[pl.BlockSpec(memory_space=pltpu.SMEM)] + [vmem] * (len(operands) - 1),
        out_specs=(vmem,) * len(out_shape),
        scratch_shapes=scratch,
        compiler_params=pltpu.CompilerParams(vmem_limit_bytes=VMEM_LIMIT),
        cost_estimate=pl.CostEstimate(
            flops=cost, bytes_accessed=4_000_000, transcendentals=300_000
        ),
        interpret=interpret,
    )(*operands)


def passed_buffers():
    return [pltpu.VMEM((count, CH, WIDTH), F32) for _, _, count, _, _ in BLOCKS]


def band_buffers():
    return [pltpu.VMEM((20, 3 * CH, WIDTH), BF16), pltpu.VMEM((18, CH, WIDTH), BF16)]


def run_level(level, flags, cols, table, wu, wm, sources, own, interpret=False):
    half = jax.ShapeDtypeStruct((HALF, CH, WIDTH), BF16)
    edge = jax.ShapeDtypeStruct((2, CH, WIDTH), BF16)
    operands = [flags, cols, table, wu, wm] + [p for s in sources for p in s] + list(own)
    scratch = [pltpu.VMEM((len(sources), 32, CH, WIDTH), BF16)]
    return on_core(
        functools.partial(level_kernel, len(sources), level),
        (half, half, edge, edge),
        scratch + band_buffers() + passed_buffers(),
        3_000_000_000,
        operands,
        interpret,
    )


def run_warp_half(is_outer, flags, cols, table, pieces, interpret=False):
    return on_core(
        functools.partial(warp_half_kernel, is_outer),
        (jax.ShapeDtypeStruct((10, CH, WIDTH), BF16),) * 2,
        [
            pltpu.VMEM((32, CH, WIDTH), BF16),
            pltpu.VMEM((2, 10, CH, WIDTH), BF16),
            pltpu.VMEM((19, CH, WIDTH), F32),
            pltpu.VMEM((13, CH, WIDTH), F32),
        ],
        800_000_000,
        [flags, cols, table, *pieces],
        interpret,
    )


def run_last_inner(flags, wu, wm, operands, interpret=False):
    return on_core(
        last_inner_kernel,
        (
            jax.ShapeDtypeStruct((8, CH, WIDTH), BF16),
            jax.ShapeDtypeStruct((6, CH, WIDTH), BF16),
        ),
        band_buffers(),
        600_000_000,
        [flags, wu, wm, *operands],
        interpret,
    )


def run_last_outer(flags, wu, wm, operands, interpret=False):
    return on_core(
        last_outer_kernel,
        (jax.ShapeDtypeStruct((2 * HALF, CH, WIDTH), BF16),),
        band_buffers(),
        900_000_000,
        [flags, wu, wm, *operands],
        interpret,
    )[0]


def send(x, frame_to=lambda t: t, row_to=lambda r: r):
    frames, rows = lax.axis_size("tm"), lax.axis_size("rows")
    route = [
        (t * rows + r, (frame_to(t) % frames) * rows + row_to(r))
        for t in range(frames)
        for r in range(rows)
        if 0 <= row_to(r) < rows
    ]
    return lax.ppermute(x, ("tm", "rows"), route)


def off_chip(r):
    return r + 1 if r % 2 else r - 1


def on_chip(r):
    return r ^ 1


def level_values(t):
    t = t.reshape(2, 2, 2, 4, 32)
    t = jnp.transpose(t, (1, 3, 0, 2, 4)).reshape(2, 4, 4, 32)
    return jnp.pad(t, ((0, 0), (0, 0), (0, 4), (0, 0))).reshape(64, 32)


def tap_weights(w):
    o, j = w.shape[2], w.shape[3]
    return jnp.transpose(w, (1, 2, 0, 3)).reshape(3 * o, 3 * j)


def with_table(rows, entries):
    plane = jnp.pad(entries.reshape(3, WIDTH), ((0, CH - 3), (0, 0)))
    return jnp.concatenate([rows, plane[None]])


def table_of(payload):
    return payload[2, 0:3].reshape(2, LEVELS, 4, 1, 32)


def shards(features, block_shift, quarter_pel, update_mask, uniting_weight, mixing_weight):
    band = features[0]
    row = lax.axis_index("rows")
    rows = lax.axis_size("rows")
    turned = row % 2
    edge = lax.dynamic_slice_in_dim(band, 8 * turned, HALF, axis=0)
    inner = lax.dynamic_slice_in_dim(band, 8 - 8 * turned, HALF, axis=0)
    rim = lax.dynamic_slice_in_dim(band, 14 * turned, 2, axis=0)
    near = lax.dynamic_slice_in_dim(band, 14 - 14 * turned, 2, axis=0)
    wu, wm = tap_weights(uniting_weight), tap_weights(mixing_weight)
    common = [turned, (row > 0).astype(jnp.int32), (row < rows - 1).astype(jnp.int32)]
    swapped = (lax.axis_index("tm") % 4 < 2).astype(jnp.int32)
    flags = jnp.stack(
        [value for k in range(LEVELS) for value in common + [update_mask[k, 0], swapped]]
    ).reshape(LEVELS, 5)

    def to_other(t):
        return t + 4

    def across(t):
        return t + 2 if t % 4 < 2 else t - 2

    def ahead(t):
        return t + 1

    def back(t):
        return t - 1

    own = jnp.stack([block_shift[:, :, 0], quarter_pel[:, :, 0]]).astype(BF16)
    at_edge = jnp.where(turned == 1, own[:, :, :, 1], own[:, :, :, 0])
    at_near = jnp.where(turned == 1, own[:, :, :, 0], own[:, :, :, 1])

    e = send(edge, to_other)
    h = send(edge, to_other, off_chip)
    i = send(inner, to_other)
    own_outer = send(with_table(rim, at_edge), row_to=off_chip)
    own_near = send(with_table(near, at_near), row_to=on_chip)
    n = send(i, row_to=on_chip)
    outer_table, near_table = table_of(own_outer), table_of(own_near)
    packed = jnp.concatenate(
        [
            jnp.where(turned == 1, near_table, outer_table),
            own,
            jnp.where(turned == 1, outer_table, near_table),
        ],
        axis=3,
    )
    values, later_values, ahead_entries, back_entries, wu, wm, flags = (
        lax.optimization_barrier(
            (
                level_values(packed[:, 2]),
                level_values(packed[:, 1]),
                packed[:, 0, 0:2],
                packed[:, 0, 2:4],
                wu,
                wm,
                flags,
            )
        )
    )
    cols, table = make_columns(values)
    edge, inner, rim, near = run_level(
        2, flags, cols, table, wu, wm, [(h, e, i, n)], (own_outer, edge, inner, own_near)
    )

    own_outer = send(rim, row_to=off_chip)
    own_near = send(near, row_to=on_chip)
    e = send(edge, across)
    i = send(inner, across)
    xe = send(e, to_other)
    xh = send(e, to_other, off_chip)
    h = send(xe, to_other, off_chip)
    xi = send(i, to_other)
    n = send(i, row_to=on_chip)
    for_ahead = send(ahead_entries, back)
    for_back = send(back_entries, ahead)
    xn = send(xi, row_to=on_chip)
    cols, table = make_columns(later_values)
    edge, inner, _, _ = run_level(
        1,
        flags,
        cols,
        table,
        wu,
        wm,
        [(h, e, i, n), (xh, xe, xi, xn)],
        (own_outer, edge, inner, own_near),
    )

    outer = send(edge, row_to=off_chip)
    near = send(inner, row_to=on_chip)
    cols, table = make_columns(
        level_values(jnp.concatenate([for_ahead, for_back], axis=1))
    )
    halves = run_warp_half(False, flags, cols, table, (edge, inner, near))
    inner_earlier = send(halves[0], ahead)
    inner_later = send(halves[1], back)
    halves = run_warp_half(True, flags, cols, table, (outer, edge, inner))
    earlier = send(halves[0], ahead)
    later = send(halves[1], back)
    inner_act, inner_rows = run_last_inner(
        flags, wu, wm, (inner, near, inner_earlier, inner_later)
    )
    refined = run_last_outer(
        flags,
        wu,
        wm,
        (
            outer,
            edge,
            inner,
            near,
            inner_earlier,
            inner_later,
            inner_act,
            inner_rows,
            earlier,
            later,
        ),
    )
    return refined[None]


def solution(mesh):
    placed = (
        P("tm", "rows", None, None),
        P(None, None, "tm", "rows", None),
        P(None, None, "tm", "rows", None),
        P(None, "tm"),
        P(),
        P(),
    )
    return jax.shard_map(
        shards, mesh=mesh, in_specs=placed, out_specs=P("tm", "rows", None, None), check_vma=False
    )
```

```python
import functools

import jax
import jax.numpy as jnp
from jax import lax
from jax.experimental import pallas as pl
from jax.experimental.pallas import tpu as pltpu
from jax.sharding import PartitionSpec as P


LEVELS = 3
CH = 64
WIDTH = 256
HALF = 8
VMEM_LIMIT = 16 << 20
F32 = jnp.float32
BF16 = jnp.bfloat16


def pick_rows(v, bits, w0, w1, outs):
    b8, b4, b2, b1 = bits
    n8, n4, n2, n1 = outs + 8, outs + 4, outs + 2, outs + 1
    x8 = [jnp.where(b8, v[j + 8], v[j]) if j < outs + 3 else v[j] for j in range(n8)]
    x4 = [jnp.where(b4, x8[j + 4], x8[j]) for j in range(n4)]
    x2 = [jnp.where(b2, x4[j + 2], x4[j]) for j in range(n2)]
    x1 = [jnp.where(b1, x2[j + 1], x2[j]) for j in range(n1)]
    return [w0 * x1[i] + w1 * x1[i + 1] for i in range(outs)]


BLOCKS = ((1, 3, 19, 8, 2), (2, 11, 19, 8, 10), (0, 1, 13, 2, 0), (3, 19, 13, 2, 18))
OWN = slice(2 * CH, 3 * CH)


def turn(turned, place, size):
    return place + turned * (size - 2 * place)


def columns_kernel(first, second, cols, table, vals):
    vals[...] = jnp.zeros_like(vals)
    for ref, entries in enumerate((first, second)):
        for k in range(4):
            rows = entries[k // 2, k % 2].astype(F32)
            for block in range(4):
                at = (ref * 4 + block) * 8 + k
                vals[at : at + 1, :] = rows[block : block + 1]
    block_of = lax.broadcasted_iota(jnp.int32, (32, WIDTH), 1) // 8
    spread = (block_of == lax.broadcasted_iota(jnp.int32, (32, WIDTH), 0)).astype(F32)
    table[...] = jnp.dot(
        vals[...].astype(BF16), spread.astype(BF16), preferred_element_type=F32
    )
    apart = lax.broadcasted_iota(jnp.int32, (WIDTH, WIDTH), 0) - lax.broadcasted_iota(
        jnp.int32, (WIDTH, WIDTH), 1
    )

    @pl.loop(0, cols.shape[0])
    def _(n):
        entry = table[pl.ds(pl.multiple_of(n * 8, 8), 8), :]
        off = apart - entry[1:2].astype(jnp.int32)
        fx = entry[3:4] * 0.25
        cols[n] = jnp.where(off == 0, 1.0 - fx, jnp.where(off == 1, fx, 0.0)).astype(BF16)


def make_columns(first, second, interpret=False):
    vmem = pl.BlockSpec(memory_space=pltpu.VMEM)
    return pl.pallas_call(
        columns_kernel,
        out_shape=(
            jax.ShapeDtypeStruct((8, WIDTH, WIDTH), BF16),
            jax.ShapeDtypeStruct((64, WIDTH), F32),
        ),
        in_specs=[vmem, vmem],
        out_specs=(vmem, vmem),
        scratch_shapes=[pltpu.VMEM((64, 32), F32)],
        compiler_params=pltpu.CompilerParams(vmem_limit_bytes=VMEM_LIMIT),
        cost_estimate=pl.CostEstimate(
            flops=100_000_000, bytes_accessed=3_000_000, transcendentals=0
        ),
        interpret=interpret,
    )(first, second)


def column_pass(buffer, window, matrix):
    count = window.shape[0]
    buffer[...] = jnp.dot(
        window.reshape(count * CH, WIDTH), matrix, preferred_element_type=F32
    ).reshape(count, CH, WIDTH)


def row_pass(buffer, entry, keep, outs, put):
    lanes = (16, WIDTH)
    s = entry[0:1].astype(jnp.int32) + 5
    bits = [jnp.broadcast_to((s & b) != 0, lanes) for b in (8, 4, 2, 1)]
    fy = entry[2:3] * 0.25
    w1 = jnp.broadcast_to(fy * keep, lanes)
    w0 = jnp.broadcast_to((1.0 - fy) * keep, lanes)
    for c in range(CH // 16):
        v = [buffer[u, 16 * c : 16 * c + 16, :] for u in range(buffer.shape[0])]
        for i, row in enumerate(pick_rows(v, bits, w0, w1, outs)):
            put(i, 16 * c, row.astype(BF16))


def entry_at(table, n):
    return table[pl.ds(pl.multiple_of(n * 8, 8), 8), :]


def warp_into(flags, cols, table, source_of, passed, put_of):
    has_above = (flags[1] > 0).astype(F32)
    has_below = (flags[2] > 0).astype(F32)

    @pl.loop(0, 2)
    def _(which):
        put = put_of(which)

        def columns(k):
            block, first, count, _, _ = BLOCKS[k]
            column_pass(passed[k], source_of(which, first, count), cols[which * 4 + block])

        def rows(k):
            block, _, _, outs, start = BLOCKS[k]
            keep = {0: has_above, 3: has_below}.get(block, 1.0)
            row_pass(
                passed[k],
                entry_at(table, which * 4 + block),
                keep,
                outs,
                lambda i, c, value: put(start + i, c, value),
            )

        columns(0)
        for k in range(4):
            if k < 3:
                columns(k + 1)
            rows(k)


class Convolutions:
    def __init__(self, flags, wu, wm, joined, act):
        self.flags, self.wu, self.wm, self.joined, self.act = flags, wu, wm, joined, act
        lane = lax.broadcasted_iota(jnp.int32, (CH, WIDTH), 1)
        self.not_first = lane > 0
        self.not_last = lane < WIDTH - 1

    def gather_taps(self, s):
        left = jnp.where(self.not_first, pltpu.roll(s[0:CH], 1, 1), 0.0)
        right = jnp.where(self.not_last, pltpu.roll(s[2 * CH :], WIDTH - 1, 1), 0.0)
        return s[CH : 2 * CH] + left + right

    def activate(self, a):
        window = self.joined[pl.ds(a, 3)].reshape(9 * CH, WIDTH)
        total = self.gather_taps(jnp.dot(self.wu[...], window, preferred_element_type=F32))
        half = 0.5 * total
        value = half + half * jnp.tanh(half)
        inside = jnp.where(
            a == 0, self.flags[1] > 0, jnp.where(a == 17, self.flags[2] > 0, True)
        )
        self.act[a] = (value * inside.astype(F32)).astype(BF16)

    def finish(self, y):
        window = self.act[pl.ds(y, 3)].reshape(3 * CH, WIDTH)
        total = self.gather_taps(jnp.dot(self.wm[...], window, preferred_element_type=F32))
        own = self.joined[y + 2, OWN, :].astype(F32)
        return (own + self.flags[3].astype(F32) * total).astype(BF16)


def stack_rows(target, turned, pieces):
    for p in range(4):
        target[pl.ds(turn(turned, 8 * p, 24), 8)] = pieces[p][...]


def level_kernel(sources, level, flags, cols, table, wu, wm, *refs):
    flags = flags.at[level]
    own_outer, own_edge, own_inner, own_near = refs[4 * sources : 4 * sources + 4]
    outs = refs[4 * sources + 4 : 4 * sources + 8]
    src, joined, act = refs[4 * sources + 8 : 4 * sources + 11]
    passed = refs[4 * sources + 11 :]
    turned = flags[0]
    for i in range(sources):
        stack_rows(src.at[i], turned, refs[4 * i : 4 * i + 4])
    joined[pl.ds(turn(turned, 0, 18), 2), OWN] = own_outer[0:2]
    joined[pl.ds(turn(turned, 2, 12), 8), OWN] = own_edge[...]
    joined[pl.ds(turn(turned, 10, 12), 8), OWN] = own_inner[...]
    joined[pl.ds(turn(turned, 18, 18), 2), OWN] = own_near[0:2]

    def source_of(which, first, count):
        return src[which ^ flags[4] if sources == 2 else 0, first : first + count]

    def put_of(which):
        def put(row, c, value):
            joined[row, pl.ds(pl.multiple_of(which * CH + c, 16), 16), :] = value

        return put

    warp_into(flags, cols, table, source_of, passed, put_of)
    conv = Convolutions(flags, wu, wm, joined, act)

    @pl.loop(0, 3)
    def _(n):
        for k in range(6):
            conv.activate(6 * n + k)

    out_edge, out_inner, out_rim, out_near = outs

    @pl.loop(0, 2)
    def _(n):
        for k in range(4):
            y = 4 * n + k
            out_edge[y] = conv.finish(y + turn(turned, 0, 8))
            out_inner[y] = conv.finish(y + turn(turned, 8, 8))

    out_rim[...] = out_edge[pl.ds(turn(turned, 0, 6), 2)]
    out_near[...] = out_inner[pl.ds(turn(turned, 6, 6), 2)]


def warp_half_kernel(is_outer, flags, cols, table, *refs):
    flags = flags.at[0]
    pieces, (ahead, back, src, both, main_rows, halo_rows) = refs[:3], refs[3:]
    turned = flags[0]
    part = turned if is_outer else 1 - turned
    for p in range(3):
        place = p if is_outer else p + 1
        src[pl.ds(turn(turned, 8 * place, 24), 8)] = pieces[p][...]
    keep = (jnp.where(part == 1, flags[2], flags[1]) > 0).astype(F32)

    @pl.loop(0, 2)
    def _(which):
        def put_from(start):
            def put(i, c, value):
                both[which, start + i, c : c + 16, :] = value

            return put

        main, halo = which * 4 + 1 + part, which * 4 + 3 * part
        column_pass(main_rows, src[pl.ds(3 + 8 * part, 19)], cols[main])
        column_pass(halo_rows, src[pl.ds(1 + 18 * part, 13)], cols[halo])
        row_pass(main_rows, entry_at(table, main), 1.0, 8, put_from(2 - 2 * part))
        row_pass(halo_rows, entry_at(table, halo), keep, 2, put_from(8 * part))

    ahead[...] = both[0]
    back[...] = both[1]


def last_inner_kernel(
    flags, wu, wm, inner, near, earlier, later, out_act, out_rows, joined, act
):
    flags = flags.at[0]
    turned = flags[0]
    part = 1 - turned
    joined[pl.ds(turn(turned, 10, 12), 8), OWN] = inner[...]
    joined[pl.ds(turn(turned, 18, 18), 2), OWN] = near[pl.ds(turn(turned, 0, 6), 2)]
    joined[pl.ds(10 * part, 10), 0:CH] = earlier[...]
    joined[pl.ds(10 * part, 10), CH : 2 * CH] = later[...]
    conv = Convolutions(flags, wu, wm, joined, act)

    @pl.loop(0, 2)
    def _(n):
        for k in range(4):
            conv.activate(10 * part + 4 * n + k)

    for k in range(6):
        out_rows[k] = conv.finish(10 * part + k)
    out_act[...] = act[pl.ds(10 * part, 8)]


def last_outer_kernel(
    flags,
    wu,
    wm,
    outer,
    edge,
    inner,
    near,
    inner_earlier,
    inner_later,
    inner_act,
    inner_rows,
    earlier,
    later,
    out,
    joined,
    act,
):
    flags = flags.at[0]
    turned = flags[0]
    part = turned
    joined[pl.ds(turn(turned, 0, 18), 2), OWN] = outer[pl.ds(turn(turned, 6, 6), 2)]
    joined[pl.ds(turn(turned, 2, 12), 8), OWN] = edge[...]
    joined[pl.ds(turn(turned, 10, 12), 8), OWN] = inner[...]
    joined[pl.ds(turn(turned, 18, 18), 2), OWN] = near[pl.ds(turn(turned, 0, 6), 2)]
    joined[pl.ds(10 * part, 10), 0:CH] = earlier[...]
    joined[pl.ds(10 * part, 10), CH : 2 * CH] = later[...]
    joined[pl.ds(10 - 10 * part, 10), 0:CH] = inner_earlier[...]
    joined[pl.ds(10 - 10 * part, 10), CH : 2 * CH] = inner_later[...]
    act[pl.ds(10 - 10 * part, 8)] = inner_act[...]
    out[pl.ds(10 - 10 * part, 6)] = inner_rows[...]
    conv = Convolutions(flags, wu, wm, joined, act)

    @pl.loop(0, 2)
    def _(n):
        for k in range(5):
            conv.activate(8 * part + 5 * n + k)

    @pl.loop(0, 2)
    def _(n):
        for k in range(5):
            y = 6 * part + 5 * n + k
            out[y] = conv.finish(y)


def on_core(kernel, out_shape, scratch, cost, operands, interpret):
    vmem = pl.BlockSpec(memory_space=pltpu.VMEM)
    return pl.pallas_call(
        kernel,
        out_shape=out_shape,
        in_specs=[pl.BlockSpec(memory_space=pltpu.SMEM)] + [vmem] * (len(operands) - 1),
        out_specs=(vmem,) * len(out_shape),
        scratch_shapes=scratch,
        compiler_params=pltpu.CompilerParams(vmem_limit_bytes=VMEM_LIMIT),
        cost_estimate=pl.CostEstimate(
            flops=cost, bytes_accessed=4_000_000, transcendentals=300_000
        ),
        interpret=interpret,
    )(*operands)


def passed_buffers():
    return [pltpu.VMEM((count, CH, WIDTH), F32) for _, _, count, _, _ in BLOCKS]


def band_buffers():
    return [pltpu.VMEM((20, 3 * CH, WIDTH), BF16), pltpu.VMEM((18, CH, WIDTH), BF16)]


def run_level(level, flags, cols, table, wu, wm, sources, own, interpret=False):
    half = jax.ShapeDtypeStruct((HALF, CH, WIDTH), BF16)
    edge = jax.ShapeDtypeStruct((2, CH, WIDTH), BF16)
    operands = [flags, cols, table, wu, wm] + [p for s in sources for p in s] + list(own)
    scratch = [pltpu.VMEM((len(sources), 32, CH, WIDTH), BF16)]
    return on_core(
        functools.partial(level_kernel, len(sources), level),
        (half, half, edge, edge),
        scratch + band_buffers() + passed_buffers(),
        3_000_000_000,
        operands,
        interpret,
    )


def run_warp_half(is_outer, flags, cols, table, pieces, interpret=False):
    return on_core(
        functools.partial(warp_half_kernel, is_outer),
        (jax.ShapeDtypeStruct((10, CH, WIDTH), BF16),) * 2,
        [
            pltpu.VMEM((32, CH, WIDTH), BF16),
            pltpu.VMEM((2, 10, CH, WIDTH), BF16),
            pltpu.VMEM((19, CH, WIDTH), F32),
            pltpu.VMEM((13, CH, WIDTH), F32),
        ],
        800_000_000,
        [flags, cols, table, *pieces],
        interpret,
    )


def run_last_inner(flags, wu, wm, operands, interpret=False):
    return on_core(
        last_inner_kernel,
        (
            jax.ShapeDtypeStruct((8, CH, WIDTH), BF16),
            jax.ShapeDtypeStruct((6, CH, WIDTH), BF16),
        ),
        band_buffers(),
        600_000_000,
        [flags, wu, wm, *operands],
        interpret,
    )


def run_last_outer(flags, wu, wm, operands, interpret=False):
    return on_core(
        last_outer_kernel,
        (jax.ShapeDtypeStruct((2 * HALF, CH, WIDTH), BF16),),
        band_buffers(),
        900_000_000,
        [flags, wu, wm, *operands],
        interpret,
    )[0]


def send(x, frame_to=lambda t: t, row_to=lambda r: r):
    frames, rows = lax.axis_size("tm"), lax.axis_size("rows")
    route = [
        (t * rows + r, (frame_to(t) % frames) * rows + row_to(r))
        for t in range(frames)
        for r in range(rows)
        if 0 <= row_to(r) < rows
    ]
    return lax.ppermute(x, ("tm", "rows"), route)


def off_chip(r):
    return r + 1 if r % 2 else r - 1


def on_chip(r):
    return r ^ 1


def tap_weights(w):
    o, j = w.shape[2], w.shape[3]
    return jnp.transpose(w, (1, 2, 0, 3)).reshape(3 * o, 3 * j)


def with_table(rows, entries):
    plane = jnp.pad(entries.reshape(3, WIDTH), ((0, CH - 3), (0, 0)))
    return jnp.concatenate([rows, plane[None]])


def table_of(payload):
    return payload[2, 0:3].reshape(2, LEVELS, 4, 1, 32)


def shards(features, block_shift, quarter_pel, update_mask, uniting_weight, mixing_weight):
    band = features[0]
    row = lax.axis_index("rows")
    rows = lax.axis_size("rows")
    turned = row % 2
    edge = lax.dynamic_slice_in_dim(band, 8 * turned, HALF, axis=0)
    inner = lax.dynamic_slice_in_dim(band, 8 - 8 * turned, HALF, axis=0)
    rim = lax.dynamic_slice_in_dim(band, 14 * turned, 2, axis=0)
    near = lax.dynamic_slice_in_dim(band, 14 - 14 * turned, 2, axis=0)
    wu, wm = tap_weights(uniting_weight), tap_weights(mixing_weight)
    common = [turned, (row > 0).astype(jnp.int32), (row < rows - 1).astype(jnp.int32)]
    swapped = (lax.axis_index("tm") % 4 < 2).astype(jnp.int32)
    flags = jnp.stack(
        [value for k in range(LEVELS) for value in common + [update_mask[k, 0], swapped]]
    ).reshape(LEVELS, 5)

    def to_other(t):
        return t + 4

    def across(t):
        return t + 2 if t % 4 < 2 else t - 2

    def ahead(t):
        return t + 1

    def back(t):
        return t - 1

    own = jnp.stack([block_shift[:, :, 0], quarter_pel[:, :, 0]]).astype(BF16)
    at_edge = jnp.where(turned == 1, own[:, :, :, 1], own[:, :, :, 0])
    at_near = jnp.where(turned == 1, own[:, :, :, 0], own[:, :, :, 1])

    e = send(edge, to_other)
    h = send(edge, to_other, off_chip)
    i = send(inner, to_other)
    own_outer = send(with_table(rim, at_edge), row_to=off_chip)
    own_near = send(with_table(near, at_near), row_to=on_chip)
    n = send(i, row_to=on_chip)
    outer_table, near_table = table_of(own_outer), table_of(own_near)
    packed = jnp.concatenate(
        [
            jnp.where(turned == 1, near_table, outer_table),
            own,
            jnp.where(turned == 1, outer_table, near_table),
        ],
        axis=3,
    )
    *entries, wu, wm, flags = lax.optimization_barrier(
        tuple(packed[:, k, j : j + 2] for k in (2, 1, 0) for j in (0, 2))
        + (wu, wm, flags)
    )
    cols, table = make_columns(entries[0], entries[1])
    edge, inner, rim, near = run_level(
        2, flags, cols, table, wu, wm, [(h, e, i, n)], (own_outer, edge, inner, own_near)
    )

    own_outer = send(rim, row_to=off_chip)
    own_near = send(near, row_to=on_chip)
    e = send(edge, across)
    i = send(inner, across)
    xe = send(e, to_other)
    xh = send(e, to_other, off_chip)
    h = send(xe, to_other, off_chip)
    xi = send(i, to_other)
    n = send(i, row_to=on_chip)
    for_ahead = send(entries[4], back)
    for_back = send(entries[5], ahead)
    xn = send(xi, row_to=on_chip)
    cols, table = make_columns(entries[2], entries[3])
    next_cols, next_table = make_columns(for_ahead, for_back)
    edge, inner, _, _ = run_level(
        1,
        flags,
        cols,
        table,
        wu,
        wm,
        [(h, e, i, n), (xh, xe, xi, xn)],
        (own_outer, edge, inner, own_near),
    )

    outer = send(edge, row_to=off_chip)
    near = send(inner, row_to=on_chip)
    halves = run_warp_half(False, flags, next_cols, next_table, (edge, inner, near))
    inner_earlier = send(halves[0], ahead)
    inner_later = send(halves[1], back)
    halves = run_warp_half(True, flags, next_cols, next_table, (outer, edge, inner))
    earlier = send(halves[0], ahead)
    later = send(halves[1], back)
    inner_act, inner_rows = run_last_inner(flags, wu, wm, (inner, near, inner_earlier, inner_later))
    refined = run_last_outer(
        flags,
        wu,
        wm,
        (
            outer,
            edge,
            inner,
            near,
            inner_earlier,
            inner_later,
            inner_act,
            inner_rows,
            earlier,
            later,
        ),
    )
    return refined[None]


def solution(mesh):
    placed = (
        P("tm", "rows", None, None),
        P(None, None, "tm", "rows", None),
        P(None, None, "tm", "rows", None),
        P(None, "tm"),
        P(),
        P(),
    )
    return jax.shard_map(
        shards, mesh=mesh, in_specs=placed, out_specs=P("tm", "rows", None, None), check_vma=False
    )
```

```python
import functools

import jax
import jax.numpy as jnp
from jax import lax
from jax.experimental import pallas as pl
from jax.experimental.pallas import tpu as pltpu
from jax.sharding import PartitionSpec as P


LEVELS = 3
CH = 64
WIDTH = 256
HALF = 8
VMEM_LIMIT = 16 << 20
F32 = jnp.float32
BF16 = jnp.bfloat16


def pick_rows(v, bits, w0, w1, outs):
    b8, b4, b2, b1 = bits
    n8, n4, n2, n1 = outs + 8, outs + 4, outs + 2, outs + 1
    x8 = [jnp.where(b8, v[j + 8], v[j]) if j < outs + 3 else v[j] for j in range(n8)]
    x4 = [jnp.where(b4, x8[j + 4], x8[j]) for j in range(n4)]
    x2 = [jnp.where(b2, x4[j + 2], x4[j]) for j in range(n2)]
    x1 = [jnp.where(b1, x2[j + 1], x2[j]) for j in range(n1)]
    return [w0 * x1[i] + w1 * x1[i + 1] for i in range(outs)]


BLOCKS = ((1, 3, 19, 8, 2), (2, 11, 19, 8, 10), (0, 1, 13, 2, 0), (3, 19, 13, 2, 18))
OWN = slice(2 * CH, 3 * CH)


def turn(turned, place, size):
    return place + turned * (size - 2 * place)


def columns_kernel(first, second, cols, table, vals):
    vals[...] = jnp.zeros_like(vals)
    for ref, entries in enumerate((first, second)):
        for k in range(4):
            rows = entries[k // 2, k % 2].astype(F32)
            for block in range(4):
                at = (ref * 4 + block) * 8 + k
                vals[at : at + 1, :] = rows[block : block + 1]
    block_of = lax.broadcasted_iota(jnp.int32, (32, WIDTH), 1) // 8
    spread = (block_of == lax.broadcasted_iota(jnp.int32, (32, WIDTH), 0)).astype(F32)
    table[...] = jnp.dot(
        vals[...].astype(BF16), spread.astype(BF16), preferred_element_type=F32
    )
    apart = lax.broadcasted_iota(jnp.int32, (WIDTH, WIDTH), 0) - lax.broadcasted_iota(
        jnp.int32, (WIDTH, WIDTH), 1
    )

    @pl.loop(0, cols.shape[0])
    def _(n):
        entry = table[pl.ds(pl.multiple_of(n * 8, 8), 8), :]
        off = apart - entry[1:2].astype(jnp.int32)
        fx = entry[3:4] * 0.25
        cols[n] = jnp.where(off == 0, 1.0 - fx, jnp.where(off == 1, fx, 0.0)).astype(BF16)


def make_columns(first, second, interpret=False):
    vmem = pl.BlockSpec(memory_space=pltpu.VMEM)
    return pl.pallas_call(
        columns_kernel,
        out_shape=(
            jax.ShapeDtypeStruct((8, WIDTH, WIDTH), BF16),
            jax.ShapeDtypeStruct((64, WIDTH), F32),
        ),
        in_specs=[vmem, vmem],
        out_specs=(vmem, vmem),
        scratch_shapes=[pltpu.VMEM((64, 32), F32)],
        compiler_params=pltpu.CompilerParams(vmem_limit_bytes=VMEM_LIMIT),
        cost_estimate=pl.CostEstimate(
            flops=100_000_000, bytes_accessed=3_000_000, transcendentals=0
        ),
        interpret=interpret,
    )(first, second)


def column_pass(buffer, window, matrix):
    count = window.shape[0]
    buffer[...] = jnp.dot(
        window.reshape(count * CH, WIDTH), matrix, preferred_element_type=F32
    ).reshape(count, CH, WIDTH)


def row_pass(buffer, entry, keep, outs, put):
    lanes = (16, WIDTH)
    s = entry[0:1].astype(jnp.int32) + 5
    bits = [jnp.broadcast_to((s & b) != 0, lanes) for b in (8, 4, 2, 1)]
    fy = entry[2:3] * 0.25
    w1 = jnp.broadcast_to(fy * keep, lanes)
    w0 = jnp.broadcast_to((1.0 - fy) * keep, lanes)
    for c in range(CH // 16):
        v = [buffer[u, 16 * c : 16 * c + 16, :] for u in range(buffer.shape[0])]
        for i, row in enumerate(pick_rows(v, bits, w0, w1, outs)):
            put(i, 16 * c, row.astype(BF16))


def entry_at(table, n):
    return table[pl.ds(pl.multiple_of(n * 8, 8), 8), :]


def warp_into(flags, cols, table, source_of, passed, put_of):
    has_above = (flags[1] > 0).astype(F32)
    has_below = (flags[2] > 0).astype(F32)

    @pl.loop(0, 2)
    def _(which):
        put = put_of(which)

        def columns(k):
            block, first, count, _, _ = BLOCKS[k]
            column_pass(passed[k], source_of(which, first, count), cols[which * 4 + block])

        def rows(k):
            block, _, _, outs, start = BLOCKS[k]
            keep = {0: has_above, 3: has_below}.get(block, 1.0)
            row_pass(
                passed[k],
                entry_at(table, which * 4 + block),
                keep,
                outs,
                lambda i, c, value: put(start + i, c, value),
            )

        columns(0)
        for k in range(4):
            if k < 3:
                columns(k + 1)
            rows(k)


class Convolutions:
    def __init__(self, flags, update, wu, wm, joined, act):
        self.flags, self.update, self.wu, self.wm = flags, update, wu, wm
        self.joined, self.act = joined, act
        lane = lax.broadcasted_iota(jnp.int32, (CH, WIDTH), 1)
        self.not_first = lane > 0
        self.not_last = lane < WIDTH - 1

    def gather_taps(self, s):
        left = jnp.where(self.not_first, pltpu.roll(s[0:CH], 1, 1), 0.0)
        right = jnp.where(self.not_last, pltpu.roll(s[2 * CH :], WIDTH - 1, 1), 0.0)
        return s[CH : 2 * CH] + left + right

    def activate(self, a):
        window = self.joined[pl.ds(a, 3)].reshape(9 * CH, WIDTH)
        total = self.gather_taps(jnp.dot(self.wu[...], window, preferred_element_type=F32))
        half = 0.5 * total
        value = half + half * jnp.tanh(half)
        inside = jnp.where(
            a == 0, self.flags[1] > 0, jnp.where(a == 17, self.flags[2] > 0, True)
        )
        self.act[a] = (value * inside.astype(F32)).astype(BF16)

    def finish(self, y):
        window = self.act[pl.ds(y, 3)].reshape(3 * CH, WIDTH)
        total = self.gather_taps(jnp.dot(self.wm[...], window, preferred_element_type=F32))
        own = self.joined[y + 2, OWN, :].astype(F32)
        return (own + self.update.astype(F32) * total).astype(BF16)


def stack_rows(target, turned, pieces):
    for p in range(4):
        target[pl.ds(turn(turned, 8 * p, 24), 8)] = pieces[p][...]


def level_kernel(sources, level, flags, mask, cols, table, wu, wm, *refs):
    own_outer, own_edge, own_inner, own_near = refs[4 * sources : 4 * sources + 4]
    outs = refs[4 * sources + 4 : 4 * sources + 8]
    src, joined, act = refs[4 * sources + 8 : 4 * sources + 11]
    passed = refs[4 * sources + 11 :]
    turned = flags[0]
    for i in range(sources):
        stack_rows(src.at[i], turned, refs[4 * i : 4 * i + 4])
    joined[pl.ds(turn(turned, 0, 18), 2), OWN] = own_outer[0:2]
    joined[pl.ds(turn(turned, 2, 12), 8), OWN] = own_edge[...]
    joined[pl.ds(turn(turned, 10, 12), 8), OWN] = own_inner[...]
    joined[pl.ds(turn(turned, 18, 18), 2), OWN] = own_near[0:2]

    def source_of(which, first, count):
        return src[which ^ flags[3] if sources == 2 else 0, first : first + count]

    def put_of(which):
        def put(row, c, value):
            joined[row, pl.ds(pl.multiple_of(which * CH + c, 16), 16), :] = value

        return put

    warp_into(flags, cols, table, source_of, passed, put_of)
    conv = Convolutions(flags, mask[level, 0], wu, wm, joined, act)

    @pl.loop(0, 3)
    def _(n):
        for k in range(6):
            conv.activate(6 * n + k)

    out_edge, out_inner, out_rim, out_near = outs

    @pl.loop(0, 2)
    def _(n):
        for k in range(4):
            y = 4 * n + k
            out_edge[y] = conv.finish(y + turn(turned, 0, 8))
            out_inner[y] = conv.finish(y + turn(turned, 8, 8))

    out_rim[...] = out_edge[pl.ds(turn(turned, 0, 6), 2)]
    out_near[...] = out_inner[pl.ds(turn(turned, 6, 6), 2)]


def warp_half_kernel(is_outer, flags, mask, cols, table, *refs):
    pieces, (ahead, back, src, both, main_rows, halo_rows) = refs[:3], refs[3:]
    turned = flags[0]
    part = turned if is_outer else 1 - turned
    for p in range(3):
        place = p if is_outer else p + 1
        src[pl.ds(turn(turned, 8 * place, 24), 8)] = pieces[p][...]
    keep = (jnp.where(part == 1, flags[2], flags[1]) > 0).astype(F32)

    @pl.loop(0, 2)
    def _(which):
        def put_from(start):
            def put(i, c, value):
                both[which, start + i, c : c + 16, :] = value

            return put

        main, halo = which * 4 + 1 + part, which * 4 + 3 * part
        column_pass(main_rows, src[pl.ds(3 + 8 * part, 19)], cols[main])
        column_pass(halo_rows, src[pl.ds(1 + 18 * part, 13)], cols[halo])
        row_pass(main_rows, entry_at(table, main), 1.0, 8, put_from(2 - 2 * part))
        row_pass(halo_rows, entry_at(table, halo), keep, 2, put_from(8 * part))

    ahead[...] = both[0]
    back[...] = both[1]


def last_inner_kernel(
    flags, mask, wu, wm, inner, near, earlier, later, out_act, out_rows, joined, act
):
    turned = flags[0]
    part = 1 - turned
    joined[pl.ds(turn(turned, 10, 12), 8), OWN] = inner[...]
    joined[pl.ds(turn(turned, 18, 18), 2), OWN] = near[pl.ds(turn(turned, 0, 6), 2)]
    joined[pl.ds(10 * part, 10), 0:CH] = earlier[...]
    joined[pl.ds(10 * part, 10), CH : 2 * CH] = later[...]
    conv = Convolutions(flags, mask[0, 0], wu, wm, joined, act)

    @pl.loop(0, 2)
    def _(n):
        for k in range(4):
            conv.activate(10 * part + 4 * n + k)

    for k in range(6):
        out_rows[k] = conv.finish(10 * part + k)
    out_act[...] = act[pl.ds(10 * part, 8)]


def last_outer_kernel(
    flags,
    mask,
    wu,
    wm,
    outer,
    edge,
    inner,
    near,
    inner_earlier,
    inner_later,
    inner_act,
    inner_rows,
    earlier,
    later,
    out,
    joined,
    act,
):
    turned = flags[0]
    part = turned
    joined[pl.ds(turn(turned, 0, 18), 2), OWN] = outer[pl.ds(turn(turned, 6, 6), 2)]
    joined[pl.ds(turn(turned, 2, 12), 8), OWN] = edge[...]
    joined[pl.ds(turn(turned, 10, 12), 8), OWN] = inner[...]
    joined[pl.ds(turn(turned, 18, 18), 2), OWN] = near[pl.ds(turn(turned, 0, 6), 2)]
    joined[pl.ds(10 * part, 10), 0:CH] = earlier[...]
    joined[pl.ds(10 * part, 10), CH : 2 * CH] = later[...]
    joined[pl.ds(10 - 10 * part, 10), 0:CH] = inner_earlier[...]
    joined[pl.ds(10 - 10 * part, 10), CH : 2 * CH] = inner_later[...]
    act[pl.ds(10 - 10 * part, 8)] = inner_act[...]
    out[pl.ds(10 - 10 * part, 6)] = inner_rows[...]
    conv = Convolutions(flags, mask[0, 0], wu, wm, joined, act)

    @pl.loop(0, 2)
    def _(n):
        for k in range(5):
            conv.activate(8 * part + 5 * n + k)

    @pl.loop(0, 2)
    def _(n):
        for k in range(5):
            y = 6 * part + 5 * n + k
            out[y] = conv.finish(y)


def on_core(kernel, out_shape, scratch, cost, operands, interpret):
    vmem = pl.BlockSpec(memory_space=pltpu.VMEM)
    return pl.pallas_call(
        kernel,
        out_shape=out_shape,
        in_specs=[pl.BlockSpec(memory_space=pltpu.SMEM)] * 2 + [vmem] * (len(operands) - 2),
        out_specs=(vmem,) * len(out_shape),
        scratch_shapes=scratch,
        compiler_params=pltpu.CompilerParams(vmem_limit_bytes=VMEM_LIMIT),
        cost_estimate=pl.CostEstimate(
            flops=cost, bytes_accessed=4_000_000, transcendentals=300_000
        ),
        interpret=interpret,
    )(*operands)


def passed_buffers():
    return [pltpu.VMEM((count, CH, WIDTH), F32) for _, _, count, _, _ in BLOCKS]


def band_buffers():
    return [pltpu.VMEM((20, 3 * CH, WIDTH), BF16), pltpu.VMEM((18, CH, WIDTH), BF16)]


def run_level(level, flags, cols, table, wu, wm, sources, own, interpret=False):
    half = jax.ShapeDtypeStruct((HALF, CH, WIDTH), BF16)
    edge = jax.ShapeDtypeStruct((2, CH, WIDTH), BF16)
    operands = [*flags, cols, table, wu, wm] + [p for s in sources for p in s] + list(own)
    scratch = [pltpu.VMEM((len(sources), 32, CH, WIDTH), BF16)]
    return on_core(
        functools.partial(level_kernel, len(sources), level),
        (half, half, edge, edge),
        scratch + band_buffers() + passed_buffers(),
        3_000_000_000,
        operands,
        interpret,
    )


def run_warp_half(is_outer, flags, cols, table, pieces, interpret=False):
    return on_core(
        functools.partial(warp_half_kernel, is_outer),
        (jax.ShapeDtypeStruct((10, CH, WIDTH), BF16),) * 2,
        [
            pltpu.VMEM((32, CH, WIDTH), BF16),
            pltpu.VMEM((2, 10, CH, WIDTH), BF16),
            pltpu.VMEM((19, CH, WIDTH), F32),
            pltpu.VMEM((13, CH, WIDTH), F32),
        ],
        800_000_000,
        [*flags, cols, table, *pieces],
        interpret,
    )


def run_last_inner(flags, wu, wm, operands, interpret=False):
    return on_core(
        last_inner_kernel,
        (
            jax.ShapeDtypeStruct((8, CH, WIDTH), BF16),
            jax.ShapeDtypeStruct((6, CH, WIDTH), BF16),
        ),
        band_buffers(),
        600_000_000,
        [*flags, wu, wm, *operands],
        interpret,
    )


def run_last_outer(flags, wu, wm, operands, interpret=False):
    return on_core(
        last_outer_kernel,
        (jax.ShapeDtypeStruct((2 * HALF, CH, WIDTH), BF16),),
        band_buffers(),
        900_000_000,
        [*flags, wu, wm, *operands],
        interpret,
    )[0]


def send(x, frame_to=lambda t: t, row_to=lambda r: r):
    frames, rows = lax.axis_size("tm"), lax.axis_size("rows")
    route = [
        (t * rows + r, (frame_to(t) % frames) * rows + row_to(r))
        for t in range(frames)
        for r in range(rows)
        if 0 <= row_to(r) < rows
    ]
    return lax.ppermute(x, ("tm", "rows"), route)


def off_chip(r):
    return r + 1 if r % 2 else r - 1


def on_chip(r):
    return r ^ 1


def weights_kernel(uniting, mixing, wu, wm):
    for ty in range(3):
        for tx in range(3):
            rows = slice(tx * CH, tx * CH + CH)
            wu[rows, ty * 3 * CH : (ty + 1) * 3 * CH] = uniting[ty, tx]
            wm[rows, ty * CH : (ty + 1) * CH] = mixing[ty, tx]


def tap_weights(uniting, mixing, interpret=False):
    vmem = pl.BlockSpec(memory_space=pltpu.VMEM)
    return pl.pallas_call(
        weights_kernel,
        out_shape=(
            jax.ShapeDtypeStruct((3 * CH, 9 * CH), BF16),
            jax.ShapeDtypeStruct((3 * CH, 3 * CH), BF16),
        ),
        in_specs=[vmem, vmem],
        out_specs=(vmem, vmem),
        compiler_params=pltpu.CompilerParams(vmem_limit_bytes=VMEM_LIMIT),
        cost_estimate=pl.CostEstimate(flops=0, bytes_accessed=600_000, transcendentals=0),
        interpret=interpret,
    )(uniting, mixing)


def with_table(rows, entries):
    plane = jnp.pad(entries.reshape(3, WIDTH), ((0, CH - 3), (0, 0)))
    return jnp.concatenate([rows, plane[None]])


def table_of(payload):
    return payload[2, 0:3].reshape(2, LEVELS, 4, 1, 32)


def shards(features, block_shift, quarter_pel, update_mask, uniting_weight, mixing_weight):
    band = features[0]
    row = lax.axis_index("rows")
    rows = lax.axis_size("rows")
    turned = row % 2
    edge = lax.dynamic_slice_in_dim(band, 8 * turned, HALF, axis=0)
    inner = lax.dynamic_slice_in_dim(band, 8 - 8 * turned, HALF, axis=0)
    rim = lax.dynamic_slice_in_dim(band, 14 * turned, 2, axis=0)
    near = lax.dynamic_slice_in_dim(band, 14 - 14 * turned, 2, axis=0)
    common = [turned, (row > 0).astype(jnp.int32), (row < rows - 1).astype(jnp.int32)]
    swapped = (lax.axis_index("tm") % 4 < 2).astype(jnp.int32)
    spot = lax.iota(jnp.int32, 4)
    flags = sum(jnp.where(spot == k, value, 0) for k, value in enumerate(common + [swapped]))

    def to_other(t):
        return t + 4

    def across(t):
        return t + 2 if t % 4 < 2 else t - 2

    def ahead(t):
        return t + 1

    def back(t):
        return t - 1

    own = jnp.stack([block_shift[:, :, 0], quarter_pel[:, :, 0]]).astype(BF16)
    at_edge = jnp.where(turned == 1, own[:, :, :, 1], own[:, :, :, 0])
    at_near = jnp.where(turned == 1, own[:, :, :, 0], own[:, :, :, 1])

    e = send(edge, to_other)
    h = send(edge, to_other, off_chip)
    i = send(inner, to_other)
    own_outer = send(with_table(rim, at_edge), row_to=off_chip)
    own_near = send(with_table(near, at_near), row_to=on_chip)
    n = send(i, row_to=on_chip)
    wu, wm = tap_weights(uniting_weight, mixing_weight)
    outer_table, near_table = table_of(own_outer), table_of(own_near)
    packed = jnp.concatenate(
        [
            jnp.where(turned == 1, near_table, outer_table),
            own,
            jnp.where(turned == 1, outer_table, near_table),
        ],
        axis=3,
    )
    *entries, wu, wm, flags = lax.optimization_barrier(
        tuple(packed[:, k, j : j + 2] for k in (2, 1, 0) for j in (0, 2))
        + (wu, wm, flags)
    )
    flags = (flags, update_mask)
    cols, table = make_columns(entries[0], entries[1])
    edge, inner, rim, near = run_level(
        2, flags, cols, table, wu, wm, [(h, e, i, n)], (own_outer, edge, inner, own_near)
    )

    own_outer = send(rim, row_to=off_chip)
    own_near = send(near, row_to=on_chip)
    e = send(edge, across)
    i = send(inner, across)
    xe = send(e, to_other)
    xh = send(e, to_other, off_chip)
    h = send(xe, to_other, off_chip)
    xi = send(i, to_other)
    n = send(i, row_to=on_chip)
    for_ahead = send(entries[4], back)
    for_back = send(entries[5], ahead)
    xn = send(xi, row_to=on_chip)
    cols, table = make_columns(entries[2], entries[3])
    next_cols, next_table = make_columns(for_ahead, for_back)
    edge, inner, _, _ = run_level(
        1,
        flags,
        cols,
        table,
        wu,
        wm,
        [(h, e, i, n), (xh, xe, xi, xn)],
        (own_outer, edge, inner, own_near),
    )

    outer = send(edge, row_to=off_chip)
    near = send(inner, row_to=on_chip)
    halves = run_warp_half(False, flags, next_cols, next_table, (edge, inner, near))
    inner_earlier = send(halves[0], ahead)
    inner_later = send(halves[1], back)
    halves = run_warp_half(True, flags, next_cols, next_table, (outer, edge, inner))
    earlier = send(halves[0], ahead)
    later = send(halves[1], back)
    inner_act, inner_rows = run_last_inner(flags, wu, wm, (inner, near, inner_earlier, inner_later))
    refined = run_last_outer(
        flags,
        wu,
        wm,
        (
            outer,
            edge,
            inner,
            near,
            inner_earlier,
            inner_later,
            inner_act,
            inner_rows,
            earlier,
            later,
        ),
    )
    return refined[None]


def solution(mesh):
    placed = (
        P("tm", "rows", None, None),
        P(None, None, "tm", "rows", None),
        P(None, None, "tm", "rows", None),
        P(None, "tm"),
        P(),
        P(),
    )
    return jax.shard_map(
        shards, mesh=mesh, in_specs=placed, out_specs=P("tm", "rows", None, None), check_vma=False
    )
```

```python
import functools

import jax
import jax.numpy as jnp
from jax import lax
from jax.experimental import pallas as pl
from jax.experimental.pallas import tpu as pltpu
from jax.sharding import PartitionSpec as P


LEVELS = 3
CH = 64
WIDTH = 256
HALF = 8
VMEM_LIMIT = 16 << 20
F32 = jnp.float32
BF16 = jnp.bfloat16


def pick_rows(v, bits, w0, w1, outs):
    b8, b4, b2, b1 = bits
    n8, n4, n2, n1 = outs + 8, outs + 4, outs + 2, outs + 1
    x8 = [jnp.where(b8, v[j + 8], v[j]) if j < outs + 3 else v[j] for j in range(n8)]
    x4 = [jnp.where(b4, x8[j + 4], x8[j]) for j in range(n4)]
    x2 = [jnp.where(b2, x4[j + 2], x4[j]) for j in range(n2)]
    x1 = [jnp.where(b1, x2[j + 1], x2[j]) for j in range(n1)]
    return [w0 * x1[i] + w1 * x1[i + 1] for i in range(outs)]


BLOCKS = ((1, 3, 19, 8, 2), (2, 11, 19, 8, 10), (0, 1, 13, 2, 0), (3, 19, 13, 2, 18))
OWN = slice(2 * CH, 3 * CH)


def turn(turned, place, size):
    return place + turned * (size - 2 * place)


def columns_kernel(first, second, cols, table, vals):
    vals[...] = jnp.zeros_like(vals)
    for ref, entries in enumerate((first, second)):
        for k in range(4):
            rows = entries[k // 2, k % 2].astype(F32)
            for block in range(4):
                at = (ref * 4 + block) * 8 + k
                vals[at : at + 1, :] = rows[block : block + 1]
    block_of = lax.broadcasted_iota(jnp.int32, (32, WIDTH), 1) // 8
    spread = (block_of == lax.broadcasted_iota(jnp.int32, (32, WIDTH), 0)).astype(F32)
    table[...] = jnp.dot(
        vals[...].astype(BF16), spread.astype(BF16), preferred_element_type=F32
    )
    apart = lax.broadcasted_iota(jnp.int32, (WIDTH, WIDTH), 0) - lax.broadcasted_iota(
        jnp.int32, (WIDTH, WIDTH), 1
    )

    @pl.loop(0, cols.shape[0])
    def _(n):
        entry = table[pl.ds(pl.multiple_of(n * 8, 8), 8), :]
        off = apart - entry[1:2].astype(jnp.int32)
        fx = entry[3:4] * 0.25
        cols[n] = jnp.where(off == 0, 1.0 - fx, jnp.where(off == 1, fx, 0.0)).astype(BF16)


def make_columns(first, second, interpret=False):
    vmem = pl.BlockSpec(memory_space=pltpu.VMEM)
    return pl.pallas_call(
        columns_kernel,
        out_shape=(
            jax.ShapeDtypeStruct((8, WIDTH, WIDTH), BF16),
            jax.ShapeDtypeStruct((64, WIDTH), F32),
        ),
        in_specs=[vmem, vmem],
        out_specs=(vmem, vmem),
        scratch_shapes=[pltpu.VMEM((64, 32), F32)],
        compiler_params=pltpu.CompilerParams(vmem_limit_bytes=VMEM_LIMIT),
        cost_estimate=pl.CostEstimate(
            flops=100_000_000, bytes_accessed=3_000_000, transcendentals=0
        ),
        interpret=interpret,
    )(first, second)


def column_pass(buffer, window, matrix):
    count = window.shape[0]
    buffer[...] = jnp.dot(
        window.reshape(count * CH, WIDTH), matrix, preferred_element_type=F32
    ).reshape(count, CH, WIDTH)


def row_pass(buffer, entry, keep, outs, put):
    lanes = (16, WIDTH)
    s = entry[0:1].astype(jnp.int32) + 5
    bits = [jnp.broadcast_to((s & b) != 0, lanes) for b in (8, 4, 2, 1)]
    fy = entry[2:3] * 0.25
    w1 = jnp.broadcast_to(fy * keep, lanes)
    w0 = jnp.broadcast_to((1.0 - fy) * keep, lanes)
    for c in range(CH // 16):
        v = [buffer[u, 16 * c : 16 * c + 16, :] for u in range(buffer.shape[0])]
        for i, row in enumerate(pick_rows(v, bits, w0, w1, outs)):
            put(i, 16 * c, row.astype(BF16))


def entry_at(table, n):
    return table[pl.ds(pl.multiple_of(n * 8, 8), 8), :]


def warp_into(flags, cols, table, source_of, passed, put_of):
    has_above = (flags[1] > 0).astype(F32)
    has_below = (flags[2] > 0).astype(F32)

    @pl.loop(0, 2)
    def _(which):
        put = put_of(which)

        def columns(k):
            block, first, count, _, _ = BLOCKS[k]
            column_pass(passed[k], source_of(which, first, count), cols[which * 4 + block])

        def rows(k):
            block, _, _, outs, start = BLOCKS[k]
            keep = {0: has_above, 3: has_below}.get(block, 1.0)
            row_pass(
                passed[k],
                entry_at(table, which * 4 + block),
                keep,
                outs,
                lambda i, c, value: put(start + i, c, value),
            )

        columns(0)
        for k in range(4):
            if k < 3:
                columns(k + 1)
            rows(k)


class Convolutions:
    def __init__(self, flags, update, wu, wm, joined, act):
        self.flags, self.update, self.wu, self.wm = flags, update, wu, wm
        self.joined, self.act = joined, act
        lane = lax.broadcasted_iota(jnp.int32, (CH, WIDTH), 1)
        self.not_first = lane > 0
        self.not_last = lane < WIDTH - 1

    def gather_taps(self, s):
        left = jnp.where(self.not_first, pltpu.roll(s[0:CH], 1, 1), 0.0)
        right = jnp.where(self.not_last, pltpu.roll(s[2 * CH :], WIDTH - 1, 1), 0.0)
        return s[CH : 2 * CH] + left + right

    def activate(self, a):
        window = self.joined[pl.ds(a, 3)].reshape(9 * CH, WIDTH)
        total = self.gather_taps(jnp.dot(self.wu[...], window, preferred_element_type=F32))
        half = 0.5 * total
        value = half + half * jnp.tanh(half)
        inside = jnp.where(
            a == 0, self.flags[1] > 0, jnp.where(a == 17, self.flags[2] > 0, True)
        )
        self.act[a] = (value * inside.astype(F32)).astype(BF16)

    def finish(self, y):
        window = self.act[pl.ds(y, 3)].reshape(3 * CH, WIDTH)
        total = self.gather_taps(jnp.dot(self.wm[...], window, preferred_element_type=F32))
        own = self.joined[y + 2, OWN, :].astype(F32)
        return (own + self.update.astype(F32) * total).astype(BF16)


def stack_rows(target, turned, pieces):
    for p in range(4):
        target[pl.ds(turn(turned, 8 * p, 24), 8)] = pieces[p][...]


def level_kernel(sources, level, split, flags, mask, cols, table, wu, wm, *refs):
    own_outer, own_edge, own_inner, own_near = refs[4 * sources : 4 * sources + 4]
    if split:
        out_edge, out_rim, joined, src, act = refs[4 * sources + 4 : 4 * sources + 9]
        passed = refs[4 * sources + 9 :]
    else:
        out_edge, out_inner, out_rim, out_near = refs[4 * sources + 4 : 4 * sources + 8]
        src, joined, act = refs[4 * sources + 8 : 4 * sources + 11]
        passed = refs[4 * sources + 11 :]
    turned = flags[0]
    for i in range(sources):
        stack_rows(src.at[i], turned, refs[4 * i : 4 * i + 4])
    joined[pl.ds(turn(turned, 0, 18), 2), OWN] = own_outer[0:2]
    joined[pl.ds(turn(turned, 2, 12), 8), OWN] = own_edge[...]
    joined[pl.ds(turn(turned, 10, 12), 8), OWN] = own_inner[...]
    joined[pl.ds(turn(turned, 18, 18), 2), OWN] = own_near[0:2]

    def source_of(which, first, count):
        return src[which ^ flags[3] if sources == 2 else 0, first : first + count]

    def put_of(which):
        def put(row, c, value):
            joined[row, pl.ds(pl.multiple_of(which * CH + c, 16), 16), :] = value

        return put

    warp_into(flags, cols, table, source_of, passed, put_of)
    conv = Convolutions(flags, mask[level, 0], wu, wm, joined, act)

    if split:

        @pl.loop(0, 2)
        def _(n):
            for k in range(5):
                conv.activate(8 * turned + 5 * n + k)

        for k in range(HALF):
            out_edge[k] = conv.finish(8 * turned + k)
        out_rim[...] = out_edge[pl.ds(turn(turned, 0, 6), 2)]
        return

    @pl.loop(0, 3)
    def _(n):
        for k in range(6):
            conv.activate(6 * n + k)

    @pl.loop(0, 2)
    def _(n):
        for k in range(4):
            y = 4 * n + k
            out_edge[y] = conv.finish(y + turn(turned, 0, 8))
            out_inner[y] = conv.finish(y + turn(turned, 8, 8))

    out_rim[...] = out_edge[pl.ds(turn(turned, 0, 6), 2)]
    out_near[...] = out_inner[pl.ds(turn(turned, 6, 6), 2)]


def inner_kernel(level, flags, mask, wu, wm, joined, out_inner, out_near, act):
    turned = flags[0]
    conv = Convolutions(flags, mask[level, 0], wu, wm, joined, act)
    start = 8 - 8 * turned

    @pl.loop(0, 2)
    def _(n):
        for k in range(5):
            conv.activate(start + 5 * n + k)

    for k in range(HALF):
        out_inner[k] = conv.finish(start + k)
    out_near[...] = out_inner[pl.ds(turn(turned, 6, 6), 2)]


def warp_half_kernel(is_outer, flags, mask, cols, table, *refs):
    pieces, (ahead, back, src, both, main_rows, halo_rows) = refs[:3], refs[3:]
    turned = flags[0]
    part = turned if is_outer else 1 - turned
    for p in range(3):
        place = p if is_outer else p + 1
        src[pl.ds(turn(turned, 8 * place, 24), 8)] = pieces[p][...]
    keep = (jnp.where(part == 1, flags[2], flags[1]) > 0).astype(F32)

    @pl.loop(0, 2)
    def _(which):
        def put_from(start):
            def put(i, c, value):
                both[which, start + i, c : c + 16, :] = value

            return put

        main, halo = which * 4 + 1 + part, which * 4 + 3 * part
        column_pass(main_rows, src[pl.ds(3 + 8 * part, 19)], cols[main])
        column_pass(halo_rows, src[pl.ds(1 + 18 * part, 13)], cols[halo])
        row_pass(main_rows, entry_at(table, main), 1.0, 8, put_from(2 - 2 * part))
        row_pass(halo_rows, entry_at(table, halo), keep, 2, put_from(8 * part))

    ahead[...] = both[0]
    back[...] = both[1]


def last_inner_kernel(
    flags, mask, wu, wm, inner, near, earlier, later, out_act, out_rows, joined, act
):
    turned = flags[0]
    part = 1 - turned
    joined[pl.ds(turn(turned, 10, 12), 8), OWN] = inner[...]
    joined[pl.ds(turn(turned, 18, 18), 2), OWN] = near[pl.ds(turn(turned, 0, 6), 2)]
    joined[pl.ds(10 * part, 10), 0:CH] = earlier[...]
    joined[pl.ds(10 * part, 10), CH : 2 * CH] = later[...]
    conv = Convolutions(flags, mask[0, 0], wu, wm, joined, act)

    @pl.loop(0, 2)
    def _(n):
        for k in range(4):
            conv.activate(10 * part + 4 * n + k)

    for k in range(6):
        out_rows[k] = conv.finish(10 * part + k)
    out_act[...] = act[pl.ds(10 * part, 8)]


def last_outer_kernel(
    flags,
    mask,
    wu,
    wm,
    outer,
    edge,
    inner,
    near,
    inner_earlier,
    inner_later,
    inner_act,
    inner_rows,
    earlier,
    later,
    out,
    joined,
    act,
):
    turned = flags[0]
    part = turned
    joined[pl.ds(turn(turned, 0, 18), 2), OWN] = outer[pl.ds(turn(turned, 6, 6), 2)]
    joined[pl.ds(turn(turned, 2, 12), 8), OWN] = edge[...]
    joined[pl.ds(turn(turned, 10, 12), 8), OWN] = inner[...]
    joined[pl.ds(turn(turned, 18, 18), 2), OWN] = near[pl.ds(turn(turned, 0, 6), 2)]
    joined[pl.ds(10 * part, 10), 0:CH] = earlier[...]
    joined[pl.ds(10 * part, 10), CH : 2 * CH] = later[...]
    joined[pl.ds(10 - 10 * part, 10), 0:CH] = inner_earlier[...]
    joined[pl.ds(10 - 10 * part, 10), CH : 2 * CH] = inner_later[...]
    act[pl.ds(10 - 10 * part, 8)] = inner_act[...]
    out[pl.ds(10 - 10 * part, 6)] = inner_rows[...]
    conv = Convolutions(flags, mask[0, 0], wu, wm, joined, act)

    @pl.loop(0, 2)
    def _(n):
        for k in range(5):
            conv.activate(8 * part + 5 * n + k)

    @pl.loop(0, 2)
    def _(n):
        for k in range(5):
            y = 6 * part + 5 * n + k
            out[y] = conv.finish(y)


def on_core(kernel, out_shape, scratch, cost, operands, interpret):
    vmem = pl.BlockSpec(memory_space=pltpu.VMEM)
    return pl.pallas_call(
        kernel,
        out_shape=out_shape,
        in_specs=[pl.BlockSpec(memory_space=pltpu.SMEM)] * 2 + [vmem] * (len(operands) - 2),
        out_specs=(vmem,) * len(out_shape),
        scratch_shapes=scratch,
        compiler_params=pltpu.CompilerParams(vmem_limit_bytes=VMEM_LIMIT),
        cost_estimate=pl.CostEstimate(
            flops=cost, bytes_accessed=4_000_000, transcendentals=300_000
        ),
        interpret=interpret,
    )(*operands)


def passed_buffers():
    return [pltpu.VMEM((count, CH, WIDTH), F32) for _, _, count, _, _ in BLOCKS]


def band_buffers():
    return [pltpu.VMEM((20, 3 * CH, WIDTH), BF16), pltpu.VMEM((18, CH, WIDTH), BF16)]


def run_level(level, flags, cols, table, wu, wm, sources, own, split=False, interpret=False):
    half = jax.ShapeDtypeStruct((HALF, CH, WIDTH), BF16)
    edge = jax.ShapeDtypeStruct((2, CH, WIDTH), BF16)
    rows = jax.ShapeDtypeStruct((20, 3 * CH, WIDTH), BF16)
    operands = [*flags, cols, table, wu, wm] + [p for s in sources for p in s] + list(own)
    scratch = [pltpu.VMEM((len(sources), 32, CH, WIDTH), BF16)]
    return on_core(
        functools.partial(level_kernel, len(sources), level, split),
        (half, edge, rows) if split else (half, half, edge, edge),
        scratch + band_buffers()[split:] + passed_buffers(),
        2_300_000_000 if split else 3_000_000_000,
        operands,
        interpret,
    )


def run_inner(level, flags, wu, wm, joined, interpret=False):
    return on_core(
        functools.partial(inner_kernel, level),
        (
            jax.ShapeDtypeStruct((HALF, CH, WIDTH), BF16),
            jax.ShapeDtypeStruct((2, CH, WIDTH), BF16),
        ),
        band_buffers()[1:],
        700_000_000,
        [*flags, wu, wm, joined],
        interpret,
    )


def run_warp_half(is_outer, flags, cols, table, pieces, interpret=False):
    return on_core(
        functools.partial(warp_half_kernel, is_outer),
        (jax.ShapeDtypeStruct((10, CH, WIDTH), BF16),) * 2,
        [
            pltpu.VMEM((32, CH, WIDTH), BF16),
            pltpu.VMEM((2, 10, CH, WIDTH), BF16),
            pltpu.VMEM((19, CH, WIDTH), F32),
            pltpu.VMEM((13, CH, WIDTH), F32),
        ],
        800_000_000,
        [*flags, cols, table, *pieces],
        interpret,
    )


def run_last_inner(flags, wu, wm, operands, interpret=False):
    return on_core(
        last_inner_kernel,
        (
            jax.ShapeDtypeStruct((8, CH, WIDTH), BF16),
            jax.ShapeDtypeStruct((6, CH, WIDTH), BF16),
        ),
        band_buffers(),
        600_000_000,
        [*flags, wu, wm, *operands],
        interpret,
    )


def run_last_outer(flags, wu, wm, operands, interpret=False):
    return on_core(
        last_outer_kernel,
        (jax.ShapeDtypeStruct((2 * HALF, CH, WIDTH), BF16),),
        band_buffers(),
        900_000_000,
        [*flags, wu, wm, *operands],
        interpret,
    )[0]


def send(x, frame_to=lambda t: t, row_to=lambda r: r):
    frames, rows = lax.axis_size("tm"), lax.axis_size("rows")
    route = [
        (t * rows + r, (frame_to(t) % frames) * rows + row_to(r))
        for t in range(frames)
        for r in range(rows)
        if 0 <= row_to(r) < rows
    ]
    return lax.ppermute(x, ("tm", "rows"), route)


def off_chip(r):
    return r + 1 if r % 2 else r - 1


def on_chip(r):
    return r ^ 1


def weights_kernel(uniting, mixing, wu, wm):
    for ty in range(3):
        for tx in range(3):
            rows = slice(tx * CH, tx * CH + CH)
            wu[rows, ty * 3 * CH : (ty + 1) * 3 * CH] = uniting[ty, tx]
            wm[rows, ty * CH : (ty + 1) * CH] = mixing[ty, tx]


def tap_weights(uniting, mixing, interpret=False):
    vmem = pl.BlockSpec(memory_space=pltpu.VMEM)
    return pl.pallas_call(
        weights_kernel,
        out_shape=(
            jax.ShapeDtypeStruct((3 * CH, 9 * CH), BF16),
            jax.ShapeDtypeStruct((3 * CH, 3 * CH), BF16),
        ),
        in_specs=[vmem, vmem],
        out_specs=(vmem, vmem),
        compiler_params=pltpu.CompilerParams(vmem_limit_bytes=VMEM_LIMIT),
        cost_estimate=pl.CostEstimate(flops=0, bytes_accessed=600_000, transcendentals=0),
        interpret=interpret,
    )(uniting, mixing)


def with_table(rows, entries):
    plane = jnp.pad(entries.reshape(3, WIDTH), ((0, CH - 3), (0, 0)))
    return jnp.concatenate([rows, plane[None]])


def table_of(payload):
    return payload[2, 0:3].reshape(2, LEVELS, 4, 1, 32)


def shards(features, block_shift, quarter_pel, update_mask, uniting_weight, mixing_weight):
    band = features[0]
    row = lax.axis_index("rows")
    rows = lax.axis_size("rows")
    turned = row % 2
    edge = lax.dynamic_slice_in_dim(band, 8 * turned, HALF, axis=0)
    inner = lax.dynamic_slice_in_dim(band, 8 - 8 * turned, HALF, axis=0)
    rim = lax.dynamic_slice_in_dim(band, 14 * turned, 2, axis=0)
    near = lax.dynamic_slice_in_dim(band, 14 - 14 * turned, 2, axis=0)
    common = [turned, (row > 0).astype(jnp.int32), (row < rows - 1).astype(jnp.int32)]
    swapped = (lax.axis_index("tm") % 4 < 2).astype(jnp.int32)
    spot = lax.iota(jnp.int32, 4)
    flags = sum(jnp.where(spot == k, value, 0) for k, value in enumerate(common + [swapped]))

    def to_other(t):
        return t + 4

    def across(t):
        return t + 2 if t % 4 < 2 else t - 2

    def ahead(t):
        return t + 1

    def back(t):
        return t - 1

    own = jnp.stack([block_shift[:, :, 0], quarter_pel[:, :, 0]]).astype(BF16)
    at_edge = jnp.where(turned == 1, own[:, :, :, 1], own[:, :, :, 0])
    at_near = jnp.where(turned == 1, own[:, :, :, 0], own[:, :, :, 1])

    e = send(edge, to_other)
    h = send(edge, to_other, off_chip)
    i = send(inner, to_other)
    own_outer = send(with_table(rim, at_edge), row_to=off_chip)
    own_near = send(with_table(near, at_near), row_to=on_chip)
    n = send(i, row_to=on_chip)
    wu, wm = tap_weights(uniting_weight, mixing_weight)
    outer_table, near_table = table_of(own_outer), table_of(own_near)
    packed = jnp.concatenate(
        [
            jnp.where(turned == 1, near_table, outer_table),
            own,
            jnp.where(turned == 1, outer_table, near_table),
        ],
        axis=3,
    )
    *entries, wu, wm, flags = lax.optimization_barrier(
        tuple(packed[:, k, j : j + 2] for k in (2, 1, 0) for j in (0, 2))
        + (wu, wm, flags)
    )
    flags = (flags, update_mask)
    cols, table = make_columns(entries[0], entries[1])
    edge, rim, joined = run_level(
        2,
        flags,
        cols,
        table,
        wu,
        wm,
        [(h, e, i, n)],
        (own_outer, edge, inner, own_near),
        split=True,
    )

    inner, near = run_inner(2, flags, wu, wm, joined)
    own_outer = send(rim, row_to=off_chip)
    own_near = send(near, row_to=on_chip)
    e = send(edge, across)
    i = send(inner, across)
    xe = send(e, to_other)
    xh = send(e, to_other, off_chip)
    h = send(xe, to_other, off_chip)
    xi = send(i, to_other)
    n = send(i, row_to=on_chip)
    for_ahead = send(entries[4], back)
    for_back = send(entries[5], ahead)
    xn = send(xi, row_to=on_chip)
    cols, table = make_columns(entries[2], entries[3])
    next_cols, next_table = make_columns(for_ahead, for_back)
    edge, _, joined = run_level(
        1,
        flags,
        cols,
        table,
        wu,
        wm,
        [(h, e, i, n), (xh, xe, xi, xn)],
        (own_outer, edge, inner, own_near),
        split=True,
    )

    inner, _ = run_inner(1, flags, wu, wm, joined)
    outer = send(edge, row_to=off_chip)
    near = send(inner, row_to=on_chip)
    halves = run_warp_half(False, flags, next_cols, next_table, (edge, inner, near))
    inner_earlier = send(halves[0], ahead)
    inner_later = send(halves[1], back)
    halves = run_warp_half(True, flags, next_cols, next_table, (outer, edge, inner))
    earlier = send(halves[0], ahead)
    later = send(halves[1], back)
    inner_act, inner_rows = run_last_inner(flags, wu, wm, (inner, near, inner_earlier, inner_later))
    refined = run_last_outer(
        flags,
        wu,
        wm,
        (
            outer,
            edge,
            inner,
            near,
            inner_earlier,
            inner_later,
            inner_act,
            inner_rows,
            earlier,
            later,
        ),
    )
    return refined[None]


def solution(mesh):
    placed = (
        P("tm", "rows", None, None),
        P(None, None, "tm", "rows", None),
        P(None, None, "tm", "rows", None),
        P(None, "tm"),
        P(),
        P(),
    )
    return jax.shard_map(
        shards, mesh=mesh, in_specs=placed, out_specs=P("tm", "rows", None, None), check_vma=False
    )
```

```python
import functools

import jax
import jax.numpy as jnp
from jax import lax
from jax.experimental import pallas as pl
from jax.experimental.pallas import tpu as pltpu
from jax.sharding import PartitionSpec as P


LEVELS = 3
CH = 64
WIDTH = 256
HALF = 8
VMEM_LIMIT = 16 << 20
F32 = jnp.float32
BF16 = jnp.bfloat16


def pick_rows(v, bits, w0, w1, outs):
    b8, b4, b2, b1 = bits
    n8, n4, n2, n1 = outs + 8, outs + 4, outs + 2, outs + 1
    x8 = [jnp.where(b8, v[j + 8], v[j]) if j < outs + 3 else v[j] for j in range(n8)]
    x4 = [jnp.where(b4, x8[j + 4], x8[j]) for j in range(n4)]
    x2 = [jnp.where(b2, x4[j + 2], x4[j]) for j in range(n2)]
    x1 = [jnp.where(b1, x2[j + 1], x2[j]) for j in range(n1)]
    return [w0 * x1[i] + w1 * x1[i + 1] for i in range(outs)]


BLOCKS = ((1, 3, 19, 8, 2), (2, 11, 19, 8, 10), (0, 1, 13, 2, 0), (3, 19, 13, 2, 18))
OWN = slice(2 * CH, 3 * CH)


def turn(turned, place, size):
    return place + turned * (size - 2 * place)


def columns_kernel(first, second, cols, table, vals):
    vals[...] = jnp.zeros_like(vals)
    for ref, entries in enumerate((first, second)):
        for k in range(4):
            rows = entries[k // 2, k % 2].astype(F32)
            for block in range(4):
                at = (ref * 4 + block) * 8 + k
                vals[at : at + 1, :] = rows[block : block + 1]
    block_of = lax.broadcasted_iota(jnp.int32, (32, WIDTH), 1) // 8
    spread = (block_of == lax.broadcasted_iota(jnp.int32, (32, WIDTH), 0)).astype(F32)
    table[...] = jnp.dot(
        vals[...].astype(BF16), spread.astype(BF16), preferred_element_type=F32
    )
    apart = lax.broadcasted_iota(jnp.int32, (WIDTH, WIDTH), 0) - lax.broadcasted_iota(
        jnp.int32, (WIDTH, WIDTH), 1
    )

    @pl.loop(0, cols.shape[0])
    def _(n):
        entry = table[pl.ds(pl.multiple_of(n * 8, 8), 8), :]
        off = apart - entry[1:2].astype(jnp.int32)
        fx = entry[3:4] * 0.25
        cols[n] = jnp.where(off == 0, 1.0 - fx, jnp.where(off == 1, fx, 0.0)).astype(BF16)


def make_columns(first, second, interpret=False):
    vmem = pl.BlockSpec(memory_space=pltpu.VMEM)
    return pl.pallas_call(
        columns_kernel,
        out_shape=(
            jax.ShapeDtypeStruct((8, WIDTH, WIDTH), BF16),
            jax.ShapeDtypeStruct((64, WIDTH), F32),
        ),
        in_specs=[vmem, vmem],
        out_specs=(vmem, vmem),
        scratch_shapes=[pltpu.VMEM((64, 32), F32)],
        compiler_params=pltpu.CompilerParams(vmem_limit_bytes=VMEM_LIMIT),
        cost_estimate=pl.CostEstimate(
            flops=100_000_000, bytes_accessed=3_000_000, transcendentals=0
        ),
        interpret=interpret,
    )(first, second)


def column_pass(buffer, window, matrix):
    count = window.shape[0]
    buffer[...] = jnp.dot(
        window.reshape(count * CH, WIDTH), matrix, preferred_element_type=F32
    ).reshape(count, CH, WIDTH)


def row_pass(buffer, entry, keep, outs, put):
    lanes = (16, WIDTH)
    s = entry[0:1].astype(jnp.int32) + 5
    bits = [jnp.broadcast_to((s & b) != 0, lanes) for b in (8, 4, 2, 1)]
    fy = entry[2:3] * 0.25
    w1 = jnp.broadcast_to(fy * keep, lanes)
    w0 = jnp.broadcast_to((1.0 - fy) * keep, lanes)
    for c in range(CH // 16):
        v = [buffer[u, 16 * c : 16 * c + 16, :] for u in range(buffer.shape[0])]
        for i, row in enumerate(pick_rows(v, bits, w0, w1, outs)):
            put(i, 16 * c, row.astype(BF16))


def entry_at(table, n):
    return table[pl.ds(pl.multiple_of(n * 8, 8), 8), :]


def warp_into(flags, cols, table, source_of, passed, put_of):
    has_above = (flags[1] > 0).astype(F32)
    has_below = (flags[2] > 0).astype(F32)

    @pl.loop(0, 2)
    def _(which):
        put = put_of(which)

        def columns(k):
            block, first, count, _, _ = BLOCKS[k]
            column_pass(passed[k], source_of(which, first, count), cols[which * 4 + block])

        def rows(k):
            block, _, _, outs, start = BLOCKS[k]
            keep = {0: has_above, 3: has_below}.get(block, 1.0)
            row_pass(
                passed[k],
                entry_at(table, which * 4 + block),
                keep,
                outs,
                lambda i, c, value: put(start + i, c, value),
            )

        columns(0)
        for k in range(4):
            if k < 3:
                columns(k + 1)
            rows(k)


class Convolutions:
    def __init__(self, flags, update, wu, wm, joined, act):
        self.flags, self.update, self.wu, self.wm = flags, update, wu, wm
        self.joined, self.act = joined, act
        lane = lax.broadcasted_iota(jnp.int32, (CH, WIDTH), 1)
        self.not_first = lane > 0
        self.not_last = lane < WIDTH - 1

    def gather_taps(self, s):
        left = jnp.where(self.not_first, pltpu.roll(s[0:CH], 1, 1), 0.0)
        right = jnp.where(self.not_last, pltpu.roll(s[2 * CH :], WIDTH - 1, 1), 0.0)
        return s[CH : 2 * CH] + left + right

    def activate(self, a):
        window = self.joined[pl.ds(a, 3)].reshape(9 * CH, WIDTH)
        total = self.gather_taps(jnp.dot(self.wu[...], window, preferred_element_type=F32))
        half = 0.5 * total
        value = half + half * jnp.tanh(half)
        inside = jnp.where(
            a == 0, self.flags[1] > 0, jnp.where(a == 17, self.flags[2] > 0, True)
        )
        self.act[a] = (value * inside.astype(F32)).astype(BF16)

    def finish(self, y):
        window = self.act[pl.ds(y, 3)].reshape(3 * CH, WIDTH)
        total = self.gather_taps(jnp.dot(self.wm[...], window, preferred_element_type=F32))
        own = self.joined[y + 2, OWN, :].astype(F32)
        return (own + self.update.astype(F32) * total).astype(BF16)


def stack_rows(target, turned, pieces):
    for p in range(4):
        target[pl.ds(turn(turned, 8 * p, 24), 8)] = pieces[p][...]


def level_kernel(sources, level, split, flags, mask, cols, table, wu, wm, *refs):
    own_outer, own_edge, own_inner, own_near = refs[4 * sources : 4 * sources + 4]
    if split:
        out_edge, out_rim, joined, src, act = refs[4 * sources + 4 : 4 * sources + 9]
        passed = refs[4 * sources + 9 :]
    else:
        out_edge, out_inner, out_rim, out_near = refs[4 * sources + 4 : 4 * sources + 8]
        src, joined, act = refs[4 * sources + 8 : 4 * sources + 11]
        passed = refs[4 * sources + 11 :]
    turned = flags[0]
    for i in range(sources):
        stack_rows(src.at[i], turned, refs[4 * i : 4 * i + 4])
    joined[pl.ds(turn(turned, 0, 18), 2), OWN] = own_outer[0:2]
    joined[pl.ds(turn(turned, 2, 12), 8), OWN] = own_edge[...]
    joined[pl.ds(turn(turned, 10, 12), 8), OWN] = own_inner[...]
    joined[pl.ds(turn(turned, 18, 18), 2), OWN] = own_near[0:2]

    def source_of(which, first, count):
        return src[which ^ flags[3] if sources == 2 else 0, first : first + count]

    def put_of(which):
        def put(row, c, value):
            joined[row, pl.ds(pl.multiple_of(which * CH + c, 16), 16), :] = value

        return put

    warp_into(flags, cols, table, source_of, passed, put_of)
    conv = Convolutions(flags, mask[level, 0], wu, wm, joined, act)

    if split:

        @pl.loop(0, 2)
        def _(n):
            for k in range(5):
                conv.activate(8 * turned + 5 * n + k)

        for k in range(HALF):
            out_edge[k] = conv.finish(8 * turned + k)
        out_rim[...] = out_edge[pl.ds(turn(turned, 0, 6), 2)]
        return

    @pl.loop(0, 3)
    def _(n):
        for k in range(6):
            conv.activate(6 * n + k)

    @pl.loop(0, 2)
    def _(n):
        for k in range(4):
            y = 4 * n + k
            out_edge[y] = conv.finish(y + turn(turned, 0, 8))
            out_inner[y] = conv.finish(y + turn(turned, 8, 8))

    out_rim[...] = out_edge[pl.ds(turn(turned, 0, 6), 2)]
    out_near[...] = out_inner[pl.ds(turn(turned, 6, 6), 2)]


def inner_kernel(level, flags, mask, wu, wm, joined, out_inner, out_near, act):
    turned = flags[0]
    conv = Convolutions(flags, mask[level, 0], wu, wm, joined, act)
    start = 8 - 8 * turned

    @pl.loop(0, 2)
    def _(n):
        for k in range(5):
            conv.activate(start + 5 * n + k)

    for k in range(HALF):
        out_inner[k] = conv.finish(start + k)
    out_near[...] = out_inner[pl.ds(turn(turned, 6, 6), 2)]


def warp_half_kernel(is_outer, flags, mask, cols, table, *refs):
    pieces, (ahead, back, src, both, main_rows, halo_rows) = refs[:3], refs[3:]
    turned = flags[0]
    part = turned if is_outer else 1 - turned
    for p in range(3):
        place = p if is_outer else p + 1
        src[pl.ds(turn(turned, 8 * place, 24), 8)] = pieces[p][...]
    keep = (jnp.where(part == 1, flags[2], flags[1]) > 0).astype(F32)

    @pl.loop(0, 2)
    def _(which):
        def put_from(start):
            def put(i, c, value):
                both[which, start + i, c : c + 16, :] = value

            return put

        main, halo = which * 4 + 1 + part, which * 4 + 3 * part
        column_pass(main_rows, src[pl.ds(3 + 8 * part, 19)], cols[main])
        column_pass(halo_rows, src[pl.ds(1 + 18 * part, 13)], cols[halo])
        row_pass(main_rows, entry_at(table, main), 1.0, 8, put_from(2 - 2 * part))
        row_pass(halo_rows, entry_at(table, halo), keep, 2, put_from(8 * part))

    ahead[...] = both[0]
    back[...] = both[1]


def last_inner_kernel(
    flags, mask, wu, wm, inner, near, earlier, later, out_act, out_rows, joined, act
):
    turned = flags[0]
    part = 1 - turned
    joined[pl.ds(turn(turned, 10, 12), 8), OWN] = inner[...]
    joined[pl.ds(turn(turned, 18, 18), 2), OWN] = near[pl.ds(turn(turned, 0, 6), 2)]
    joined[pl.ds(10 * part, 10), 0:CH] = earlier[...]
    joined[pl.ds(10 * part, 10), CH : 2 * CH] = later[...]
    conv = Convolutions(flags, mask[0, 0], wu, wm, joined, act)

    @pl.loop(0, 2)
    def _(n):
        for k in range(4):
            conv.activate(10 * part + 4 * n + k)

    for k in range(6):
        out_rows[k] = conv.finish(10 * part + k)
    out_act[...] = act[pl.ds(10 * part, 8)]


def last_outer_kernel(
    flags,
    mask,
    wu,
    wm,
    outer,
    edge,
    inner,
    inner_earlier,
    inner_later,
    inner_act,
    inner_rows,
    earlier,
    later,
    out,
    joined,
    act,
):
    turned = flags[0]
    part = turned
    joined[pl.ds(turn(turned, 0, 18), 2), OWN] = outer[pl.ds(turn(turned, 6, 6), 2)]
    joined[pl.ds(turn(turned, 2, 12), 8), OWN] = edge[...]
    middle = pl.ds(10 - 2 * part, 2)
    joined[middle, OWN] = inner[pl.ds(6 * part, 2)]
    joined[pl.ds(10 * part, 10), 0:CH] = earlier[...]
    joined[pl.ds(10 * part, 10), CH : 2 * CH] = later[...]
    joined[middle, 0:CH] = inner_earlier[pl.ds(8 * part, 2)]
    joined[middle, CH : 2 * CH] = inner_later[pl.ds(8 * part, 2)]
    act[pl.ds(10 - 4 * part, 2)] = inner_act[pl.ds(6 * part, 2)]
    out[pl.ds(10 - 10 * part, 6)] = inner_rows[...]
    conv = Convolutions(flags, mask[0, 0], wu, wm, joined, act)

    for k in range(10):
        conv.activate(8 * part + k)
    for k in range(10):
        out[6 * part + k] = conv.finish(6 * part + k)


def on_core(kernel, out_shape, scratch, cost, operands, interpret):
    vmem = pl.BlockSpec(memory_space=pltpu.VMEM)
    return pl.pallas_call(
        kernel,
        out_shape=out_shape,
        in_specs=[pl.BlockSpec(memory_space=pltpu.SMEM)] * 2 + [vmem] * (len(operands) - 2),
        out_specs=(vmem,) * len(out_shape),
        scratch_shapes=scratch,
        compiler_params=pltpu.CompilerParams(vmem_limit_bytes=VMEM_LIMIT),
        cost_estimate=pl.CostEstimate(
            flops=cost, bytes_accessed=4_000_000, transcendentals=300_000
        ),
        interpret=interpret,
    )(*operands)


def passed_buffers():
    return [pltpu.VMEM((count, CH, WIDTH), F32) for _, _, count, _, _ in BLOCKS]


def band_buffers():
    return [pltpu.VMEM((20, 3 * CH, WIDTH), BF16), pltpu.VMEM((18, CH, WIDTH), BF16)]


def run_level(level, flags, cols, table, wu, wm, sources, own, split=False, interpret=False):
    half = jax.ShapeDtypeStruct((HALF, CH, WIDTH), BF16)
    edge = jax.ShapeDtypeStruct((2, CH, WIDTH), BF16)
    rows = jax.ShapeDtypeStruct((20, 3 * CH, WIDTH), BF16)
    operands = [*flags, cols, table, wu, wm] + [p for s in sources for p in s] + list(own)
    scratch = [pltpu.VMEM((len(sources), 32, CH, WIDTH), BF16)]
    return on_core(
        functools.partial(level_kernel, len(sources), level, split),
        (half, edge, rows) if split else (half, half, edge, edge),
        scratch + band_buffers()[split:] + passed_buffers(),
        2_300_000_000 if split else 3_000_000_000,
        operands,
        interpret,
    )


def run_inner(level, flags, wu, wm, joined, interpret=False):
    return on_core(
        functools.partial(inner_kernel, level),
        (
            jax.ShapeDtypeStruct((HALF, CH, WIDTH), BF16),
            jax.ShapeDtypeStruct((2, CH, WIDTH), BF16),
        ),
        band_buffers()[1:],
        700_000_000,
        [*flags, wu, wm, joined],
        interpret,
    )


def run_warp_half(is_outer, flags, cols, table, pieces, interpret=False):
    return on_core(
        functools.partial(warp_half_kernel, is_outer),
        (jax.ShapeDtypeStruct((10, CH, WIDTH), BF16),) * 2,
        [
            pltpu.VMEM((32, CH, WIDTH), BF16),
            pltpu.VMEM((2, 10, CH, WIDTH), BF16),
            pltpu.VMEM((19, CH, WIDTH), F32),
            pltpu.VMEM((13, CH, WIDTH), F32),
        ],
        800_000_000,
        [*flags, cols, table, *pieces],
        interpret,
    )


def run_last_inner(flags, wu, wm, operands, interpret=False):
    return on_core(
        last_inner_kernel,
        (
            jax.ShapeDtypeStruct((8, CH, WIDTH), BF16),
            jax.ShapeDtypeStruct((6, CH, WIDTH), BF16),
        ),
        band_buffers(),
        600_000_000,
        [*flags, wu, wm, *operands],
        interpret,
    )


def run_last_outer(flags, wu, wm, operands, interpret=False):
    return on_core(
        last_outer_kernel,
        (jax.ShapeDtypeStruct((2 * HALF, CH, WIDTH), BF16),),
        band_buffers(),
        900_000_000,
        [*flags, wu, wm, *operands],
        interpret,
    )[0]


def send(x, frame_to=lambda t: t, row_to=lambda r: r):
    frames, rows = lax.axis_size("tm"), lax.axis_size("rows")
    route = [
        (t * rows + r, (frame_to(t) % frames) * rows + row_to(r))
        for t in range(frames)
        for r in range(rows)
        if 0 <= row_to(r) < rows
    ]
    return lax.ppermute(x, ("tm", "rows"), route)


def off_chip(r):
    return r + 1 if r % 2 else r - 1


def on_chip(r):
    return r ^ 1


def weights_kernel(uniting, mixing, wu, wm):
    for ty in range(3):
        for tx in range(3):
            rows = slice(tx * CH, tx * CH + CH)
            wu[rows, ty * 3 * CH : (ty + 1) * 3 * CH] = uniting[ty, tx]
            wm[rows, ty * CH : (ty + 1) * CH] = mixing[ty, tx]


def tap_weights(uniting, mixing, interpret=False):
    vmem = pl.BlockSpec(memory_space=pltpu.VMEM)
    return pl.pallas_call(
        weights_kernel,
        out_shape=(
            jax.ShapeDtypeStruct((3 * CH, 9 * CH), BF16),
            jax.ShapeDtypeStruct((3 * CH, 3 * CH), BF16),
        ),
        in_specs=[vmem, vmem],
        out_specs=(vmem, vmem),
        compiler_params=pltpu.CompilerParams(vmem_limit_bytes=VMEM_LIMIT),
        cost_estimate=pl.CostEstimate(flops=0, bytes_accessed=600_000, transcendentals=0),
        interpret=interpret,
    )(uniting, mixing)


def with_table(rows, entries):
    plane = jnp.pad(entries.reshape(3, WIDTH), ((0, CH - 3), (0, 0)))
    return jnp.concatenate([rows, plane[None]])


def table_of(payload):
    return payload[2, 0:3].reshape(2, LEVELS, 4, 1, 32)


def shards(features, block_shift, quarter_pel, update_mask, uniting_weight, mixing_weight):
    band = features[0]
    row = lax.axis_index("rows")
    rows = lax.axis_size("rows")
    turned = row % 2
    edge = lax.dynamic_slice_in_dim(band, 8 * turned, HALF, axis=0)
    inner = lax.dynamic_slice_in_dim(band, 8 - 8 * turned, HALF, axis=0)
    rim = lax.dynamic_slice_in_dim(band, 14 * turned, 2, axis=0)
    near = lax.dynamic_slice_in_dim(band, 14 - 14 * turned, 2, axis=0)
    common = [turned, (row > 0).astype(jnp.int32), (row < rows - 1).astype(jnp.int32)]
    swapped = (lax.axis_index("tm") % 4 < 2).astype(jnp.int32)
    spot = lax.iota(jnp.int32, 4)
    flags = sum(jnp.where(spot == k, value, 0) for k, value in enumerate(common + [swapped]))

    def to_other(t):
        return t + 4

    def across(t):
        return t + 2 if t % 4 < 2 else t - 2

    def ahead(t):
        return t + 1

    def back(t):
        return t - 1

    own = jnp.stack([block_shift[:, :, 0], quarter_pel[:, :, 0]]).astype(BF16)
    at_edge = jnp.where(turned == 1, own[:, :, :, 1], own[:, :, :, 0])
    at_near = jnp.where(turned == 1, own[:, :, :, 0], own[:, :, :, 1])

    e = send(edge, to_other)
    h = send(edge, to_other, off_chip)
    i = send(inner, to_other)
    own_outer = send(with_table(rim, at_edge), row_to=off_chip)
    own_near = send(with_table(near, at_near), row_to=on_chip)
    n = send(i, row_to=on_chip)
    wu, wm = tap_weights(uniting_weight, mixing_weight)
    outer_table, near_table = table_of(own_outer), table_of(own_near)
    packed = jnp.concatenate(
        [
            jnp.where(turned == 1, near_table, outer_table),
            own,
            jnp.where(turned == 1, outer_table, near_table),
        ],
        axis=3,
    )
    *entries, wu, wm, flags = lax.optimization_barrier(
        tuple(packed[:, k, j : j + 2] for k in (2, 1, 0) for j in (0, 2))
        + (wu, wm, flags)
    )
    flags = (flags, update_mask)
    cols, table = make_columns(entries[0], entries[1])
    edge, rim, joined = run_level(
        2,
        flags,
        cols,
        table,
        wu,
        wm,
        [(h, e, i, n)],
        (own_outer, edge, inner, own_near),
        split=True,
    )

    inner, near = run_inner(2, flags, wu, wm, joined)
    own_outer = send(rim, row_to=off_chip)
    own_near = send(near, row_to=on_chip)
    e = send(edge, across)
    i = send(inner, across)
    xe = send(e, to_other)
    xh = send(e, to_other, off_chip)
    h = send(xe, to_other, off_chip)
    xi = send(i, to_other)
    n = send(i, row_to=on_chip)
    for_ahead = send(entries[4], back)
    for_back = send(entries[5], ahead)
    xn = send(xi, row_to=on_chip)
    cols, table = make_columns(entries[2], entries[3])
    next_cols, next_table = make_columns(for_ahead, for_back)
    edge, _, joined = run_level(
        1,
        flags,
        cols,
        table,
        wu,
        wm,
        [(h, e, i, n), (xh, xe, xi, xn)],
        (own_outer, edge, inner, own_near),
        split=True,
    )

    inner, _ = run_inner(1, flags, wu, wm, joined)
    outer = send(edge, row_to=off_chip)
    near = send(inner, row_to=on_chip)
    halves = run_warp_half(False, flags, next_cols, next_table, (edge, inner, near))
    inner_earlier = send(halves[0], ahead)
    inner_later = send(halves[1], back)
    halves = run_warp_half(True, flags, next_cols, next_table, (outer, edge, inner))
    earlier = send(halves[0], ahead)
    later = send(halves[1], back)
    inner_act, inner_rows = run_last_inner(flags, wu, wm, (inner, near, inner_earlier, inner_later))
    refined = run_last_outer(
        flags,
        wu,
        wm,
        (
            outer,
            edge,
            inner,
            inner_earlier,
            inner_later,
            inner_act,
            inner_rows,
            earlier,
            later,
        ),
    )
    return refined[None]


def solution(mesh):
    placed = (
        P("tm", "rows", None, None),
        P(None, None, "tm", "rows", None),
        P(None, None, "tm", "rows", None),
        P(None, "tm"),
        P(),
        P(),
    )
    return jax.shard_map(
        shards, mesh=mesh, in_specs=placed, out_specs=P("tm", "rows", None, None), check_vma=False
    )
```
